512 devices in a mesh: dp: 32 (over y_lo, z), gx: 2 (over core), gy: 8 (over x, y_hi).
Axes of the slice: x: 4, y: 4 (y_hi: 2, y_lo: 2; y = y_hi * 2 + y_lo), z: 16, core: 2. Of those that a mesh axis runs over, the one named last changes fastest.
Arguments:
- field: float32 [32, 64, 1024], P('dp', 'gx', 'gy'), may hold values from -6 to 6
- cotangent: float32 [32, 64, 1024], P('dp', 'gx', 'gy')
- checker: int32 [64, 1024], P('gx', 'gy'), may hold values from 0 to 1, as said below
- weight_in: float32 [3, 3, 32], replicated, may hold values from -2 to 2
- weight_mid: bfloat16 [3, 3, 32, 32], replicated, may hold values from -0.375 to 0.375
- weight_head: bfloat16 [2, 32], replicated, may hold values from -1 to 1
- prior_grads: float32 [32, 2, 8, 23, 9568], P('dp', 'gx', 'gy')
Outputs:
- coupled: float32 [32, 64, 1024], P('dp', 'gx', 'gy')
- field_grad: float32 [32, 64, 1024], P('dp', 'gx', 'gy')
- summed_grads: float32 [24, 9568], replicated
The draws below stay inside these ranges and needn't reach their ends.
Inputs may be any that keep to these rules, and one draw needn't show every extreme that they name: Each row alternates along the columns: checker[i, j] = (j + p[i]) mod 2, with a parity p[i] of its own for every row i.
All inputs are finite; a program needn't handle non-finite values.
Results may differ from the reference program's by a relative error of at most 0.0034.
Values may be sent and summed in bfloat16 or wider, within the bound.
A program may use at most 64 MiB of HBM per device.

```python
import math
import jax
import jax.numpy as jnp
from jax import lax

HID = 32
LAYERS = 24
LX = 32
LY = 128
REPL = 32
NX = 64
NY = 1024
PARAMS = 9568


def draw_checker(key, part):
    parity = jax.random.randint(jax.random.fold_in(key, 11), (NX, 1), 0, 2).astype(jnp.int32)
    cols_idx = jnp.arange(NY, dtype=jnp.int32)[None, :]
    return ((cols_idx + parity) % 2).astype(jnp.int32)


def draw_cotangent(key, part):
    scales = jnp.exp(jnp.linspace(0.0, math.log(3.0), REPL)).astype(jnp.float32)[:, None, None]
    base = jax.random.truncated_normal(jax.random.fold_in(key, 23), -4.0, 4.0, (REPL, NX, NY), jnp.float32)
    return (base * scales).astype(jnp.float32)


def draw_prior_grads(key, part):
    split_x = NX // LX
    split_y = NY // LY
    count = REPL * split_x * split_y
    factors = jnp.exp(jnp.linspace(0.0, math.log(3.0), count)).astype(jnp.float32)
    factors = factors.reshape(REPL, split_x, split_y, 1, 1) / math.sqrt(count)
    shape = (REPL, split_x, split_y, LAYERS - 1, PARAMS)
    base = jax.random.truncated_normal(jax.random.fold_in(key, 33), -4.0, 4.0, shape, jnp.float32)
    return (base * factors).astype(jnp.float32)


def block_levels(rng, extent, split, low, largest):
    factor_of = 1.0
    for axis_at, blocks in split:
        draws = jax.random.uniform(jax.random.fold_in(jax.random.fold_in(rng, 6), axis_at), (blocks,), jnp.float32, low / len(split), largest / len(split))
        factor_of = factor_of * jnp.repeat(jnp.exp(draws), extent[axis_at] // blocks).reshape((-1,) + (1,) * (len(extent) - 1 - axis_at))
    return factor_of


def scatter_about(stream_key, dims, scale, most, cuts=(), kind=jnp.bfloat16):
    drawn = jax.random.normal(stream_key, dims, jnp.float32) * scale
    if len(cuts) > 0:
        drawn = block_levels(stream_key, dims, cuts, -0.22, 0.18) * drawn
    return jnp.clip(drawn, min=-most, max=most).astype(kind)


def setup_inputs(seed: int = 0) -> dict:
    keys = jax.random.split(jax.random.key(seed), 8)
    field = scatter_about(keys[0], (REPL, NX, NY), 1.0, 6.0, ((0, 32), (1, 2), (2, 8)), jnp.float32)
    cotangent = draw_cotangent(jax.random.fold_in(keys[7], 71), 0)
    checker = draw_checker(jax.random.fold_in(keys[7], 71), 0)
    weight_in = scatter_about(keys[3], (3, 3, HID), 9 ** -0.5, 2.0, (), jnp.float32)
    weight_mid = scatter_about(keys[4], (3, 3, HID, HID), (9 * HID) ** -0.5, 0.375)
    weight_head = scatter_about(keys[5], (2, HID), HID ** -0.5, 1.0)
    prior_grads = draw_prior_grads(jax.random.fold_in(keys[7], 71), 0)
    return {"field": field, "cotangent": cotangent, "checker": checker, "weight_in": weight_in, "weight_mid": weight_mid, "weight_head": weight_head, "prior_grads": prior_grads}


def shifted(values, row_tap, col_tap):
    return jnp.roll(values, (1 - row_tap, 1 - col_tap), axis=(-2, -1))

def back_shifted(values, row_tap, col_tap):
    return jnp.roll(values, (row_tap - 1, col_tap - 1), axis=(-2, -1))

def one_replica(field, cotangent, frozen, weight_in, weight_mid, weight_head):
    highest = lax.Precision.HIGHEST
    unfrozen = 1.0 - frozen
    masked = frozen * field
    mid_f = weight_mid.astype(jnp.float32)
    head_f = weight_head.astype(jnp.float32)
    pre_one = jnp.zeros((HID, NX, NY), jnp.float32)
    for row_tap in range(3):
        for col_tap in range(3):
            pre_one = pre_one + weight_in[row_tap, col_tap][:, None, None] * shifted(masked, row_tap, col_tap)[None]
    hidden_one = jnp.tanh(pre_one).astype(jnp.bfloat16)
    one_f = hidden_one.astype(jnp.float32)
    pre_two = jnp.zeros((HID, NX, NY), jnp.float32)
    for row_tap in range(3):
        for col_tap in range(3):
            pre_two = pre_two + jnp.einsum('oc,cxy->oxy', mid_f[row_tap, col_tap], shifted(one_f, row_tap, col_tap))
    hidden_two = jnp.tanh(pre_two).astype(jnp.bfloat16)
    two_f = hidden_two.astype(jnp.float32)
    pair = jnp.einsum('ko,oxy->kxy', head_f, two_f)
    expo = jnp.exp(pair[0])
    coupled = masked + unfrozen * (field * expo + pair[1])
    d_pair = jnp.stack([unfrozen * cotangent * field * expo, unfrozen * cotangent]).astype(jnp.bfloat16)
    pair_f = d_pair.astype(jnp.float32)
    grad_head = jnp.einsum('kxy,oxy->ko', pair_f, two_f)
    d_hidden_two = jnp.einsum('ko,kxy->oxy', head_f, pair_f)
    d_pre_two = (d_hidden_two * (1.0 - two_f * two_f)).astype(jnp.bfloat16)
    dtwo_f = d_pre_two.astype(jnp.float32)
    mid_list = []
    d_hidden_one = jnp.zeros((HID, NX, NY), jnp.float32)
    for row_tap in range(3):
        for col_tap in range(3):
            mid_list.append(jnp.einsum('oxy,cxy->oc', dtwo_f, shifted(one_f, row_tap, col_tap)))
            d_hidden_one = d_hidden_one + jnp.einsum('oc,oxy->cxy', mid_f[row_tap, col_tap], back_shifted(dtwo_f, row_tap, col_tap))
    d_pre_one = d_hidden_one * (1.0 - one_f * one_f)
    in_list = []
    d_masked = jnp.zeros((NX, NY), jnp.float32)
    for row_tap in range(3):
        for col_tap in range(3):
            in_list.append(jnp.einsum('oxy,xy->o', d_pre_one, shifted(masked, row_tap, col_tap), precision=highest))
            d_masked = d_masked + jnp.einsum('o,oxy->xy', weight_in[row_tap, col_tap], back_shifted(d_pre_one, row_tap, col_tap), precision=highest)
    field_grad = frozen * cotangent + unfrozen * cotangent * expo + frozen * d_masked
    grads = jnp.concatenate([jnp.stack(in_list).reshape(-1), jnp.stack(mid_list).reshape(-1), grad_head.reshape(-1)])
    return (coupled, field_grad, grads)

def reference(field, cotangent, checker, weight_in, weight_mid, weight_head, prior_grads):
    frozen = checker.astype(jnp.float32)
    grad_scale = 1.0 / math.sqrt(REPL * NX * NY)

    def per_replica(pieces):
        coupled, field_grad, grads = one_replica(pieces[0], pieces[1], frozen, weight_in, weight_mid, weight_head)
        return (coupled, field_grad, grads * grad_scale)
    coupled, field_grad, grads = lax.map(per_replica, (field, cotangent))
    window = lax.optimization_barrier(jnp.sum(grads, axis=0))
    others = lax.optimization_barrier(jnp.sum(prior_grads, axis=(0, 1, 2)))
    summed_grads = jnp.concatenate([window[None], others], axis=0)
    return (coupled, field_grad, summed_grads)
```

```python
import functools
import math

import jax
import jax.numpy as jnp
from jax import lax
from jax.experimental import pallas as pl
from jax.experimental.pallas import tpu as pltpu
from jax.sharding import PartitionSpec as P


MESH = pl.DeviceIdType.MESH
ROWS = 64


def all_reduce_kernel(sizes, prior_ref, layer_ref, out_ref, packed, half_in, xs, xr, zs, zr, fin, wide, sem_c, sem_x, sem_z, sem_t, sem_a, sem_b):
    n_y, n_gy, n_z = sizes
    n_p = n_y * n_gy
    core = lax.axis_index("gx")
    dp = lax.axis_index("dp")
    gy = lax.axis_index("gy")
    z = lax.rem(dp, n_z)
    p = lax.div(dp, n_z) * n_gy + gy
    other = 1 - core

    def plane(q):
        return {"dp": lax.div(q, n_gy) * n_z + z, "gx": core, "gy": lax.rem(q, n_gy)}

    def along(w):
        return {"dp": dp - z + w, "gx": core, "gy": gy}

    partner = {"dp": dp, "gx": other, "gy": gy}
    barrier = pltpu.get_barrier_semaphore()
    pl.semaphore_signal(barrier, inc=1, device_id=partner, device_id_type=MESH)

    def hello_plane(i, _):
        pl.semaphore_signal(barrier, inc=1, device_id=plane(lax.rem(p + i, n_p)), device_id_type=MESH)
        return 0

    def hello_along(i, _):
        pl.semaphore_signal(barrier, inc=1, device_id=along(lax.rem(z + i, n_z)), device_id_type=MESH)
        return 0

    lax.fori_loop(1, n_p, hello_plane, 0)
    lax.fori_loop(1, n_z, hello_along, 0)

    n_cols = prior_ref.shape[1]
    full = n_cols // 128
    rest = n_cols - full * 128
    units = packed.shape[0]

    def pack(k, _):
        at = pl.multiple_of(k * 128, 128)
        block = jnp.concatenate([prior_ref[:, pl.ds(at, 128)], layer_ref[:, pl.ds(at, 128)]], axis=0)
        packed[pl.ds(3 * k, 3)] = block.reshape(3, 8, 128)
        return 0

    lax.fori_loop(0, full, pack, 0)
    used = 3 * (full + (1 if rest else 0))
    if rest:
        block = jnp.concatenate([prior_ref[:, full * 128 :], layer_ref[:, full * 128 :]], axis=0)
        block = jnp.concatenate([block, jnp.zeros((24, 128 - rest), jnp.float32)], axis=1)
        packed[3 * full : 3 * full + 3] = block.reshape(3, 8, 128)
    packed[used:] = jnp.zeros((units - used, 8, 128), jnp.float32)

    pl.semaphore_wait(barrier, 1 + (n_p - 1) + (n_z - 1))

    half = units // 2
    swap = pltpu.make_async_remote_copy(
        src_ref=packed.at[pl.ds(other * half, half)], dst_ref=half_in,
        send_sem=sem_c.at[0], recv_sem=sem_c.at[1], device_id=partner, device_id_type=MESH)
    swap.start()
    swap.wait()

    def pair_sum(q, _):
        value = packed[pl.ds(core * half + 8 * q, 8)] + half_in[pl.ds(8 * q, 8)]
        xs[q] = value.reshape(ROWS, 128).astype(jnp.bfloat16)
        return 0

    lax.fori_loop(0, n_p, pair_sum, 0)

    def to_plane(q, slot):
        return pltpu.make_async_remote_copy(
            src_ref=xs.at[q], dst_ref=xr.at[slot], send_sem=sem_x.at[0, q], recv_sem=sem_x.at[1, slot],
            device_id=plane(q), device_id_type=MESH)

    def send_plane(i, _):
        to_plane(lax.rem(p + i, n_p), p).start()
        return 0

    lax.fori_loop(1, n_p, send_plane, 0)

    def take_plane(i, total):
        q = lax.rem(p + n_p - i, n_p)
        to_plane(q, q).wait_recv()
        return total + xr[q].astype(jnp.float32)

    total = lax.fori_loop(1, n_p, take_plane, xs[p].astype(jnp.float32))
    zs[...] = total.astype(jnp.bfloat16).reshape(4, 16, 128)

    def to_along(w, slot):
        return pltpu.make_async_remote_copy(
            src_ref=zs.at[lax.rem(w, 4)], dst_ref=zr.at[slot], send_sem=sem_z.at[0, w], recv_sem=sem_z.at[1, slot],
            device_id=along(w), device_id_type=MESH)

    def send_along(i, _):
        to_along(lax.rem(z + i, n_z), z).start()
        return 0

    lax.fori_loop(1, n_z, send_along, 0)
    tile = lax.rem(z, 4)

    def take_along(i, total):
        w = lax.rem(z + n_z - i, n_z)
        to_along(w, w).wait_recv()
        return total + zr[w].astype(jnp.float32)

    total = lax.fori_loop(1, n_z, take_along, zs[tile].astype(jnp.float32))
    fin[core, p, tile] = total.astype(jnp.bfloat16)

    def to_four(i, slot):
        w = z - tile + lax.rem(tile + i, 4)
        return pltpu.make_async_remote_copy(
            src_ref=fin.at[core, p, tile], dst_ref=fin.at[core, p, slot], send_sem=sem_t.at[0, i], recv_sem=sem_t.at[1, slot],
            device_id=along(w), device_id_type=MESH)

    for i in range(1, 4):
        to_four(i, tile).start()
    for i in range(1, 4):
        to_four(i, lax.rem(tile + i, 4)).wait_recv()

    def all_plane(q, slot):
        return pltpu.make_async_remote_copy(
            src_ref=fin.at[core, p], dst_ref=fin.at[core, slot], send_sem=sem_a.at[0, q], recv_sem=sem_a.at[1, slot],
            device_id=plane(q), device_id_type=MESH)

    def to_partner(which, slot):
        return pltpu.make_async_remote_copy(
            src_ref=fin.at[core, slot], dst_ref=fin.at[which, slot], send_sem=sem_b.at[0, slot], recv_sem=sem_b.at[1, slot],
            device_id=partner, device_id_type=MESH)

    def send_all(i, _):
        all_plane(lax.rem(p + i, n_p), p).start()
        return 0

    lax.fori_loop(1, n_p, send_all, 0)
    to_partner(core, p).start()

    def take_all(i, _):
        q = lax.rem(p + n_p - i, n_p)
        all_plane(q, q).wait_recv()
        to_partner(core, q).start()
        return 0

    lax.fori_loop(1, n_p, take_all, 0)

    def widen_own(q, _):
        wide[pl.ds((core * n_p + q) * 8, 8)] = fin[core, q].reshape(ROWS, 128).astype(jnp.float32).reshape(8, 8, 128)
        return 0

    lax.fori_loop(0, n_p, widen_own, 0)

    def widen_other(q, _):
        to_partner(other, q).wait_recv()
        wide[pl.ds((other * n_p + q) * 8, 8)] = fin[other, q].reshape(ROWS, 128).astype(jnp.float32).reshape(8, 8, 128)
        return 0

    lax.fori_loop(0, n_p, widen_other, 0)

    def unpack(k, _):
        at = pl.multiple_of(k * 128, 128)
        block = wide[pl.ds(3 * k, 3)].reshape(24, 128)
        out_ref[:, pl.ds(at, 128)] = pltpu.roll(block, 1, 0)
        return 0

    lax.fori_loop(0, full, unpack, 0)
    if rest:
        block = wide[3 * full : 3 * full + 3].reshape(24, 128)
        out_ref[:, full * 128 :] = pltpu.roll(block, 1, 0)[:, :rest]

    def drain_plane(i, _):
        q = lax.rem(p + i, n_p)
        to_plane(q, p).wait_send()
        all_plane(q, p).wait_send()
        return 0

    def drain_along(i, _):
        to_along(lax.rem(z + i, n_z), z).wait_send()
        return 0

    def drain_partner(q, _):
        to_partner(core, q).wait_send()
        return 0

    lax.fori_loop(1, n_p, drain_plane, 0)
    lax.fori_loop(1, n_z, drain_along, 0)
    lax.fori_loop(0, n_p, drain_partner, 0)
    for i in range(1, 4):
        to_four(i, tile).wait_send()


def all_reduce(prior, layer, sizes):
    n_y, n_gy, n_z = sizes
    n_p = n_y * n_gy
    units = 2 * n_p * 8
    bf, f32 = jnp.bfloat16, jnp.float32
    sem = pltpu.SemaphoreType.DMA
    return pl.pallas_call(
        functools.partial(all_reduce_kernel, sizes),
        out_shape=jax.ShapeDtypeStruct((prior.shape[0] + 1, prior.shape[1]), f32),
        in_specs=[pl.BlockSpec(memory_space=pltpu.VMEM)] * 2,
        out_specs=pl.BlockSpec(memory_space=pltpu.VMEM),
        scratch_shapes=[
            pltpu.VMEM((units, 8, 128), f32),
            pltpu.VMEM((units // 2, 8, 128), f32),
            pltpu.VMEM((n_p, ROWS, 128), bf),
            pltpu.VMEM((n_p, ROWS, 128), bf),
            pltpu.VMEM((4, 16, 128), bf),
            pltpu.VMEM((n_z, 16, 128), bf),
            pltpu.VMEM((2, n_p, 4, 16, 128), bf),
            pltpu.VMEM((units, 8, 128), f32),
            sem((2,)), sem((2, n_p)), sem((2, n_z)), sem((2, 4)), sem((2, n_p)), sem((2, n_p)),
        ],
        compiler_params=pltpu.CompilerParams(collective_id=0, has_side_effects=True),
    )(prior, layer)


def extended(value, sides, width):
    for axis, dim in sides:
        size, length = (lax.axis_size(axis), value.shape[dim])
        up = [(i, (i + 1) % size) for i in range(size)]
        down = [(j, i) for i, j in up]
        last = lax.slice_in_dim(value, length - width, length, axis=dim)
        initial = lax.slice_in_dim(value, 0, width, axis=dim)
        before = lax.ppermute(last, axis, up)
        after = lax.ppermute(initial, axis, down)
        value = jnp.concatenate([before, value, after], axis=dim)
    return value


def first_conv(padded, weight_in, row_count, col_count):
    total = jnp.zeros((weight_in.shape[2], row_count, col_count), jnp.float32)
    for row_tap in range(3):
        for col_tap in range(3):
            window = padded[row_tap : row_tap + row_count, col_tap : col_tap + col_count]
            total = total + weight_in[row_tap, col_tap][:, None, None] * window[None]
    return total


def on_device(field, cotangent, checker, weight_in, weight_mid, weight_head, prior_grads):
    highest = lax.Precision.HIGHEST
    row_count = field.shape[1]
    col_count = field.shape[2]
    hidden_width = weight_mid.shape[2]
    cell_total = (
        lax.axis_size("dp") * row_count * lax.axis_size("gx") * col_count * lax.axis_size("gy")
    )
    grad_scale = 1.0 / math.sqrt(cell_total)
    values = field[0]
    downstream = cotangent[0]
    frozen = checker.astype(jnp.float32)
    unfrozen = 1.0 - frozen
    masked = frozen * values
    partial_prior = prior_grads.reshape(prior_grads.shape[3], prior_grads.shape[4])
    padded_field = extended(masked, (("gx", 0), ("gy", 1)), 1)
    hidden_one = jnp.tanh(first_conv(padded_field, weight_in, row_count, col_count)).astype(
        jnp.bfloat16
    )
    hidden_pad = extended(hidden_one, (("gx", 1), ("gy", 2)), 1)
    hidden_inner = hidden_pad[:, 1:-1, 1:-1]
    pre_two = jnp.zeros((hidden_width, row_count, col_count), jnp.float32)
    for row_tap in range(3):
        for col_tap in range(3):
            window = hidden_pad[:, row_tap : row_tap + row_count, col_tap : col_tap + col_count]
            pre_two = pre_two + jnp.einsum(
                "oc,cxy->oxy",
                weight_mid[row_tap, col_tap],
                window,
                preferred_element_type=jnp.float32,
            )
    hidden_two = jnp.tanh(pre_two).astype(jnp.bfloat16)
    pair = jnp.einsum("ko,oxy->kxy", weight_head, hidden_two, preferred_element_type=jnp.float32)
    expo = jnp.exp(pair[0])
    coupled = masked + unfrozen * (values * expo + pair[1])
    d_pair = jnp.stack([unfrozen * downstream * values * expo, unfrozen * downstream]).astype(
        jnp.bfloat16
    )
    grad_head = jnp.einsum("kxy,oxy->ko", d_pair, hidden_two, preferred_element_type=jnp.float32)
    d_hidden_two = jnp.einsum(
        "ko,kxy->oxy", weight_head, d_pair, preferred_element_type=jnp.float32
    )
    two_f = hidden_two.astype(jnp.float32)
    d_pre_two = (d_hidden_two * (1.0 - two_f * two_f)).astype(jnp.bfloat16)
    d_two_pad = extended(d_pre_two, (("gx", 1), ("gy", 2)), 1)
    mid_list = []
    d_hidden_one = jnp.zeros((hidden_width, row_count, col_count), jnp.float32)
    for row_tap in range(3):
        for col_tap in range(3):
            window = hidden_pad[:, row_tap : row_tap + row_count, col_tap : col_tap + col_count]
            mid_list.append(
                jnp.einsum("oxy,cxy->oc", d_pre_two, window, preferred_element_type=jnp.float32)
            )
            back_window = d_two_pad[
                :, 2 - row_tap : 2 - row_tap + row_count, 2 - col_tap : 2 - col_tap + col_count
            ]
            d_hidden_one = d_hidden_one + jnp.einsum(
                "oc,oxy->cxy",
                weight_mid[row_tap, col_tap],
                back_window,
                preferred_element_type=jnp.float32,
            )
    one_f = hidden_inner.astype(jnp.float32)
    d_pre_one = d_hidden_one * (1.0 - one_f * one_f)
    in_list = []
    for row_tap in range(3):
        for col_tap in range(3):
            window = padded_field[row_tap : row_tap + row_count, col_tap : col_tap + col_count]
            in_list.append(jnp.einsum("oxy,xy->o", d_pre_one, window, precision=highest))
    d_one_pad = extended(d_pre_one, (("gx", 1), ("gy", 2)), 1)
    d_masked = jnp.zeros((row_count, col_count), jnp.float32)
    for row_tap in range(3):
        for col_tap in range(3):
            back_window = d_one_pad[
                :, 2 - row_tap : 2 - row_tap + row_count, 2 - col_tap : 2 - col_tap + col_count
            ]
            d_masked = d_masked + jnp.einsum(
                "o,oxy->xy", weight_in[row_tap, col_tap], back_window, precision=highest
            )
    field_grad = frozen * downstream + unfrozen * downstream * expo + frozen * d_masked
    layer_grads = (
        jnp.concatenate(
            [jnp.stack(in_list).reshape(-1), jnp.stack(mid_list).reshape(-1), grad_head.reshape(-1)]
        )
        * grad_scale
    )
    sizes = (2, lax.axis_size("gy"), lax.axis_size("dp") // 2)
    summed_grads = all_reduce(partial_prior, layer_grads[None], sizes)
    return (coupled[None], field_grad[None], summed_grads)


def solution(mesh):
    placed = (
        P("dp", "gx", "gy"),
        P("dp", "gx", "gy"),
        P("gx", "gy"),
        P(),
        P(),
        P(),
        P("dp", "gx", "gy", None, None),
    )
    return jax.shard_map(
        on_device,
        mesh=mesh,
        in_specs=placed,
        out_specs=(P("dp", "gx", "gy"), P("dp", "gx", "gy"), P()),
        check_vma=False,
    )
```

```python
import functools
import math

import jax
import jax.numpy as jnp
from jax import lax
from jax.experimental import pallas as pl
from jax.experimental.pallas import tpu as pltpu
from jax.sharding import PartitionSpec as P

MESH = pl.DeviceIdType.MESH
ROWS = 64


def all_reduce_kernel(sizes, prior_ref, layer_ref, out_ref, packed, half_in, xs, xr, zs, zr, fin, wide, sem_c, sem_x, sem_z, sem_t, sem_a, sem_b):
    n_y, n_gy, n_z = sizes
    n_p = n_y * n_gy
    core = lax.axis_index("gx")
    dp = lax.axis_index("dp")
    gy = lax.axis_index("gy")
    z = lax.rem(dp, n_z)
    p = lax.div(dp, n_z) * n_gy + gy
    other = 1 - core

    def plane(q):
        return {"dp": lax.div(q, n_gy) * n_z + z, "gx": core, "gy": lax.rem(q, n_gy)}

    def along(w):
        return {"dp": dp - z + w, "gx": core, "gy": gy}

    partner = {"dp": dp, "gx": other, "gy": gy}
    barrier = pltpu.get_barrier_semaphore()
    pl.semaphore_signal(barrier, inc=1, device_id=partner, device_id_type=MESH)

    def hello_plane(i, _):
        pl.semaphore_signal(barrier, inc=1, device_id=plane(lax.rem(p + i, n_p)), device_id_type=MESH)
        return 0

    def hello_along(i, _):
        pl.semaphore_signal(barrier, inc=1, device_id=along(lax.rem(z + i, n_z)), device_id_type=MESH)
        return 0

    lax.fori_loop(1, n_p, hello_plane, 0)
    lax.fori_loop(1, n_z, hello_along, 0)

    n_cols = prior_ref.shape[1]
    full = n_cols // 128
    rest = n_cols - full * 128
    units = packed.shape[0]

    def pack(k, _):
        at = pl.multiple_of(k * 128, 128)
        block = jnp.concatenate([prior_ref[:, pl.ds(at, 128)], layer_ref[pl.ds(k, 1), :]], axis=0)
        packed[pl.ds(3 * k, 3)] = block.reshape(3, 8, 128)
        return 0

    lax.fori_loop(0, full, pack, 0)
    used = 3 * (full + (1 if rest else 0))
    if rest:
        block = jnp.concatenate([prior_ref[:, full * 128 :], layer_ref[full : full + 1, :rest]], axis=0)
        block = jnp.concatenate([block, jnp.zeros((24, 128 - rest), jnp.float32)], axis=1)
        packed[3 * full : 3 * full + 3] = block.reshape(3, 8, 128)
    packed[used:] = jnp.zeros((units - used, 8, 128), jnp.float32)

    pl.semaphore_wait(barrier, 1 + (n_p - 1) + (n_z - 1))

    half = units // 2
    swap = pltpu.make_async_remote_copy(
        src_ref=packed.at[pl.ds(other * half, half)], dst_ref=half_in,
        send_sem=sem_c.at[0], recv_sem=sem_c.at[1], device_id=partner, device_id_type=MESH)
    swap.start()
    swap.wait()

    def pair_sum(q, _):
        value = packed[pl.ds(core * half + 8 * q, 8)] + half_in[pl.ds(8 * q, 8)]
        xs[q] = value.reshape(ROWS, 128).astype(jnp.bfloat16)
        return 0

    lax.fori_loop(0, n_p, pair_sum, 0)

    def to_plane(q, slot):
        return pltpu.make_async_remote_copy(
            src_ref=xs.at[q], dst_ref=xr.at[slot], send_sem=sem_x.at[0, q], recv_sem=sem_x.at[1, slot],
            device_id=plane(q), device_id_type=MESH)

    def send_plane(i, _):
        to_plane(lax.rem(p + i, n_p), p).start()
        return 0

    lax.fori_loop(1, n_p, send_plane, 0)

    def take_plane(i, total):
        q = lax.rem(p + n_p - i, n_p)
        to_plane(q, q).wait_recv()
        return total + xr[q].astype(jnp.float32)

    total = lax.fori_loop(1, n_p, take_plane, xs[p].astype(jnp.float32))
    zs[...] = total.astype(jnp.bfloat16).reshape(4, 16, 128)

    def to_along(w, slot):
        return pltpu.make_async_remote_copy(
            src_ref=zs.at[lax.rem(w, 4)], dst_ref=zr.at[slot], send_sem=sem_z.at[0, w], recv_sem=sem_z.at[1, slot],
            device_id=along(w), device_id_type=MESH)

    def send_along(i, _):
        to_along(lax.rem(z + i, n_z), z).start()
        return 0

    lax.fori_loop(1, n_z, send_along, 0)
    tile = lax.rem(z, 4)

    def take_along(i, total):
        w = lax.rem(z + n_z - i, n_z)
        to_along(w, w).wait_recv()
        return total + zr[w].astype(jnp.float32)

    total = lax.fori_loop(1, n_z, take_along, zs[tile].astype(jnp.float32))
    fin[core, p, tile] = total.astype(jnp.bfloat16)

    def to_four(i, slot):
        w = z - tile + lax.rem(tile + i, 4)
        return pltpu.make_async_remote_copy(
            src_ref=fin.at[core, p, tile], dst_ref=fin.at[core, p, slot], send_sem=sem_t.at[0, i], recv_sem=sem_t.at[1, slot],
            device_id=along(w), device_id_type=MESH)

    for i in range(1, 4):
        to_four(i, tile).start()
    for i in range(1, 4):
        to_four(i, lax.rem(tile + i, 4)).wait_recv()

    def all_plane(q, slot):
        return pltpu.make_async_remote_copy(
            src_ref=fin.at[core, p], dst_ref=fin.at[core, slot], send_sem=sem_a.at[0, q], recv_sem=sem_a.at[1, slot],
            device_id=plane(q), device_id_type=MESH)

    def to_partner(which, slot):
        return pltpu.make_async_remote_copy(
            src_ref=fin.at[core, slot], dst_ref=fin.at[which, slot], send_sem=sem_b.at[0, slot], recv_sem=sem_b.at[1, slot],
            device_id=partner, device_id_type=MESH)

    def send_all(i, _):
        all_plane(lax.rem(p + i, n_p), p).start()
        return 0

    lax.fori_loop(1, n_p, send_all, 0)
    to_partner(core, p).start()

    def take_all(i, _):
        q = lax.rem(p + n_p - i, n_p)
        all_plane(q, q).wait_recv()
        to_partner(core, q).start()
        return 0

    lax.fori_loop(1, n_p, take_all, 0)

    def widen_own(q, _):
        wide[pl.ds((core * n_p + q) * 8, 8)] = fin[core, q].reshape(ROWS, 128).astype(jnp.float32).reshape(8, 8, 128)
        return 0

    lax.fori_loop(0, n_p, widen_own, 0)

    def widen_other(q, _):
        to_partner(other, q).wait_recv()
        wide[pl.ds((other * n_p + q) * 8, 8)] = fin[other, q].reshape(ROWS, 128).astype(jnp.float32).reshape(8, 8, 128)
        return 0

    lax.fori_loop(0, n_p, widen_other, 0)

    def unpack(k, _):
        at = pl.multiple_of(k * 128, 128)
        block = wide[pl.ds(3 * k, 3)].reshape(24, 128)
        out_ref[:, pl.ds(at, 128)] = pltpu.roll(block, 1, 0)
        return 0

    lax.fori_loop(0, full, unpack, 0)
    if rest:
        block = wide[3 * full : 3 * full + 3].reshape(24, 128)
        out_ref[:, full * 128 :] = pltpu.roll(block, 1, 0)[:, :rest]

    def drain_plane(i, _):
        q = lax.rem(p + i, n_p)
        to_plane(q, p).wait_send()
        all_plane(q, p).wait_send()
        return 0

    def drain_along(i, _):
        to_along(lax.rem(z + i, n_z), z).wait_send()
        return 0

    def drain_partner(q, _):
        to_partner(core, q).wait_send()
        return 0

    lax.fori_loop(1, n_p, drain_plane, 0)
    lax.fori_loop(1, n_z, drain_along, 0)
    lax.fori_loop(0, n_p, drain_partner, 0)
    for i in range(1, 4):
        to_four(i, tile).wait_send()


def all_reduce(prior, layer, sizes):
    n_y, n_gy, n_z = sizes
    n_p = n_y * n_gy
    units = 2 * n_p * 8
    bf, f32 = jnp.bfloat16, jnp.float32
    sem = pltpu.SemaphoreType.DMA
    return pl.pallas_call(
        functools.partial(all_reduce_kernel, sizes),
        out_shape=jax.ShapeDtypeStruct((prior.shape[0] + 1, prior.shape[1]), f32),
        in_specs=[pl.BlockSpec(memory_space=pltpu.VMEM)] * 2,
        out_specs=pl.BlockSpec(memory_space=pltpu.VMEM),
        scratch_shapes=[
            pltpu.VMEM((units, 8, 128), f32),
            pltpu.VMEM((units // 2, 8, 128), f32),
            pltpu.VMEM((n_p, ROWS, 128), bf),
            pltpu.VMEM((n_p, ROWS, 128), bf),
            pltpu.VMEM((4, 16, 128), bf),
            pltpu.VMEM((n_z, 16, 128), bf),
            pltpu.VMEM((2, n_p, 4, 16, 128), bf),
            pltpu.VMEM((units, 8, 128), f32),
            sem((2,)), sem((2, n_p)), sem((2, n_z)), sem((2, 4)), sem((2, n_p)), sem((2, n_p)),
        ],
        compiler_params=pltpu.CompilerParams(collective_id=0, has_side_effects=True),
    )(prior, layer)


def flat_roll(value, offset):
    return pltpu.roll(value, (-offset) % value.shape[-1], value.ndim - 1)


def halves(value):
    high = value.astype(jnp.bfloat16)
    return high, (value - high.astype(jnp.float32)).astype(jnp.bfloat16)


def nt(a, b, **how):
    return lax.dot_general(a, b, (((1,), (1,)), ((), ())), preferred_element_type=jnp.float32, **how)


def dot(a, b):
    return jnp.dot(a, b, preferred_element_type=jnp.float32)


def lanes_of(shape):
    return lax.broadcasted_iota(jnp.int32, shape, len(shape) - 1)


def layer_kernel(scale, field_ref, cot_ref, check_ref, win_ref, wmid_ref, whead_ref,
                 coupled_ref, fgrad_ref, layer_ref,
                 near_f, near_c, near_k, ext, pack_out, pack_in, taps, edge_taps, w9, w2, w3,
                 xm, xs, xd, xds, cp, pair_rows, t_rows, acc_mid, b_rows, sem_r, sem_p):
    f32, bf = jnp.float32, jnp.bfloat16
    dp, core, gy = lax.axis_index("dp"), lax.axis_index("gx"), lax.axis_index("gy")
    n_gy = lax.axis_size("gy")
    partner = {"dp": dp, "gx": 1 - core, "gy": gy}
    left = {"dp": dp, "gx": core, "gy": lax.rem(gy + n_gy - 1, n_gy)}
    right = {"dp": dp, "gx": core, "gy": lax.rem(gy + 1, n_gy)}
    barrier = pltpu.get_barrier_semaphore()
    for who in (partner, left, right):
        pl.semaphore_signal(barrier, inc=1, device_id=who, device_id_type=MESH)

    for a in range(3):
        w9[3 * a : 3 * a + 3, 0:32] = win_ref[a]
    w9[9:16, 0:32] = jnp.zeros((7, 32), f32)
    eye_f = (lax.broadcasted_iota(jnp.int32, (32, 32), 0) == lanes_of((32, 32))).astype(f32)
    eye = eye_f.astype(bf)
    w_taps = w9[:, 0:32]
    taps_t = nt(eye_f, w_taps, precision=lax.Precision.HIGHEST)
    th, tl = halves(taps_t)
    w_one = jnp.concatenate([th, th, tl], axis=1)
    wh, wl = halves(w_taps)
    w_back = jnp.concatenate([wh, wh, wl], axis=1)
    head = whead_ref[...]
    head_t = nt(eye, head)
    head_0, head_1 = head_t[:, 0:1], head_t[:, 1:2]
    for a in range(3):
        for b in range(3):
            k = 3 * a + b
            w2[:, 32 * k : 32 * k + 32] = wmid_ref[a, b]
            kb = 3 * (2 - a) + b
            w3[:, 32 * kb : 32 * kb + 32] = wmid_ref[a, b].astype(f32).T.astype(bf)

    pl.semaphore_wait(barrier, 3)
    swaps = [
        pltpu.make_async_remote_copy(src_ref=src, dst_ref=dst, send_sem=sem_r.at[0, i], recv_sem=sem_r.at[1, i], device_id=partner, device_id_type=MESH)
        for i, (src, dst) in enumerate(((field_ref, near_f), (cot_ref, near_c), (check_ref, near_k)))
    ]
    for swap in swaps:
        swap.start()
    zeros = jnp.zeros((8, 128), f32)
    for i in range(3):
        ext[i, 40:48] = zeros
    ext[0, 4:36] = field_ref[0]
    ext[1, 4:36] = cot_ref[0]
    ext[2, 4:36] = check_ref[...].astype(f32)
    for swap in swaps:
        swap.wait_recv()
    ext[0, 0:4], ext[0, 36:40] = near_f[0, 28:32], near_f[0, 0:4]
    ext[1, 0:4], ext[1, 36:40] = near_c[0, 28:32], near_c[0, 0:4]
    ext[2, 0:4], ext[2, 36:40] = near_k[28:32].astype(f32), near_k[0:4].astype(f32)

    row_16 = lax.broadcasted_iota(jnp.int32, (16, 128), 0)
    lane_16 = lanes_of((16, 128))
    own_lanes = lax.div(lane_16, 8) == row_16
    for i in range(3):
        for t in range(3):
            turned = pltpu.roll(ext[i, 16 * t : 16 * t + 16], 4, 1, stride=8, stride_axis=0)
            pack_out[3 * i + t : 3 * i + t + 1] = jnp.sum(jnp.where(own_lanes, turned, 0.0), axis=0, keepdims=True)
    pack_out[9:16] = jnp.zeros((7, 128), f32)
    posts = [
        pltpu.make_async_remote_copy(src_ref=pack_out, dst_ref=pack_in.at[i], send_sem=sem_p.at[0, i], recv_sem=sem_p.at[1, i], device_id=who, device_id_type=MESH)
        for i, who in ((1, left), (0, right))
    ]
    for post in posts:
        post.start()
    for post in posts:
        post.wait_recv()
    column = lax.rem(lane_16, 8)
    own = pack_out[...]
    slab_l = jnp.where(column >= 4, own, pack_in[0])
    slab_r = jnp.where(column < 4, own, pack_in[1])

    def flat(slab, i):
        return jnp.concatenate([slab[3 * i + t : 3 * i + t + 1] for t in range(3)], axis=1)

    def flat_both(i):
        return jnp.concatenate([flat(slab_l, i), flat(slab_r, i)], axis=1)

    field_s, cot_s, frozen_s = flat_both(0), flat_both(1), flat_both(2)
    masked_s = field_s * frozen_s

    def both_rolled(value, offset):
        return jnp.concatenate([flat_roll(value[:, :384], offset), flat_roll(value[:, 384:], offset)], axis=1)

    def unflat(vector, e):
        parts = []
        for t in range(3):
            spread = jnp.broadcast_to(vector[:, 128 * t : 128 * t + 128], (16, 128))
            parts.append(jnp.sum(jnp.where(lane_16 == 8 * row_16 + e, spread, 0.0), axis=1, keepdims=True))
        return jnp.concatenate(parts, axis=0)

    masked = ext[0] * ext[2]
    lane_48 = lanes_of((48, 128))
    shifts = (
        jnp.where(lane_48 == 0, unflat(masked_s[:, :384], 3), pltpu.roll(masked, 1, 1)),
        masked,
        jnp.where(lane_48 == 127, unflat(masked_s[:, 384:], 4), pltpu.roll(masked, 127, 1)),
    )
    taps[...] = jnp.zeros(taps.shape, f32)
    edge_taps[...] = jnp.zeros(edge_taps.shape, f32)
    for a in range(3):
        for b in range(3):
            k = 3 * a + b
            taps[pl.ds(16 + k, 38, stride=16), :] = shifts[b][a : a + 38]
            edge_taps[k : k + 1, :] = both_rolled(masked_s, 8 * (a - 1) + b - 1)

    def first(tap_values):
        high, low = halves(tap_values)
        return jnp.tanh(dot(w_one, jnp.concatenate([high, low, high], axis=0))).astype(bf)

    lane_384 = lanes_of((32, 384))

    def spread_edges(value, back, store):
        for a in range(3):
            for b in range(3):
                k = 3 * a + b
                offset = 8 * (a - 1) + (1 - b if back else b - 1)
                store[32 * k : 32 * k + 32, :] = both_rolled(value, offset).astype(bf)
        mixed = jnp.where(lax.rem(lane_384, 8) == 4, flat_roll(value[:, :384], -1), flat_roll(value[:, 384:], 1))
        for t in range(3):
            cp[t] = mixed[:, 128 * t : 128 * t + 128]

    lane_32 = lanes_of((32, 128))

    def spread_row(q, value, back, store):
        edge = pltpu.roll(cp[lax.div(q, 16)], lax.rem(252 - 8 * lax.rem(q, 16), 128), 1)
        before = jnp.where(lane_32 == 0, edge, pltpu.roll(value, 1, 1)).astype(bf)
        after = jnp.where(lane_32 == 127, edge, pltpu.roll(value, 127, 1)).astype(bf)
        store[q, 0:32] = after if back else before
        store[q, 32:64] = value.astype(bf)
        store[q, 64:96] = before if back else after

    one_s = first(edge_taps[...])
    spread_edges(one_s.astype(f32), False, xs)

    def one_rows(rows):
        values = jnp.concatenate([taps[pl.ds(pl.multiple_of(16 * q, 16), 16), :] for q in rows], axis=1)
        out = first(values).astype(f32)
        for i, q in enumerate(rows):
            spread_row(q, out[:, 128 * i : 128 * i + 128], False, xm)

    def over_rows(step):
        def body(i, _):
            step([4 + 4 * i + n for n in range(4)])
            return 0

        lax.fori_loop(0, 8, body, 0)

    for q in (0, 39):
        xm[q] = jnp.zeros((96, 128), bf)
    one_rows([1, 2, 3, 36])
    one_rows([37, 38])
    over_rows(one_rows)

    def second(windows, field, cot, frozen):
        two = jnp.tanh(dot(w2[...], windows)).astype(bf)
        pair = dot(head, two)
        expo = jnp.exp(pair[0:1])
        open_cot = (1.0 - frozen) * cot
        d_0 = (open_cot * field * expo).astype(bf)
        d_1 = open_cot.astype(bf)
        two_f = two.astype(f32)
        d_two = (head_0 * d_0.astype(f32) + head_1 * d_1.astype(f32)) * (1.0 - two_f * two_f)
        return two, pair, d_0, d_1, d_two.astype(bf).astype(f32)

    _, _, _, _, d_two_s = second(xs[...], field_s, cot_s, frozen_s)
    spread_edges(d_two_s, True, xds)

    def windows_of(store, rows):
        return jnp.concatenate([store[pl.ds(q - 1, 3)].reshape(288, 128) for q in rows], axis=1)

    def rows_of(i, rows):
        return jnp.concatenate([ext[i, pl.ds(q, 1), :] for q in rows], axis=1)

    acc_mid[...] = jnp.zeros(acc_mid.shape, f32)
    b_rows[...] = jnp.zeros(b_rows.shape, f32)

    def two_rows(rows, inner=True):
        two, pair, d_0, d_1, d_two = second(windows_of(xm, rows), rows_of(0, rows), rows_of(1, rows), rows_of(2, rows))
        for i, q in enumerate(rows):
            at = slice(128 * i, 128 * i + 128)
            spread_row(q, d_two[:, at], True, xd)
            if inner:
                pair_rows[pl.ds(pl.multiple_of(8 * q, 8), 2), :] = pair[:, at]
        if inner:
            b_rows[297:299, 0:32] += nt(jnp.concatenate([d_0, d_1], axis=0), two)

    for q in (0, 1, 38, 39):
        xd[q] = jnp.zeros((96, 128), bf)
    two_rows([2, 3, 36, 37], inner=False)
    over_rows(two_rows)

    def third(windows, one):
        one_f = one.astype(f32)
        d_one = dot(w3[...], windows) * (1.0 - one_f * one_f)
        high, low = halves(d_one)
        return high, low, dot(w_back, jnp.concatenate([high, low, high], axis=0))

    _, _, t_s = third(xds[...], one_s)

    def three_rows(rows, inner=True):
        windows = windows_of(xd, rows)
        one = jnp.concatenate([xm[q, 32:64] for q in rows], axis=1)
        high, low, t_values = third(windows, one)
        for i, q in enumerate(rows):
            t_rows[pl.ds(pl.multiple_of(16 * q, 16), 16), :] = t_values[:, 128 * i : 128 * i + 128]
        if inner:
            acc_mid[...] += nt(windows, one)
            values = jnp.concatenate([taps[pl.ds(pl.multiple_of(16 * q, 16), 16), :] for q in rows], axis=1)
            m_high, m_low = halves(values)
            parts = nt(jnp.concatenate([m_high, m_low], axis=0), jnp.concatenate([high, low], axis=0))
            parts = parts[0:16] + parts[16:32]
            b_rows[0:9, 0:32] += (parts[:, 0:32] + parts[:, 32:64])[0:9]

    three_rows([3, 36], inner=False)
    over_rows(three_rows)

    def column_sum(b):
        total = None
        for a in range(3):
            part = t_rows[pl.ds(16 * (5 - a) + 3 * a + b, 32, stride=16), :]
            total = part if total is None else total + part
        return total

    def edge_sum(b, side):
        total = None
        for a in range(3):
            k = 3 * a + b
            part = flat_roll(t_s[k : k + 1, 384 * side : 384 * side + 384], 8 * (1 - a))
            total = part if total is None else total + part
        return total

    lane = lanes_of((32, 128))
    from_right = unflat(edge_sum(0, 1), 4)[4:36]
    from_left = unflat(edge_sum(2, 0), 3)[4:36]
    d_masked = (
        jnp.where(lane == 127, from_right, pltpu.roll(column_sum(0), 127, 1))
        + column_sum(1)
        + jnp.where(lane == 0, from_left, pltpu.roll(column_sum(2), 1, 1))
    )
    frozen = check_ref[...].astype(f32)
    unfrozen = 1.0 - frozen
    expo = jnp.exp(pair_rows[pl.ds(32, 32, stride=8), :])
    offset = pair_rows[pl.ds(33, 32, stride=8), :]
    values, cot = field_ref[0], cot_ref[0]
    coupled_ref[0] = frozen * values + unfrozen * (values * expo + offset)
    fgrad_ref[0] = frozen * cot + unfrozen * cot * expo + frozen * d_masked

    for j in range(3):
        b_rows[9 + 96 * (2 - j) : 9 + 96 * (2 - j) + 96, 0:32] = acc_mid[96 * j : 96 * j + 96]
    rows = layer_ref.shape[0]
    layer = b_rows[pl.ds(0, rows, stride=4), :]
    for g in range(1, 4):
        layer = layer + pltpu.roll(b_rows[pl.ds(g, rows, stride=4), :], 32 * g, 1)
    layer_ref[...] = layer * scale
    for copy in (*swaps, *posts):
        copy.wait_send()


def layer_call(scale, field, cot, checker, weight_in, weight_mid, weight_head):
    f32, bf = jnp.float32, jnp.bfloat16
    sem = pltpu.SemaphoreType.DMA
    vmem = pl.BlockSpec(memory_space=pltpu.VMEM)
    return pl.pallas_call(
        functools.partial(layer_kernel, scale),
        out_shape=(
            jax.ShapeDtypeStruct(field.shape, f32),
            jax.ShapeDtypeStruct(field.shape, f32),
            jax.ShapeDtypeStruct((80, 128), f32),
        ),
        in_specs=[vmem] * 6,
        out_specs=(vmem,) * 3,
        scratch_shapes=[
            pltpu.VMEM(field.shape, f32), pltpu.VMEM(field.shape, f32), pltpu.VMEM(checker.shape, jnp.int32),
            pltpu.VMEM((3, 48, 128), f32),
            pltpu.VMEM((16, 128), f32), pltpu.VMEM((2, 16, 128), f32),
            pltpu.VMEM((640, 128), f32), pltpu.VMEM((16, 768), f32),
            pltpu.VMEM((16, 128), f32), pltpu.VMEM((32, 288), bf), pltpu.VMEM((32, 288), bf),
            pltpu.VMEM((40, 96, 128), bf), pltpu.VMEM((288, 768), bf),
            pltpu.VMEM((40, 96, 128), bf), pltpu.VMEM((288, 768), bf),
            pltpu.VMEM((3, 32, 128), f32),
            pltpu.VMEM((320, 128), f32), pltpu.VMEM((640, 128), f32),
            pltpu.VMEM((288, 32), f32), pltpu.VMEM((320, 128), f32),
            sem((2, 3)), sem((2, 2)),
        ],
        compiler_params=pltpu.CompilerParams(collective_id=1, has_side_effects=True),
    )(field, cot, checker, weight_in, weight_mid, weight_head)


def on_device(field, cotangent, checker, weight_in, weight_mid, weight_head, prior_grads):
    cell_total = field.size * lax.axis_size("dp") * lax.axis_size("gx") * lax.axis_size("gy")
    scale = 1.0 / math.sqrt(cell_total)
    coupled, field_grad, layer = layer_call(scale, field, cotangent, checker, weight_in, weight_mid, weight_head)
    partial_prior = prior_grads.reshape(prior_grads.shape[3], prior_grads.shape[4])
    sizes = (2, lax.axis_size("gy"), lax.axis_size("dp") // 2)
    return coupled, field_grad, all_reduce(partial_prior, layer, sizes)


def solution(mesh):
    placed = (
        P("dp", "gx", "gy"),
        P("dp", "gx", "gy"),
        P("gx", "gy"),
        P(),
        P(),
        P(),
        P("dp", "gx", "gy", None, None),
    )
    return jax.shard_map(
        on_device,
        mesh=mesh,
        in_specs=placed,
        out_specs=(P("dp", "gx", "gy"), P("dp", "gx", "gy"), P()),
        check_vma=False,
    )
```

```python
import functools
import math

import jax
import jax.numpy as jnp
from jax import lax
from jax.experimental import pallas as pl
from jax.experimental.pallas import tpu as pltpu
from jax.sharding import PartitionSpec as P

MESH = pl.DeviceIdType.MESH
UNITS = 10


def flat_roll(value, offset):
    return pltpu.roll(value, (-offset) % value.shape[-1], value.ndim - 1)


def halves(value):
    high = value.astype(jnp.bfloat16)
    return high, (value - high.astype(jnp.float32)).astype(jnp.bfloat16)


def nt(a, b, **how):
    return lax.dot_general(a, b, (((1,), (1,)), ((), ())), preferred_element_type=jnp.float32, **how)


def dot(a, b):
    return jnp.dot(a, b, preferred_element_type=jnp.float32)


def lanes_of(shape):
    return lax.broadcasted_iota(jnp.int32, shape, len(shape) - 1)


def fused_kernel(scale, field_ref, cot_ref, check_ref, win_ref, wmid_ref, whead_ref, prior_ref,
                 coupled_ref, fgrad_ref, out_ref,
                 near_f, near_c, near_k, ext, pack_out, pack_in, taps, edge_taps, w9, w2, w3,
                 xm, xs_one, xd, xds, cp, pair_rows, t_rows, acc_mid, b_rows,
                 c_own, c_in, xs, xr, zs, zr, fin, wide, mine, mine_in, mine_x, mine_z, own_sum, mine_fin,
                 sem_r, sem_p, sem_own, sem_c, sem_x, sem_z, sem_t, sem_a, sem_b, sem_l, sem_lx, sem_lz, sem_la, sem_lr):
    f32, bf = jnp.float32, jnp.bfloat16
    dp, core, gy = lax.axis_index("dp"), lax.axis_index("gx"), lax.axis_index("gy")
    n_gy = lax.axis_size("gy")
    n_z = lax.axis_size("dp") // 2
    n_p = 2 * n_gy
    z = lax.rem(dp, n_z)
    p = lax.div(dp, n_z) * n_gy + gy
    other = 1 - core
    share = c_own.shape[0]

    def plane(q, which=core):
        return {"dp": lax.div(q, n_gy) * n_z + z, "gx": which, "gy": lax.rem(q, n_gy)}

    def along(w):
        return {"dp": dp - z + w, "gx": core, "gy": gy}

    def chunk(q, rows=64):
        return pl.ds(pl.multiple_of(rows * q, rows), rows)

    partner = {"dp": dp, "gx": other, "gy": gy}
    left = {"dp": dp, "gx": core, "gy": lax.rem(gy + n_gy - 1, n_gy)}
    right = {"dp": dp, "gx": core, "gy": lax.rem(gy + 1, n_gy)}
    barrier = pltpu.get_barrier_semaphore()

    def hello(who):
        pl.semaphore_signal(barrier, inc=1, device_id=who, device_id_type=MESH)

    def hello_along(i, _):
        hello(along(lax.rem(z + i, n_z)))
        return 0

    def hello_plane(i, _):
        hello(plane(lax.rem(p + i, n_p)))
        hello(plane(lax.rem(p + i, n_p), other))
        return 0

    lax.fori_loop(1, n_z, hello_along, 0)
    lax.fori_loop(1, n_p, hello_plane, 0)
    hello(partner)

    def remote(src, dst, sends, recvs, who):
        return pltpu.make_async_remote_copy(src_ref=src, dst_ref=dst, send_sem=sends, recv_sem=recvs, device_id=who, device_id_type=MESH)

    skip = prior_ref.shape[0] - share
    load = pltpu.make_async_copy(prior_ref.at[pl.ds(skip * core, share)], c_own, sem_own)
    load.start()

    def to_plane(q, slot):
        return remote(xs.at[chunk(q)], xr.at[slot], sem_x.at[0, q], sem_x.at[1, slot], plane(q))

    def to_along(w, slot):
        return remote(zs.at[lax.rem(w, 4)], zr.at[slot], sem_z.at[0, w], sem_z.at[1, slot], along(w))

    for a in range(3):
        w9[3 * a : 3 * a + 3, 0:32] = win_ref[a]
    w9[9:16, 0:32] = jnp.zeros((7, 32), f32)
    eye_f = (lax.broadcasted_iota(jnp.int32, (32, 32), 0) == lanes_of((32, 32))).astype(f32)
    eye = eye_f.astype(bf)
    w_taps = w9[:, 0:32]
    taps_t = nt(eye_f, w_taps, precision=lax.Precision.HIGHEST)
    th, tl = halves(taps_t)
    w_one = jnp.concatenate([th, th, tl], axis=1)
    wh, wl = halves(w_taps)
    w_back = jnp.concatenate([wh, wh, wl], axis=1)
    head = whead_ref[...]
    head_t = nt(eye, head)
    head_0, head_1 = head_t[:, 0:1], head_t[:, 1:2]
    for a in range(3):
        for b in range(3):
            k = 3 * a + b
            w2[:, 32 * k : 32 * k + 32] = wmid_ref[a, b]
            kb = 3 * (2 - a) + b
            w3[:, 32 * kb : 32 * kb + 32] = wmid_ref[a, b].astype(f32).T.astype(bf)

    zeros = jnp.zeros((8, 128), f32)
    for i in range(3):
        ext[i, 40:48] = zeros
    ext[0, 4:36] = field_ref[0]
    ext[1, 4:36] = cot_ref[0]
    ext[2, 4:36] = check_ref[...].astype(f32)
    pl.semaphore_wait(barrier, 1 + 2 * (n_p - 1) + (n_z - 1))
    swaps = [
        pltpu.make_async_remote_copy(src_ref=src, dst_ref=dst, send_sem=sem_r.at[0, i], recv_sem=sem_r.at[1, i], device_id=partner, device_id_type=MESH)
        for i, (src, dst) in enumerate(((field_ref, near_f), (cot_ref, near_c), (check_ref, near_k)))
    ]
    for swap in swaps:
        swap.start()
    halves_swap = remote(prior_ref.at[pl.ds(skip * other, share)], c_in, sem_c.at[0], sem_c.at[1], partner)
    halves_swap.start()
    for swap in swaps:
        swap.wait_recv()
    ext[0, 0:4], ext[0, 36:40] = near_f[0, 28:32], near_f[0, 0:4]
    ext[1, 0:4], ext[1, 36:40] = near_c[0, 28:32], near_c[0, 0:4]
    ext[2, 0:4], ext[2, 36:40] = near_k[28:32].astype(f32), near_k[0:4].astype(f32)

    row_16 = lax.broadcasted_iota(jnp.int32, (16, 128), 0)
    lane_16 = lanes_of((16, 128))
    own_lanes = lax.div(lane_16, 8) == row_16
    for i in range(3):
        for t in range(3):
            turned = pltpu.roll(ext[i, 16 * t : 16 * t + 16], 4, 1, stride=8, stride_axis=0)
            pack_out[3 * i + t : 3 * i + t + 1] = jnp.sum(jnp.where(own_lanes, turned, 0.0), axis=0, keepdims=True)
    pack_out[9:16] = jnp.zeros((7, 128), f32)
    posts = [
        pltpu.make_async_remote_copy(src_ref=pack_out, dst_ref=pack_in.at[i], send_sem=sem_p.at[0, i], recv_sem=sem_p.at[1, i], device_id=who, device_id_type=MESH)
        for i, who in ((1, left), (0, right))
    ]
    for post in posts:
        post.start()

    load.wait()
    halves_swap.wait_recv()
    n_cols = prior_ref.shape[2]
    whole = n_cols // 128 * 128

    def pair_sum(r, _):
        at = pl.multiple_of(80 * r, 16)
        for j in range(4):
            cols = slice(2048 * j, 2048 * j + 2048)
            value = c_own[r, :, cols] + c_in[r, :, cols]
            xs[pl.ds(at + 16 * j, 16)] = value.reshape(16, 128).astype(bf)
        value = (c_own[r, :, 8192:whole] + c_in[r, :, 8192:whole]).reshape((whole - 8192) // 128, 128)
        last = c_own[r, :, whole:] + c_in[r, :, whole:]
        last = jnp.concatenate([last, jnp.zeros((1, whole + 128 - n_cols), f32)], axis=1)
        value = jnp.concatenate([value, last, jnp.zeros((16 - 1 - value.shape[0], 128), f32)], axis=0)
        xs[pl.ds(at + 64, 16)] = value.astype(bf)
        return 0

    lax.fori_loop(0, share, pair_sum, 0)
    xs[80 * share :] = jnp.zeros((xs.shape[0] - 80 * share, 128), bf)

    def send_plane(i, _):
        to_plane(lax.rem(p + i, n_p), p).start()
        return 0

    lax.fori_loop(1, n_p, send_plane, 0)

    for post in posts:
        post.wait_recv()
    column = lax.rem(lane_16, 8)
    own = pack_out[...]
    slab_l = jnp.where(column >= 4, own, pack_in[0])
    slab_r = jnp.where(column < 4, own, pack_in[1])

    def flat(slab, i):
        return jnp.concatenate([slab[3 * i + t : 3 * i + t + 1] for t in range(3)], axis=1)

    def flat_both(i):
        return jnp.concatenate([flat(slab_l, i), flat(slab_r, i)], axis=1)

    field_s, cot_s, frozen_s = flat_both(0), flat_both(1), flat_both(2)
    masked_s = field_s * frozen_s

    def both_rolled(value, offset):
        return jnp.concatenate([flat_roll(value[:, :384], offset), flat_roll(value[:, 384:], offset)], axis=1)

    def unflat(vector, e):
        parts = []
        for t in range(3):
            spread = jnp.broadcast_to(vector[:, 128 * t : 128 * t + 128], (16, 128))
            parts.append(jnp.sum(jnp.where(lane_16 == 8 * row_16 + e, spread, 0.0), axis=1, keepdims=True))
        return jnp.concatenate(parts, axis=0)

    masked = ext[0] * ext[2]
    lane_48 = lanes_of((48, 128))
    shifts = (
        jnp.where(lane_48 == 0, unflat(masked_s[:, :384], 3), pltpu.roll(masked, 1, 1)),
        masked,
        jnp.where(lane_48 == 127, unflat(masked_s[:, 384:], 4), pltpu.roll(masked, 127, 1)),
    )
    taps[...] = jnp.zeros(taps.shape, f32)
    edge_taps[...] = jnp.zeros(edge_taps.shape, f32)
    for a in range(3):
        for b in range(3):
            k = 3 * a + b
            taps[pl.ds(16 + k, 38, stride=16), :] = shifts[b][a : a + 38]
            edge_taps[k : k + 1, :] = both_rolled(masked_s, 8 * (a - 1) + b - 1)

    def first(tap_values):
        high, low = halves(tap_values)
        return jnp.tanh(dot(w_one, jnp.concatenate([high, low, high], axis=0))).astype(bf)

    lane_384 = lanes_of((32, 384))

    def spread_edges(value, back, store):
        for a in range(3):
            for b in range(3):
                k = 3 * a + b
                offset = 8 * (a - 1) + (1 - b if back else b - 1)
                store[32 * k : 32 * k + 32, :] = both_rolled(value, offset).astype(bf)
        mixed = jnp.where(lax.rem(lane_384, 8) == 4, flat_roll(value[:, :384], -1), flat_roll(value[:, 384:], 1))
        for t in range(3):
            cp[t] = mixed[:, 128 * t : 128 * t + 128]

    lane_32 = lanes_of((32, 128))

    def spread_row(q, value, back, store):
        edge = pltpu.roll(cp[lax.div(q, 16)], lax.rem(252 - 8 * lax.rem(q, 16), 128), 1)
        before = jnp.where(lane_32 == 0, edge, pltpu.roll(value, 1, 1)).astype(bf)
        after = jnp.where(lane_32 == 127, edge, pltpu.roll(value, 127, 1)).astype(bf)
        store[q, 0:32] = after if back else before
        store[q, 32:64] = value.astype(bf)
        store[q, 64:96] = before if back else after

    one_s = first(edge_taps[...])
    spread_edges(one_s.astype(f32), False, xs_one)

    def one_rows(rows):
        values = jnp.concatenate([taps[pl.ds(pl.multiple_of(16 * q, 16), 16), :] for q in rows], axis=1)
        out = first(values).astype(f32)
        for i, q in enumerate(rows):
            spread_row(q, out[:, 128 * i : 128 * i + 128], False, xm)

    def over_rows(step, first_group=0, last_group=8):
        def body(i, _):
            step([4 + 4 * i + n for n in range(4)])
            return 0

        lax.fori_loop(first_group, last_group, body, 0)

    for q in (0, 39):
        xm[q] = jnp.zeros((96, 128), bf)
    one_rows([1, 2, 3, 36])
    one_rows([37, 38])
    over_rows(one_rows)

    def second(windows, field, cot, frozen):
        two = jnp.tanh(dot(w2[...], windows)).astype(bf)
        pair = dot(head, two)
        expo = jnp.exp(pair[0:1])
        open_cot = (1.0 - frozen) * cot
        d_0 = (open_cot * field * expo).astype(bf)
        d_1 = open_cot.astype(bf)
        two_f = two.astype(f32)
        d_two = (head_0 * d_0.astype(f32) + head_1 * d_1.astype(f32)) * (1.0 - two_f * two_f)
        return two, pair, d_0, d_1, d_two.astype(bf).astype(f32)

    _, _, _, _, d_two_s = second(xs_one[...], field_s, cot_s, frozen_s)
    spread_edges(d_two_s, True, xds)

    def windows_of(store, rows):
        return jnp.concatenate([store[pl.ds(q - 1, 3)].reshape(288, 128) for q in rows], axis=1)

    def rows_of(i, rows):
        return jnp.concatenate([ext[i, pl.ds(q, 1), :] for q in rows], axis=1)

    acc_mid[...] = jnp.zeros(acc_mid.shape, f32)
    b_rows[...] = jnp.zeros(b_rows.shape, f32)

    def two_rows(rows, inner=True):
        two, pair, d_0, d_1, d_two = second(windows_of(xm, rows), rows_of(0, rows), rows_of(1, rows), rows_of(2, rows))
        for i, q in enumerate(rows):
            at = slice(128 * i, 128 * i + 128)
            spread_row(q, d_two[:, at], True, xd)
            if inner:
                pair_rows[pl.ds(pl.multiple_of(8 * q, 8), 2), :] = pair[:, at]
        if inner:
            b_rows[297:299, 0:32] += nt(jnp.concatenate([d_0, d_1], axis=0), two)

    for q in (0, 1, 38, 39):
        xd[q] = jnp.zeros((96, 128), bf)
    two_rows([2, 3, 36, 37], inner=False)
    over_rows(two_rows, 0, 4)
    def take_plane(i, total):
        q = lax.rem(p + n_p - i, n_p)
        to_plane(q, q).wait_recv()
        return total + xr[q].astype(f32)

    total = lax.fori_loop(1, n_p, take_plane, xs[chunk(p)].astype(f32))
    zs[...] = total.astype(bf).reshape(4, 16, 128)

    def send_along(i, _):
        to_along(lax.rem(z + i, n_z), z).start()
        return 0

    lax.fori_loop(1, n_z, send_along, 0)
    over_rows(two_rows, 4, 8)

    def third(windows, one):
        one_f = one.astype(f32)
        d_one = dot(w3[...], windows) * (1.0 - one_f * one_f)
        high, low = halves(d_one)
        return high, low, dot(w_back, jnp.concatenate([high, low, high], axis=0))

    _, _, t_s = third(xds[...], one_s)

    def three_rows(rows, inner=True):
        windows = windows_of(xd, rows)
        one = jnp.concatenate([xm[q, 32:64] for q in rows], axis=1)
        high, low, t_values = third(windows, one)
        for i, q in enumerate(rows):
            t_rows[pl.ds(pl.multiple_of(16 * q, 16), 16), :] = t_values[:, 128 * i : 128 * i + 128]
        if inner:
            acc_mid[...] += nt(windows, one)
            values = jnp.concatenate([taps[pl.ds(pl.multiple_of(16 * q, 16), 16), :] for q in rows], axis=1)
            m_high, m_low = halves(values)
            parts = nt(jnp.concatenate([m_high, m_low], axis=0), jnp.concatenate([high, low], axis=0))
            parts = parts[0:16] + parts[16:32]
            b_rows[0:9, 0:32] += (parts[:, 0:32] + parts[:, 32:64])[0:9]

    three_rows([3, 36], inner=False)
    over_rows(three_rows)

    for j in range(3):
        b_rows[9 + 96 * (2 - j) : 9 + 96 * (2 - j) + 96, 0:32] = acc_mid[96 * j : 96 * j + 96]
    rows = mine.shape[0]
    layer = b_rows[pl.ds(0, rows, stride=4), :]
    for g in range(1, 4):
        layer = layer + pltpu.roll(b_rows[pl.ds(g, rows, stride=4), :], 32 * g, 1)
    mine[...] = layer * scale

    mine_swap = remote(mine, mine_in, sem_l.at[0], sem_l.at[1], partner)
    mine_swap.start()

    def column_sum(b):
        total = None
        for a in range(3):
            part = t_rows[pl.ds(16 * (5 - a) + 3 * a + b, 32, stride=16), :]
            total = part if total is None else total + part
        return total

    def edge_sum(b, side):
        total = None
        for a in range(3):
            k = 3 * a + b
            part = flat_roll(t_s[k : k + 1, 384 * side : 384 * side + 384], 8 * (1 - a))
            total = part if total is None else total + part
        return total

    lane = lanes_of((32, 128))
    from_right = unflat(edge_sum(0, 1), 4)[4:36]
    from_left = unflat(edge_sum(2, 0), 3)[4:36]
    d_masked = (
        jnp.where(lane == 127, from_right, pltpu.roll(column_sum(0), 127, 1))
        + column_sum(1)
        + jnp.where(lane == 0, from_left, pltpu.roll(column_sum(2), 1, 1))
    )
    frozen = check_ref[...].astype(f32)
    unfrozen = 1.0 - frozen
    expo = jnp.exp(pair_rows[pl.ds(32, 32, stride=8), :])
    offset = pair_rows[pl.ds(33, 32, stride=8), :]
    values, cot = field_ref[0], cot_ref[0]
    coupled_ref[0] = frozen * values + unfrozen * (values * expo + offset)
    fgrad_ref[0] = frozen * cot + unfrozen * cot * expo + frozen * d_masked


    mine_swap.wait()
    for i in range(UNITS // 2):
        unit = 2 * i + core
        own_sum[unit] = mine[chunk(unit, 8)] + mine_in[chunk(unit, 8)]

    def to_owner(i, slot):
        unit = 2 * i + core
        return remote(own_sum.at[unit], mine_x.at[slot], sem_lx.at[0, i], sem_lx.at[1, slot], plane(unit))

    for i in range(UNITS // 2):

        @pl.when(2 * i + core != p)
        def _():
            to_owner(i, p).start()

    tile = lax.rem(z, 4)

    def take_along(i, total):
        w = lax.rem(z + n_z - i, n_z)
        to_along(w, w).wait_recv()
        return total + zr[w].astype(f32)

    total = lax.fori_loop(1, n_z, take_along, zs[tile].astype(f32))
    fin[core, chunk(4 * p + tile, 16)] = total.astype(bf)

    def to_four(i, slot):
        w = z - tile + lax.rem(tile + i, 4)
        at = chunk(4 * p + slot, 16)
        return remote(fin.at[core, chunk(4 * p + tile, 16)], fin.at[core, at], sem_t.at[0, i], sem_t.at[1, slot], along(w))

    for i in range(1, 4):
        to_four(i, tile).start()

    is_owner = (p < UNITS) & (lax.rem(p, 2) == core)

    def to_along_mine(w, slot):
        return remote(mine_x.at[p], mine_z.at[slot], sem_lz.at[0, w], sem_lz.at[1, slot], along(w))

    @pl.when(is_owner)
    def _():
        def take(i, total):
            q = lax.rem(p + n_p - i, n_p)
            to_owner(lax.div(p, 2), q).wait_recv()
            return total + mine_x[q]

        mine_x[p] = lax.fori_loop(1, n_p, take, own_sum[p])

        def send(i, _):
            to_along_mine(lax.rem(z + i, n_z), z).start()
            return 0

        lax.fori_loop(1, n_z, send, 0)

    for i in range(1, 4):
        to_four(i, lax.rem(tile + i, 4)).wait_recv()

    def all_plane(q, slot):
        return remote(fin.at[core, chunk(p)], fin.at[core, chunk(slot)], sem_a.at[0, q], sem_a.at[1, slot], plane(q))

    def to_partner(which, slot):
        return remote(fin.at[core, chunk(slot)], fin.at[which, chunk(slot)], sem_b.at[0, slot], sem_b.at[1, slot], partner)

    def send_all(i, _):
        all_plane(lax.rem(p + i, n_p), p).start()
        return 0

    lax.fori_loop(1, n_p, send_all, 0)
    to_partner(core, p).start()

    def take_all(i, _):
        q = lax.rem(p + n_p - i, n_p)
        all_plane(q, q).wait_recv()
        to_partner(core, q).start()
        return 0

    lax.fori_loop(1, n_p, take_all, 0)

    def to_all_mine(q, which, unit):
        return remote(mine_fin.at[unit], mine_fin.at[unit], sem_la.at[which, q], sem_lr.at[unit], plane(q, which))

    @pl.when(is_owner)
    def _():
        def take(i, total):
            w = lax.rem(z + n_z - i, n_z)
            to_along_mine(w, w).wait_recv()
            return total + mine_z[w]

        mine_fin[p] = lax.fori_loop(1, n_z, take, mine_x[p])

        def send(i, _):
            q = lax.rem(p + i, n_p)
            to_all_mine(q, core, p).start()
            to_all_mine(q, other, p).start()
            return 0

        lax.fori_loop(1, n_p, send, 0)
        to_all_mine(p, other, p).start()

    base = 80 * (1 + skip * core)
    for_other = 80 * (1 + skip * other)
    used = 80 * share // 64

    def widen(q, _):
        wide[pl.ds(pl.multiple_of(base + 64 * q, 16), 64)] = fin[core, chunk(q)].astype(f32)
        return 0

    def widen_other(q, _):
        to_partner(other, q).wait_recv()
        wide[pl.ds(pl.multiple_of(for_other + 64 * q, 16), 64)] = fin[other, chunk(q)].astype(f32)
        return 0

    lax.fori_loop(0, used, widen, 0)
    lax.fori_loop(0, used, widen_other, 0)
    for q in range(used, n_p):
        to_partner(other, q).wait_recv()

    for unit in range(UNITS):

        @pl.when((p != unit) | (core != unit % 2))
        def _():
            to_all_mine(p, other, unit).wait_recv()

        wide[8 * unit : 8 * unit + 8] = mine_fin[unit]

    def unpack(k, _):
        out_ref[:, pl.ds(pl.multiple_of(k * 128, 128), 128)] = wide[pl.ds(k, 24, stride=80), :]
        return 0

    lax.fori_loop(0, whole // 128, unpack, 0)
    out_ref[:, whole:] = wide[pl.ds(whole // 128, 24, stride=80), :][:, : n_cols - whole]

    for copy in (*swaps, *posts, halves_swap):
        copy.wait_send()

    def drain_plane(i, _):
        q = lax.rem(p + i, n_p)
        to_plane(q, p).wait_send()
        all_plane(q, p).wait_send()
        return 0

    def drain_along(i, _):
        to_along(lax.rem(z + i, n_z), z).wait_send()
        return 0

    def drain_partner(q, _):
        to_partner(core, q).wait_send()
        return 0

    lax.fori_loop(1, n_p, drain_plane, 0)
    lax.fori_loop(1, n_z, drain_along, 0)
    lax.fori_loop(0, n_p, drain_partner, 0)
    for i in range(1, 4):
        to_four(i, tile).wait_send()
    for i in range(UNITS // 2):

        @pl.when(2 * i + core != p)
        def _():
            to_owner(i, p).wait_send()

    @pl.when(is_owner)
    def _():
        def drain_z(i, _):
            to_along_mine(lax.rem(z + i, n_z), z).wait_send()
            return 0

        def drain_all(i, _):
            q = lax.rem(p + i, n_p)
            to_all_mine(q, core, p).wait_send()
            to_all_mine(q, other, p).wait_send()
            return 0

        lax.fori_loop(1, n_z, drain_z, 0)
        lax.fori_loop(1, n_p, drain_all, 0)
        to_all_mine(p, other, p).wait_send()


def fused_call(scale, field, cot, checker, weight_in, weight_mid, weight_head, prior):
    f32, bf = jnp.float32, jnp.bfloat16
    sem = pltpu.SemaphoreType.DMA
    vmem = pl.BlockSpec(memory_space=pltpu.VMEM)
    n_p, n_z = 2 * lax.axis_size("gy"), lax.axis_size("dp") // 2
    rows, _, cols = prior.shape
    share = (rows + 1) // 2
    return pl.pallas_call(
        functools.partial(fused_kernel, scale),
        out_shape=(
            jax.ShapeDtypeStruct(field.shape, f32),
            jax.ShapeDtypeStruct(field.shape, f32),
            jax.ShapeDtypeStruct((rows + 1, cols), f32),
        ),
        in_specs=[vmem] * 6 + [pl.BlockSpec(memory_space=pl.ANY)],
        out_specs=(vmem,) * 3,
        scratch_shapes=[
            pltpu.VMEM(field.shape, f32), pltpu.VMEM(field.shape, f32), pltpu.VMEM(checker.shape, jnp.int32),
            pltpu.VMEM((3, 48, 128), f32),
            pltpu.VMEM((16, 128), f32), pltpu.VMEM((2, 16, 128), f32),
            pltpu.VMEM((640, 128), f32), pltpu.VMEM((16, 768), f32),
            pltpu.VMEM((16, 128), f32), pltpu.VMEM((32, 288), bf), pltpu.VMEM((32, 288), bf),
            pltpu.VMEM((40, 96, 128), bf), pltpu.VMEM((288, 768), bf),
            pltpu.VMEM((40, 96, 128), bf), pltpu.VMEM((288, 768), bf),
            pltpu.VMEM((3, 32, 128), f32),
            pltpu.VMEM((320, 128), f32), pltpu.VMEM((640, 128), f32),
            pltpu.VMEM((288, 32), f32), pltpu.VMEM((320, 128), f32),
            pltpu.VMEM((share, 1, cols), f32), pltpu.VMEM((share, 1, cols), f32),
            pltpu.VMEM((n_p * 64, 128), bf), pltpu.VMEM((n_p, 64, 128), bf),
            pltpu.VMEM((4, 16, 128), bf), pltpu.VMEM((n_z, 16, 128), bf),
            pltpu.VMEM((2, n_p * 64, 128), bf), pltpu.VMEM((80 * (rows + 1), 128), f32),
            pltpu.VMEM((80, 128), f32), pltpu.VMEM((80, 128), f32),
            pltpu.VMEM((n_p, 8, 128), f32), pltpu.VMEM((n_z, 8, 128), f32),
            pltpu.VMEM((UNITS, 8, 128), f32), pltpu.VMEM((UNITS, 8, 128), f32),
            sem((2, 3)), sem((2, 2)), sem, sem((2,)), sem((2, n_p)), sem((2, n_z)), sem((2, 4)), sem((2, n_p)), sem((2, n_p)),
            sem((2,)), sem((2, n_p)), sem((2, n_z)), sem((2, n_p)), sem((UNITS,)),
        ],
        compiler_params=pltpu.CompilerParams(collective_id=0, has_side_effects=True),
    )(field, cot, checker, weight_in, weight_mid, weight_head, prior)


def on_device(field, cotangent, checker, weight_in, weight_mid, weight_head, prior_grads):
    cell_total = field.size * lax.axis_size("dp") * lax.axis_size("gx") * lax.axis_size("gy")
    scale = 1.0 / math.sqrt(cell_total)
    prior = prior_grads.reshape(prior_grads.shape[3], 1, prior_grads.shape[4])
    return fused_call(scale, field, cotangent, checker, weight_in, weight_mid, weight_head, prior)


def solution(mesh):
    placed = (
        P("dp", "gx", "gy"),
        P("dp", "gx", "gy"),
        P("gx", "gy"),
        P(),
        P(),
        P(),
        P("dp", "gx", "gy", None, None),
    )
    return jax.shard_map(
        on_device,
        mesh=mesh,
        in_specs=placed,
        out_specs=(P("dp", "gx", "gy"), P("dp", "gx", "gy"), P()),
        check_vma=False,
    )
```

```python
import functools
import itertools
import math

import jax
import jax.numpy as jnp
from jax import lax
from jax.experimental import pallas as pl
from jax.experimental.pallas import tpu as pltpu
from jax.sharding import PartitionSpec as P

MESH = pl.DeviceIdType.MESH
UNITS = 10


def ring_distance(offset, size):
    return min(offset, size - offset)


def farthest_first(*sizes):
    offsets = [at for at in itertools.product(*(range(n) for n in sizes)) if any(at)]
    return sorted(offsets, key=lambda at: -sum(ring_distance(o, n) for o, n in zip(at, sizes)))


def flat_roll(value, offset):
    return pltpu.roll(value, (-offset) % value.shape[-1], value.ndim - 1)


def halves(value):
    high = value.astype(jnp.bfloat16)
    return high, (value - high.astype(jnp.float32)).astype(jnp.bfloat16)


def nt(a, b, **how):
    return lax.dot_general(a, b, (((1,), (1,)), ((), ())), preferred_element_type=jnp.float32, **how)


def dot(a, b):
    return jnp.dot(a, b, preferred_element_type=jnp.float32)


def lanes_of(shape):
    return lax.broadcasted_iota(jnp.int32, shape, len(shape) - 1)


def fused_kernel(scale, field_ref, cot_ref, check_ref, win_ref, wmid_ref, whead_ref, prior_ref,
                 coupled_ref, fgrad_ref, fin, mine_fin,
                 near_f, near_c, near_k, ext, pack_out, pack_in, taps, edge_taps, w9, w2, w3,
                 xm, xs_one, xd, xds, cp, pair_rows, t_rows, acc_mid, b_rows,
                 c_own, c_in, xs, xr, zs, zr, mine, mine_x, mine_z, own_sum,
                 sem_r, sem_p, sem_own, sem_c, sem_x, sem_z, sem_t, sem_a, sem_b, sem_l, sem_lx, sem_lz, sem_la, sem_lr):
    f32, bf = jnp.float32, jnp.bfloat16
    dp, core, gy = lax.axis_index("dp"), lax.axis_index("gx"), lax.axis_index("gy")
    n_gy = lax.axis_size("gy")
    n_z = lax.axis_size("dp") // 2
    n_p = 2 * n_gy
    z = lax.rem(dp, n_z)
    p = lax.div(dp, n_z) * n_gy + gy
    other = 1 - core
    share = c_own.shape[0]

    n_x, n_y = n_gy // 2, 4
    at_x, at_y = lax.div(gy, 2), 2 * lax.rem(gy, 2) + lax.div(dp, n_z)
    plane_order = farthest_first(n_x, n_y)
    line_order = [w for (w,) in farthest_first(n_z)]

    def beside(dx, dy):
        to_x, to_y = lax.rem(at_x + dx, n_x), lax.rem(at_y + dy, n_y)
        return lax.rem(to_y, 2) * n_gy + 2 * to_x + lax.div(to_y, 2)

    def from_beside(dx, dy):
        return beside(n_x - dx, n_y - dy)

    def plane(q, which=core):
        return {"dp": lax.div(q, n_gy) * n_z + z, "gx": which, "gy": lax.rem(q, n_gy)}

    def along(w):
        return {"dp": dp - z + w, "gx": core, "gy": gy}

    def chunk(q, rows=64):
        return pl.ds(pl.multiple_of(rows * q, rows), rows)

    partner = {"dp": dp, "gx": other, "gy": gy}
    left = {"dp": dp, "gx": core, "gy": lax.rem(gy + n_gy - 1, n_gy)}
    right = {"dp": dp, "gx": core, "gy": lax.rem(gy + 1, n_gy)}
    barrier = pltpu.get_barrier_semaphore()

    def hello(who):
        pl.semaphore_signal(barrier, inc=1, device_id=who, device_id_type=MESH)

    def hello_along(i, _):
        hello(along(lax.rem(z + i, n_z)))
        return 0

    def hello_plane(i, _):
        hello(plane(lax.rem(p + i, n_p)))
        hello(plane(lax.rem(p + i, n_p), other))
        return 0

    lax.fori_loop(1, n_z, hello_along, 0)
    lax.fori_loop(1, n_p, hello_plane, 0)
    hello(partner)

    def remote(src, dst, sends, recvs, who):
        return pltpu.make_async_remote_copy(src_ref=src, dst_ref=dst, send_sem=sends, recv_sem=recvs, device_id=who, device_id_type=MESH)

    skip = prior_ref.shape[0] - share
    load = pltpu.make_async_copy(prior_ref.at[pl.ds(skip * core, share)], c_own, sem_own)
    load.start()

    def to_plane(q, slot):
        return remote(xs.at[chunk(q)], xr.at[slot], sem_x.at[0, q], sem_x.at[1, slot], plane(q))

    def to_along(w, slot):
        return remote(zs.at[lax.rem(w, 4)], zr.at[slot], sem_z.at[0, w], sem_z.at[1, slot], along(w))

    for a in range(3):
        w9[3 * a : 3 * a + 3, 0:32] = win_ref[a]
    w9[9:16, 0:32] = jnp.zeros((7, 32), f32)
    eye_f = (lax.broadcasted_iota(jnp.int32, (32, 32), 0) == lanes_of((32, 32))).astype(f32)
    eye = eye_f.astype(bf)
    w_taps = w9[:, 0:32]
    taps_t = nt(eye_f, w_taps, precision=lax.Precision.HIGHEST)
    th, tl = halves(taps_t)
    w_one = jnp.concatenate([th, th, tl], axis=1)
    wh, wl = halves(w_taps)
    w_back = jnp.concatenate([wh, wh, wl], axis=1)
    head = whead_ref[...]
    head_t = nt(eye, head)
    head_0, head_1 = head_t[:, 0:1], head_t[:, 1:2]
    for a in range(3):
        for b in range(3):
            k = 3 * a + b
            w2[:, 32 * k : 32 * k + 32] = wmid_ref[a, b]
            kb = 3 * (2 - a) + b
            w3[:, 32 * kb : 32 * kb + 32] = wmid_ref[a, b].astype(f32).T.astype(bf)

    zeros = jnp.zeros((8, 128), f32)
    for i in range(3):
        ext[i, 40:48] = zeros
    ext[0, 4:36] = field_ref[0]
    ext[1, 4:36] = cot_ref[0]
    ext[2, 4:36] = check_ref[...].astype(f32)
    pl.semaphore_wait(barrier, 1 + 2 * (n_p - 1) + (n_z - 1))
    swaps = [
        pltpu.make_async_remote_copy(src_ref=src, dst_ref=dst, send_sem=sem_r.at[0, i], recv_sem=sem_r.at[1, i], device_id=partner, device_id_type=MESH)
        for i, (src, dst) in enumerate(((field_ref, near_f), (cot_ref, near_c), (check_ref, near_k)))
    ]
    for swap in swaps:
        swap.start()
    halves_swap = remote(prior_ref.at[pl.ds(skip * other, share)], c_in, sem_c.at[0], sem_c.at[1], partner)
    halves_swap.start()
    for swap in swaps:
        swap.wait_recv()
    ext[0, 0:4], ext[0, 36:40] = near_f[0, 28:32], near_f[0, 0:4]
    ext[1, 0:4], ext[1, 36:40] = near_c[0, 28:32], near_c[0, 0:4]
    ext[2, 0:4], ext[2, 36:40] = near_k[28:32].astype(f32), near_k[0:4].astype(f32)

    row_16 = lax.broadcasted_iota(jnp.int32, (16, 128), 0)
    lane_16 = lanes_of((16, 128))
    own_lanes = lax.div(lane_16, 8) == row_16
    for i in range(3):
        for t in range(3):
            turned = pltpu.roll(ext[i, 16 * t : 16 * t + 16], 4, 1, stride=8, stride_axis=0)
            pack_out[3 * i + t : 3 * i + t + 1] = jnp.sum(jnp.where(own_lanes, turned, 0.0), axis=0, keepdims=True)
    pack_out[9:16] = jnp.zeros((7, 128), f32)
    posts = [
        pltpu.make_async_remote_copy(src_ref=pack_out, dst_ref=pack_in.at[i], send_sem=sem_p.at[0, i], recv_sem=sem_p.at[1, i], device_id=who, device_id_type=MESH)
        for i, who in ((1, left), (0, right))
    ]
    for post in posts:
        post.start()

    load.wait()
    halves_swap.wait_recv()
    n_cols = prior_ref.shape[2]
    whole = n_cols // 128 * 128

    def pair_sum(r, _):
        at = pl.multiple_of(80 * r, 16)
        for j in range(4):
            cols = slice(2048 * j, 2048 * j + 2048)
            value = c_own[r, :, cols] + c_in[r, :, cols]
            xs[pl.ds(at + 16 * j, 16)] = value.reshape(16, 128).astype(bf)
        value = (c_own[r, :, 8192:whole] + c_in[r, :, 8192:whole]).reshape((whole - 8192) // 128, 128)
        last = c_own[r, :, whole:] + c_in[r, :, whole:]
        last = jnp.concatenate([last, jnp.zeros((1, whole + 128 - n_cols), f32)], axis=1)
        value = jnp.concatenate([value, last, jnp.zeros((16 - 1 - value.shape[0], 128), f32)], axis=0)
        xs[pl.ds(at + 64, 16)] = value.astype(bf)
        return 0

    lax.fori_loop(0, share, pair_sum, 0)
    xs[80 * share :] = jnp.zeros((xs.shape[0] - 80 * share, 128), bf)

    for offset in plane_order:
        to_plane(beside(*offset), p).start()

    for post in posts:
        post.wait_recv()
    column = lax.rem(lane_16, 8)
    own = pack_out[...]
    slab_l = jnp.where(column >= 4, own, pack_in[0])
    slab_r = jnp.where(column < 4, own, pack_in[1])

    def flat(slab, i):
        return jnp.concatenate([slab[3 * i + t : 3 * i + t + 1] for t in range(3)], axis=1)

    def flat_both(i):
        return jnp.concatenate([flat(slab_l, i), flat(slab_r, i)], axis=1)

    field_s, cot_s, frozen_s = flat_both(0), flat_both(1), flat_both(2)
    masked_s = field_s * frozen_s

    def both_rolled(value, offset):
        return jnp.concatenate([flat_roll(value[:, :384], offset), flat_roll(value[:, 384:], offset)], axis=1)

    def unflat(vector, e):
        parts = []
        for t in range(3):
            spread = jnp.broadcast_to(vector[:, 128 * t : 128 * t + 128], (16, 128))
            parts.append(jnp.sum(jnp.where(lane_16 == 8 * row_16 + e, spread, 0.0), axis=1, keepdims=True))
        return jnp.concatenate(parts, axis=0)

    masked = ext[0] * ext[2]
    lane_48 = lanes_of((48, 128))
    shifts = (
        jnp.where(lane_48 == 0, unflat(masked_s[:, :384], 3), pltpu.roll(masked, 1, 1)),
        masked,
        jnp.where(lane_48 == 127, unflat(masked_s[:, 384:], 4), pltpu.roll(masked, 127, 1)),
    )
    taps[...] = jnp.zeros(taps.shape, f32)
    edge_taps[...] = jnp.zeros(edge_taps.shape, f32)
    for a in range(3):
        for b in range(3):
            k = 3 * a + b
            taps[pl.ds(16 + k, 38, stride=16), :] = shifts[b][a : a + 38]
            edge_taps[k : k + 1, :] = both_rolled(masked_s, 8 * (a - 1) + b - 1)

    def first(tap_values):
        high, low = halves(tap_values)
        return jnp.tanh(dot(w_one, jnp.concatenate([high, low, high], axis=0))).astype(bf)

    lane_384 = lanes_of((32, 384))

    def spread_edges(value, back, store):
        for a in range(3):
            for b in range(3):
                k = 3 * a + b
                offset = 8 * (a - 1) + (1 - b if back else b - 1)
                store[32 * k : 32 * k + 32, :] = both_rolled(value, offset).astype(bf)
        mixed = jnp.where(lax.rem(lane_384, 8) == 4, flat_roll(value[:, :384], -1), flat_roll(value[:, 384:], 1))
        for t in range(3):
            cp[t] = mixed[:, 128 * t : 128 * t + 128]

    lane_32 = lanes_of((32, 128))

    def spread_row(q, value, back, store):
        edge = pltpu.roll(cp[lax.div(q, 16)], lax.rem(252 - 8 * lax.rem(q, 16), 128), 1)
        before = jnp.where(lane_32 == 0, edge, pltpu.roll(value, 1, 1)).astype(bf)
        after = jnp.where(lane_32 == 127, edge, pltpu.roll(value, 127, 1)).astype(bf)
        store[q, 0:32] = after if back else before
        store[q, 32:64] = value.astype(bf)
        store[q, 64:96] = before if back else after

    one_s = first(edge_taps[...])
    spread_edges(one_s.astype(f32), False, xs_one)

    def one_rows(rows):
        values = jnp.concatenate([taps[pl.ds(pl.multiple_of(16 * q, 16), 16), :] for q in rows], axis=1)
        out = first(values).astype(f32)
        for i, q in enumerate(rows):
            spread_row(q, out[:, 128 * i : 128 * i + 128], False, xm)

    def over_rows(step, first_group=0, last_group=8):
        def body(i, _):
            step([4 + 4 * i + n for n in range(4)])
            return 0

        lax.fori_loop(first_group, last_group, body, 0)

    for q in (0, 39):
        xm[q] = jnp.zeros((96, 128), bf)
    one_rows([1, 2, 3, 36])
    one_rows([37, 38])
    over_rows(one_rows)

    def second(windows, field, cot, frozen):
        two = jnp.tanh(dot(w2[...], windows)).astype(bf)
        pair = dot(head, two)
        expo = jnp.exp(pair[0:1])
        open_cot = (1.0 - frozen) * cot
        d_0 = (open_cot * field * expo).astype(bf)
        d_1 = open_cot.astype(bf)
        two_f = two.astype(f32)
        d_two = (head_0 * d_0.astype(f32) + head_1 * d_1.astype(f32)) * (1.0 - two_f * two_f)
        return two, pair, d_0, d_1, d_two.astype(bf).astype(f32)

    _, _, _, _, d_two_s = second(xs_one[...], field_s, cot_s, frozen_s)
    spread_edges(d_two_s, True, xds)

    def windows_of(store, rows):
        return jnp.concatenate([store[pl.ds(q - 1, 3)].reshape(288, 128) for q in rows], axis=1)

    def rows_of(i, rows):
        return jnp.concatenate([ext[i, pl.ds(q, 1), :] for q in rows], axis=1)

    acc_mid[...] = jnp.zeros(acc_mid.shape, f32)
    b_rows[...] = jnp.zeros(b_rows.shape, f32)

    def two_rows(rows, inner=True):
        two, pair, d_0, d_1, d_two = second(windows_of(xm, rows), rows_of(0, rows), rows_of(1, rows), rows_of(2, rows))
        for i, q in enumerate(rows):
            at = slice(128 * i, 128 * i + 128)
            spread_row(q, d_two[:, at], True, xd)
            if inner:
                pair_rows[pl.ds(pl.multiple_of(8 * q, 8), 2), :] = pair[:, at]
        if inner:
            b_rows[297:299, 0:32] += nt(jnp.concatenate([d_0, d_1], axis=0), two)

    for q in (0, 1, 38, 39):
        xd[q] = jnp.zeros((96, 128), bf)
    two_rows([2, 3, 36, 37], inner=False)
    over_rows(two_rows, 0, 4)
    total = xs[chunk(p)].astype(f32)
    for offset in plane_order:
        q = from_beside(*offset)
        to_plane(q, q).wait_recv()
        total = total + xr[q].astype(f32)
    zs[...] = total.astype(bf).reshape(4, 16, 128)

    for offset in line_order:
        to_along(lax.rem(z + offset, n_z), z).start()
    over_rows(two_rows, 4, 8)

    def third(windows, one):
        one_f = one.astype(f32)
        d_one = dot(w3[...], windows) * (1.0 - one_f * one_f)
        high, low = halves(d_one)
        return high, low, dot(w_back, jnp.concatenate([high, low, high], axis=0))

    _, _, t_s = third(xds[...], one_s)

    def three_rows(rows, inner=True):
        windows = windows_of(xd, rows)
        one = jnp.concatenate([xm[q, 32:64] for q in rows], axis=1)
        high, low, t_values = third(windows, one)
        for i, q in enumerate(rows):
            t_rows[pl.ds(pl.multiple_of(16 * q, 16), 16), :] = t_values[:, 128 * i : 128 * i + 128]
        if inner:
            acc_mid[...] += nt(windows, one)
            values = jnp.concatenate([taps[pl.ds(pl.multiple_of(16 * q, 16), 16), :] for q in rows], axis=1)
            m_high, m_low = halves(values)
            parts = nt(jnp.concatenate([m_high, m_low], axis=0), jnp.concatenate([high, low], axis=0))
            parts = parts[0:16] + parts[16:32]
            b_rows[0:9, 0:32] += (parts[:, 0:32] + parts[:, 32:64])[0:9]

    three_rows([3, 36], inner=False)
    over_rows(three_rows)

    for j in range(3):
        b_rows[9 + 96 * (2 - j) : 9 + 96 * (2 - j) + 96, 0:32] = acc_mid[96 * j : 96 * j + 96]
    rows = mine.shape[0]
    layer = b_rows[pl.ds(0, rows, stride=4), :]
    for g in range(1, 4):
        layer = layer + pltpu.roll(b_rows[pl.ds(g, rows, stride=4), :], 32 * g, 1)
    mine[...] = layer * scale

    is_owner = (p < UNITS) & (lax.rem(p, 2) == core)

    def to_owner(unit, slot):
        return remote(mine.at[pl.ds(8 * unit, 8)], mine_x.at[slot], sem_l.at[unit], sem_lx.at[slot], plane(unit, unit % 2))

    def is_other(unit):
        return (p != unit) | (core != unit % 2)

    for unit in range(UNITS):

        @pl.when(is_other(unit))
        def _():
            to_owner(unit, n_p * core + p).start()

    def column_sum(b):
        total = None
        for a in range(3):
            part = t_rows[pl.ds(16 * (5 - a) + 3 * a + b, 32, stride=16), :]
            total = part if total is None else total + part
        return total

    def edge_sum(b, side):
        total = None
        for a in range(3):
            k = 3 * a + b
            part = flat_roll(t_s[k : k + 1, 384 * side : 384 * side + 384], 8 * (1 - a))
            total = part if total is None else total + part
        return total

    lane = lanes_of((32, 128))
    from_right = unflat(edge_sum(0, 1), 4)[4:36]
    from_left = unflat(edge_sum(2, 0), 3)[4:36]
    d_masked = (
        jnp.where(lane == 127, from_right, pltpu.roll(column_sum(0), 127, 1))
        + column_sum(1)
        + jnp.where(lane == 0, from_left, pltpu.roll(column_sum(2), 1, 1))
    )
    frozen = check_ref[...].astype(f32)
    unfrozen = 1.0 - frozen
    expo = jnp.exp(pair_rows[pl.ds(32, 32, stride=8), :])
    offset = pair_rows[pl.ds(33, 32, stride=8), :]
    values, cot = field_ref[0], cot_ref[0]
    coupled_ref[0] = frozen * values + unfrozen * (values * expo + offset)
    fgrad_ref[0] = frozen * cot + unfrozen * cot * expo + frozen * d_masked


    tile = lax.rem(z, 4)

    total = zs[tile].astype(f32)
    for offset in line_order:
        w = lax.rem(z + n_z - offset, n_z)
        to_along(w, w).wait_recv()
        total = total + zr[w].astype(f32)
    fin[core, chunk(4 * p + tile, 16)] = total.astype(bf)

    def to_four(i, slot):
        w = z - tile + lax.rem(tile + i, 4)
        at = chunk(4 * p + slot, 16)
        return remote(fin.at[core, chunk(4 * p + tile, 16)], fin.at[core, at], sem_t.at[0, i], sem_t.at[1, slot], along(w))

    for i in range(1, 4):
        to_four(i, tile).start()

    def to_along_mine(w, slot):
        return remote(own_sum, mine_z.at[slot], sem_lz.at[0, w], sem_lz.at[1, slot], along(w))

    @pl.when(is_owner)
    def _():
        def take(i, total):
            slot = lax.rem(n_p * core + p + i, 2 * n_p)
            to_owner(0, slot).wait_recv()
            return total + mine_x[slot]

        own_sum[...] = lax.fori_loop(1, 2 * n_p, take, mine[chunk(p, 8)])
        for offset in line_order:
            to_along_mine(lax.rem(z + offset, n_z), z).start()

    for i in range(1, 4):
        to_four(i, lax.rem(tile + i, 4)).wait_recv()

    def all_plane(q, slot):
        return remote(fin.at[core, chunk(p)], fin.at[core, chunk(slot)], sem_a.at[0, q], sem_a.at[1, slot], plane(q))

    def to_partner(which, slot):
        return remote(fin.at[core, chunk(slot)], fin.at[which, chunk(slot)], sem_b.at[0, slot], sem_b.at[1, slot], partner)

    for offset in plane_order:
        all_plane(beside(*offset), p).start()
    to_partner(core, p).start()
    for offset in plane_order:
        q = from_beside(*offset)
        all_plane(q, q).wait_recv()
        to_partner(core, q).start()

    def to_all_mine(q, which, unit):
        return remote(mine_fin.at[unit], mine_fin.at[unit], sem_la.at[which, q], sem_lr.at[unit], plane(q, which))

    @pl.when(is_owner)
    def _():
        def take(i, total):
            w = lax.rem(z + n_z - i, n_z)
            to_along_mine(w, w).wait_recv()
            return total + mine_z[w]

        mine_fin[p] = lax.fori_loop(1, n_z, take, own_sum[...])
        for offset in plane_order:
            to_all_mine(beside(*offset), core, p).start()
            to_all_mine(beside(*offset), other, p).start()
        to_all_mine(p, other, p).start()

    for q in range(n_p):
        to_partner(other, q).wait_recv()
    for unit in range(UNITS):

        @pl.when(is_other(unit))
        def _():
            to_all_mine(p, other, unit).wait_recv()

    for copy in (*swaps, *posts, halves_swap):
        copy.wait_send()

    def drain_plane(i, _):
        q = lax.rem(p + i, n_p)
        to_plane(q, p).wait_send()
        all_plane(q, p).wait_send()
        return 0

    def drain_along(i, _):
        to_along(lax.rem(z + i, n_z), z).wait_send()
        return 0

    def drain_partner(q, _):
        to_partner(core, q).wait_send()
        return 0

    lax.fori_loop(1, n_p, drain_plane, 0)
    lax.fori_loop(1, n_z, drain_along, 0)
    lax.fori_loop(0, n_p, drain_partner, 0)
    for i in range(1, 4):
        to_four(i, tile).wait_send()
    for unit in range(UNITS):

        @pl.when(is_other(unit))
        def _():
            to_owner(unit, n_p * core + p).wait_send()

    @pl.when(is_owner)
    def _():
        def drain_z(i, _):
            to_along_mine(lax.rem(z + i, n_z), z).wait_send()
            return 0

        def drain_all(i, _):
            q = lax.rem(p + i, n_p)
            to_all_mine(q, core, p).wait_send()
            to_all_mine(q, other, p).wait_send()
            return 0

        lax.fori_loop(1, n_z, drain_z, 0)
        lax.fori_loop(1, n_p, drain_all, 0)
        to_all_mine(p, other, p).wait_send()


def unpack_kernel(coupled_in, fgrad_in, fin, mine_fin, coupled_ref, fgrad_ref, out_ref, wide):
    coupled_ref[...] = coupled_in[...]
    fgrad_ref[...] = fgrad_in[...]
    n_rows, n_cols = out_ref.shape
    share = n_rows // 2
    for unit in range(UNITS):
        wide[8 * unit : 8 * unit + 8] = mine_fin[unit]
    for which in range(2):
        base = 80 * (1 + (n_rows - 1 - share) * which)

        def widen(r, _):
            rows = fin[which, pl.ds(pl.multiple_of(80 * r, 16), 80)].astype(jnp.float32)
            wide[pl.ds(pl.multiple_of(base + 80 * r, 16), 80)] = rows
            return 0

        lax.fori_loop(0, share, widen, 0, unroll=2)

    def unpack(k, _):
        out_ref[:, pl.ds(pl.multiple_of(k * 128, 128), 128)] = wide[pl.ds(k, n_rows, stride=80), :]
        return 0

    whole = n_cols // 128
    lax.fori_loop(0, whole, unpack, 0, unroll=2)
    out_ref[:, 128 * whole :] = wide[pl.ds(whole, n_rows, stride=80), :][:, : n_cols - 128 * whole]


def unpack_call(coupled, fgrad, fin, mine_fin, rows, cols):
    f32 = jnp.float32
    vmem = pl.BlockSpec(memory_space=pltpu.VMEM)
    return pl.pallas_call(
        unpack_kernel,
        out_shape=(
            jax.ShapeDtypeStruct(coupled.shape, f32),
            jax.ShapeDtypeStruct(fgrad.shape, f32),
            jax.ShapeDtypeStruct((rows, cols), f32),
        ),
        in_specs=[vmem] * 4,
        out_specs=(vmem,) * 3,
        scratch_shapes=[pltpu.VMEM((80 * rows, 128), f32)],
    )(coupled, fgrad, fin, mine_fin)


def fused_call(scale, field, cot, checker, weight_in, weight_mid, weight_head, prior):
    f32, bf = jnp.float32, jnp.bfloat16
    sem = pltpu.SemaphoreType.DMA
    vmem = pl.BlockSpec(memory_space=pltpu.VMEM)
    n_p, n_z = 2 * lax.axis_size("gy"), lax.axis_size("dp") // 2
    rows, _, cols = prior.shape
    share = (rows + 1) // 2
    return pl.pallas_call(
        functools.partial(fused_kernel, scale),
        out_shape=(
            jax.ShapeDtypeStruct(field.shape, f32),
            jax.ShapeDtypeStruct(field.shape, f32),
            jax.ShapeDtypeStruct((2, n_p * 64, 128), bf),
            jax.ShapeDtypeStruct((UNITS, 8, 128), f32),
        ),
        in_specs=[vmem] * 6 + [pl.BlockSpec(memory_space=pl.ANY)],
        out_specs=(vmem,) * 4,
        scratch_shapes=[
            pltpu.VMEM(field.shape, f32), pltpu.VMEM(field.shape, f32), pltpu.VMEM(checker.shape, jnp.int32),
            pltpu.VMEM((3, 48, 128), f32),
            pltpu.VMEM((16, 128), f32), pltpu.VMEM((2, 16, 128), f32),
            pltpu.VMEM((640, 128), f32), pltpu.VMEM((16, 768), f32),
            pltpu.VMEM((16, 128), f32), pltpu.VMEM((32, 288), bf), pltpu.VMEM((32, 288), bf),
            pltpu.VMEM((40, 96, 128), bf), pltpu.VMEM((288, 768), bf),
            pltpu.VMEM((40, 96, 128), bf), pltpu.VMEM((288, 768), bf),
            pltpu.VMEM((3, 32, 128), f32),
            pltpu.VMEM((320, 128), f32), pltpu.VMEM((640, 128), f32),
            pltpu.VMEM((288, 32), f32), pltpu.VMEM((320, 128), f32),
            pltpu.VMEM((share, 1, cols), f32), pltpu.VMEM((share, 1, cols), f32),
            pltpu.VMEM((n_p * 64, 128), bf), pltpu.VMEM((n_p, 64, 128), bf),
            pltpu.VMEM((4, 16, 128), bf), pltpu.VMEM((n_z, 16, 128), bf),
            pltpu.VMEM((80, 128), f32),
            pltpu.VMEM((2 * n_p, 8, 128), f32), pltpu.VMEM((n_z, 8, 128), f32),
            pltpu.VMEM((8, 128), f32),
            sem((2, 3)), sem((2, 2)), sem, sem((2,)), sem((2, n_p)), sem((2, n_z)), sem((2, 4)), sem((2, n_p)), sem((2, n_p)),
            sem((UNITS,)), sem((2 * n_p,)), sem((2, n_z)), sem((2, n_p)), sem((UNITS,)),
        ],
        compiler_params=pltpu.CompilerParams(collective_id=0, has_side_effects=True),
    )(field, cot, checker, weight_in, weight_mid, weight_head, prior)


def on_device(field, cotangent, checker, weight_in, weight_mid, weight_head, prior_grads):
    cell_total = field.size * lax.axis_size("dp") * lax.axis_size("gx") * lax.axis_size("gy")
    scale = 1.0 / math.sqrt(cell_total)
    prior = prior_grads.reshape(prior_grads.shape[3], 1, prior_grads.shape[4])
    sums = fused_call(scale, field, cotangent, checker, weight_in, weight_mid, weight_head, prior)
    return unpack_call(*sums, prior.shape[0] + 1, prior.shape[2])


def solution(mesh):
    placed = (
        P("dp", "gx", "gy"),
        P("dp", "gx", "gy"),
        P("gx", "gy"),
        P(),
        P(),
        P(),
        P("dp", "gx", "gy", None, None),
    )
    return jax.shard_map(
        on_device,
        mesh=mesh,
        in_specs=placed,
        out_specs=(P("dp", "gx", "gy"), P("dp", "gx", "gy"), P()),
        check_vma=False,
    )
```

```python
import functools
import itertools
import math

import jax
import jax.numpy as jnp
from jax import lax
from jax.experimental import pallas as pl
from jax.experimental.pallas import tpu as pltpu
from jax.sharding import PartitionSpec as P

MESH = pl.DeviceIdType.MESH
PIECES = 3
UNITS = 10


def ring_distance(offset, size):
    return min(offset, size - offset)


def farthest_first(*sizes):
    offsets = [at for at in itertools.product(*(range(n) for n in sizes)) if any(at)]
    return sorted(offsets, key=lambda at: -sum(ring_distance(o, n) for o, n in zip(at, sizes)))


def flat_roll(value, offset):
    return pltpu.roll(value, (-offset) % value.shape[-1], value.ndim - 1)


def halves(value):
    high = value.astype(jnp.bfloat16)
    return high, (value - high.astype(jnp.float32)).astype(jnp.bfloat16)


def nt(a, b, **how):
    return lax.dot_general(a, b, (((1,), (1,)), ((), ())), preferred_element_type=jnp.float32, **how)


def dot(a, b):
    return jnp.dot(a, b, preferred_element_type=jnp.float32)


def lanes_of(shape):
    return lax.broadcasted_iota(jnp.int32, shape, len(shape) - 1)


def fused_kernel(scale, field_ref, cot_ref, check_ref, win_ref, wmid_ref, whead_ref, prior_ref,
                 coupled_ref, fgrad_ref, fin, mine_fin, late_fin,
                 near_f, near_c, near_k, ext, pack_out, pack_in, taps, edge_taps, w9, w2, w3,
                 xm, xs_one, xd, xds, cp, pair_rows, t_rows, acc_mid, b_rows,
                 c_own, c_in, xs, xr, zs, zr, mine, mine_x, mine_z, own_sum, b_in, late_x, late_z,
                 sem_r, sem_p, sem_own, sem_c, sem_x, sem_z, sem_t, sem_a, sem_b, sem_l, sem_lx, sem_lz, sem_la, sem_mr, sem_ls, sem_lr, sem_lt):
    f32, bf = jnp.float32, jnp.bfloat16
    dp, core, gy = lax.axis_index("dp"), lax.axis_index("gx"), lax.axis_index("gy")
    n_gy = lax.axis_size("gy")
    n_z = lax.axis_size("dp") // 2
    n_p = 2 * n_gy
    z = lax.rem(dp, n_z)
    p = lax.div(dp, n_z) * n_gy + gy
    other = 1 - core
    share = c_own.shape[0]

    n_x, n_y = n_gy // 2, 4
    at_x, at_y = lax.div(gy, 2), 2 * lax.rem(gy, 2) + lax.div(dp, n_z)
    plane_order = farthest_first(n_x, n_y)
    line_order = [w for (w,) in farthest_first(n_z)]

    def beside(dx, dy):
        to_x, to_y = lax.rem(at_x + dx, n_x), lax.rem(at_y + dy, n_y)
        return lax.rem(to_y, 2) * n_gy + 2 * to_x + lax.div(to_y, 2)

    def from_beside(dx, dy):
        return beside(n_x - dx, n_y - dy)

    def plane(q, which=core):
        return {"dp": lax.div(q, n_gy) * n_z + z, "gx": which, "gy": lax.rem(q, n_gy)}

    def along(w):
        return {"dp": dp - z + w, "gx": core, "gy": gy}

    def chunk(q, rows=64):
        return pl.ds(pl.multiple_of(rows * q, rows), rows)

    partner = {"dp": dp, "gx": other, "gy": gy}
    left = {"dp": dp, "gx": core, "gy": lax.rem(gy + n_gy - 1, n_gy)}
    right = {"dp": dp, "gx": core, "gy": lax.rem(gy + 1, n_gy)}
    barrier = pltpu.get_barrier_semaphore()

    def hello(who):
        pl.semaphore_signal(barrier, inc=1, device_id=who, device_id_type=MESH)

    def hello_along(i, _):
        hello(along(lax.rem(z + i, n_z)))
        return 0

    def hello_plane(i, _):
        hello(plane(lax.rem(p + i, n_p)))
        hello(plane(lax.rem(p + i, n_p), other))
        return 0

    lax.fori_loop(1, n_z, hello_along, 0)
    lax.fori_loop(1, n_p, hello_plane, 0)
    hello(partner)

    def remote(src, dst, sends, recvs, who):
        return pltpu.make_async_remote_copy(src_ref=src, dst_ref=dst, send_sem=sends, recv_sem=recvs, device_id=who, device_id_type=MESH)

    skip = prior_ref.shape[0] - share
    load = pltpu.make_async_copy(prior_ref.at[pl.ds(skip * core, share)], c_own, sem_own)
    load.start()

    def to_plane(q, slot):
        return remote(xs.at[chunk(q)], xr.at[slot], sem_x.at[0, q], sem_x.at[1, slot], plane(q))

    def to_along(w, slot):
        return remote(zs.at[lax.rem(w, 4)], zr.at[slot], sem_z.at[0, w], sem_z.at[1, slot], along(w))

    for a in range(3):
        w9[3 * a : 3 * a + 3, 0:32] = win_ref[a]
    w9[9:16, 0:32] = jnp.zeros((7, 32), f32)
    eye_f = (lax.broadcasted_iota(jnp.int32, (32, 32), 0) == lanes_of((32, 32))).astype(f32)
    eye = eye_f.astype(bf)
    w_taps = w9[:, 0:32]
    taps_t = nt(eye_f, w_taps, precision=lax.Precision.HIGHEST)
    th, tl = halves(taps_t)
    w_one = jnp.concatenate([th, th, tl], axis=1)
    wh, wl = halves(w_taps)
    w_back = jnp.concatenate([wh, wh, wl], axis=1)
    head = whead_ref[...]
    head_t = nt(eye, head)
    head_0, head_1 = head_t[:, 0:1], head_t[:, 1:2]
    for a in range(3):
        for b in range(3):
            k = 3 * a + b
            w2[:, 32 * k : 32 * k + 32] = wmid_ref[a, b]
            kb = 3 * (2 - a) + b
            w3[:, 32 * kb : 32 * kb + 32] = wmid_ref[a, b].astype(f32).T.astype(bf)

    zeros = jnp.zeros((8, 128), f32)
    for i in range(3):
        ext[i, 40:48] = zeros
    ext[0, 4:36] = field_ref[0]
    ext[1, 4:36] = cot_ref[0]
    ext[2, 4:36] = check_ref[...].astype(f32)
    row_16 = lax.broadcasted_iota(jnp.int32, (16, 128), 0)
    lane_16 = lanes_of((16, 128))
    own_lanes = lax.div(lane_16, 8) == row_16
    for i in range(3):
        for t in range(2):
            turned = pltpu.roll(ext[i, 4 + 16 * t : 20 + 16 * t], 4, 1, stride=8, stride_axis=0)
            pack_out[2 * i + t : 2 * i + t + 1] = jnp.sum(jnp.where(own_lanes, turned, 0.0), axis=0, keepdims=True)
    pack_out[6:8] = jnp.zeros((2, 128), f32)
    pl.semaphore_wait(barrier, 1 + 2 * (n_p - 1) + (n_z - 1))
    swaps = [
        pltpu.make_async_remote_copy(src_ref=src, dst_ref=dst, send_sem=sem_r.at[0, i], recv_sem=sem_r.at[1, i], device_id=partner, device_id_type=MESH)
        for i, (src, dst) in enumerate(((field_ref, near_f), (cot_ref, near_c), (check_ref, near_k)))
    ]
    for swap in swaps:
        swap.start()
    posts = [
        remote(pack_out, pack_in.at[slot], sem_p.at[0, slot], sem_p.at[1, slot], who)
        for slot, who in (
            (1, left), (0, right), (3, {**left, "gx": other}), (2, {**right, "gx": other}), (4, partner),
        )
    ]
    for post in posts:
        post.start()
    piece = share // PIECES
    pieces = [
        remote(prior_ref.at[pl.ds(skip * other + piece * k, piece)], c_in.at[pl.ds(piece * k, piece)], sem_c.at[0, k], sem_c.at[1, k], partner)
        for k in range(PIECES)
    ]
    for copy in pieces:
        copy.start()
    for swap in swaps:
        swap.wait_recv()
    ext[0, 0:4], ext[0, 36:40] = near_f[0, 28:32], near_f[0, 0:4]
    ext[1, 0:4], ext[1, 36:40] = near_c[0, 28:32], near_c[0, 0:4]
    ext[2, 0:4], ext[2, 36:40] = near_k[28:32].astype(f32), near_k[0:4].astype(f32)


    load.wait()
    n_cols = prior_ref.shape[2]
    whole = n_cols // 128 * 128

    def pair_sum(r, _):
        at = pl.multiple_of(80 * r, 16)
        for j in range(4):
            cols = slice(2048 * j, 2048 * j + 2048)
            value = c_own[r, :, cols] + c_in[r, :, cols]
            xs[pl.ds(at + 16 * j, 16)] = value.reshape(16, 128).astype(bf)
        value = (c_own[r, :, 8192:whole] + c_in[r, :, 8192:whole]).reshape((whole - 8192) // 128, 128)
        last = c_own[r, :, whole:] + c_in[r, :, whole:]
        last = jnp.concatenate([last, jnp.zeros((1, whole + 128 - n_cols), f32)], axis=1)
        value = jnp.concatenate([value, last, jnp.zeros((16 - 1 - value.shape[0], 128), f32)], axis=0)
        xs[pl.ds(at + 64, 16)] = value.astype(bf)
        return 0

    xs[80 * share :] = jnp.zeros((xs.shape[0] - 80 * share, 128), bf)
    chunks = 80 * piece // 64

    def reduce_piece(k):
        pieces[k].wait_recv()
        lax.fori_loop(piece * k, piece * k + piece, pair_sum, 0)
        for q in range(chunks * k, n_p if k == PIECES - 1 else chunks * k + chunks):

            @pl.when(p != q)
            def _():
                to_plane(q, p).start()

    for k in range(PIECES):
        reduce_piece(k)

    for post in posts:
        post.wait_recv()
    column = lax.rem(lanes_of((8, 128)), 8)
    own = pack_out[...]
    sides = (
        (jnp.where(column >= 4, own, pack_in[0]), jnp.where(column >= 4, pack_in[4], pack_in[2])),
        (jnp.where(column < 4, own, pack_in[1]), jnp.where(column < 4, pack_in[4], pack_in[3])),
    )
    lane_flat = lanes_of((1, 384))
    blank = jnp.zeros((1, 128), f32)

    def flat(side, i):
        near, far = (part[2 * i : 2 * i + 2] for part in side)
        inner = pltpu.roll(jnp.concatenate([near[0:1], near[1:2], blank], axis=1), 32, 1)
        outer = jnp.concatenate([pltpu.roll(far[1:2], 32, 1), blank, pltpu.roll(far[0:1], 32, 1)], axis=1)
        value = jnp.where((lane_flat >= 32) & (lane_flat < 288), inner, outer)
        return jnp.where(lane_flat < 320, value, 0.0)

    def flat_both(i):
        return jnp.concatenate([flat(sides[0], i), flat(sides[1], i)], axis=1)

    field_s, cot_s, frozen_s = flat_both(0), flat_both(1), flat_both(2)
    masked_s = field_s * frozen_s

    def both_rolled(value, offset):
        return jnp.concatenate([flat_roll(value[:, :384], offset), flat_roll(value[:, 384:], offset)], axis=1)

    def unflat(vector, e):
        parts = []
        for t in range(3):
            spread = jnp.broadcast_to(vector[:, 128 * t : 128 * t + 128], (16, 128))
            parts.append(jnp.sum(jnp.where(lane_16 == 8 * row_16 + e, spread, 0.0), axis=1, keepdims=True))
        return jnp.concatenate(parts, axis=0)

    masked = ext[0] * ext[2]
    lane_48 = lanes_of((48, 128))
    shifts = (
        jnp.where(lane_48 == 0, unflat(masked_s[:, :384], 3), pltpu.roll(masked, 1, 1)),
        masked,
        jnp.where(lane_48 == 127, unflat(masked_s[:, 384:], 4), pltpu.roll(masked, 127, 1)),
    )
    taps[...] = jnp.zeros(taps.shape, f32)
    edge_taps[...] = jnp.zeros(edge_taps.shape, f32)
    for a in range(3):
        for b in range(3):
            k = 3 * a + b
            taps[pl.ds(16 + k, 38, stride=16), :] = shifts[b][a : a + 38]
            edge_taps[k : k + 1, :] = both_rolled(masked_s, 8 * (a - 1) + b - 1)

    def first(tap_values):
        high, low = halves(tap_values)
        return jnp.tanh(dot(w_one, jnp.concatenate([high, low, high], axis=0))).astype(bf)

    lane_384 = lanes_of((32, 384))

    def spread_edges(value, back, store):
        for a in range(3):
            for b in range(3):
                k = 3 * a + b
                offset = 8 * (a - 1) + (1 - b if back else b - 1)
                store[32 * k : 32 * k + 32, :] = both_rolled(value, offset).astype(bf)
        mixed = jnp.where(lax.rem(lane_384, 8) == 4, flat_roll(value[:, :384], -1), flat_roll(value[:, 384:], 1))
        for t in range(3):
            cp[t] = mixed[:, 128 * t : 128 * t + 128]

    lane_32 = lanes_of((32, 128))

    def spread_row(q, value, back, store):
        edge = pltpu.roll(cp[lax.div(q, 16)], lax.rem(252 - 8 * lax.rem(q, 16), 128), 1)
        before = jnp.where(lane_32 == 0, edge, pltpu.roll(value, 1, 1)).astype(bf)
        after = jnp.where(lane_32 == 127, edge, pltpu.roll(value, 127, 1)).astype(bf)
        store[q, 0:32] = after if back else before
        store[q, 32:64] = value.astype(bf)
        store[q, 64:96] = before if back else after

    one_s = first(edge_taps[...])
    spread_edges(one_s.astype(f32), False, xs_one)

    def one_rows(rows):
        values = jnp.concatenate([taps[pl.ds(pl.multiple_of(16 * q, 16), 16), :] for q in rows], axis=1)
        out = first(values).astype(f32)
        for i, q in enumerate(rows):
            spread_row(q, out[:, 128 * i : 128 * i + 128], False, xm)

    def over_rows(step, first_group=0, last_group=8):
        def body(i, _):
            step([4 + 4 * i + n for n in range(4)])
            return 0

        lax.fori_loop(first_group, last_group, body, 0)

    for q in (0, 39):
        xm[q] = jnp.zeros((96, 128), bf)
    one_rows([1, 2, 3, 36])
    one_rows([37, 38])
    over_rows(one_rows, 0, 4)
    over_rows(one_rows, 4, 8)

    def second(windows, field, cot, frozen):
        two = jnp.tanh(dot(w2[...], windows)).astype(bf)
        pair = dot(head, two)
        expo = jnp.exp(pair[0:1])
        open_cot = (1.0 - frozen) * cot
        d_0 = (open_cot * field * expo).astype(bf)
        d_1 = open_cot.astype(bf)
        two_f = two.astype(f32)
        d_two = (head_0 * d_0.astype(f32) + head_1 * d_1.astype(f32)) * (1.0 - two_f * two_f)
        return two, pair, d_0, d_1, d_two.astype(bf).astype(f32)

    _, _, _, _, d_two_s = second(xs_one[...], field_s, cot_s, frozen_s)
    spread_edges(d_two_s, True, xds)

    def windows_of(store, rows):
        return jnp.concatenate([store[pl.ds(q - 1, 3)].reshape(288, 128) for q in rows], axis=1)

    def rows_of(i, rows):
        return jnp.concatenate([ext[i, pl.ds(q, 1), :] for q in rows], axis=1)

    acc_mid[...] = jnp.zeros(acc_mid.shape, f32)
    b_rows[...] = jnp.zeros(b_rows.shape, f32)

    def two_rows(rows, inner=True):
        two, pair, d_0, d_1, d_two = second(windows_of(xm, rows), rows_of(0, rows), rows_of(1, rows), rows_of(2, rows))
        for i, q in enumerate(rows):
            at = slice(128 * i, 128 * i + 128)
            spread_row(q, d_two[:, at], True, xd)
            if inner:
                pair_rows[pl.ds(pl.multiple_of(8 * q, 8), 2), :] = pair[:, at]
        if inner:
            b_rows[297:299, 0:32] += nt(jnp.concatenate([d_0, d_1], axis=0), two)

    for q in (0, 1, 38, 39):
        xd[q] = jnp.zeros((96, 128), bf)
    two_rows([2, 3, 36, 37], inner=False)
    over_rows(two_rows, 0, 4)
    total = xs[chunk(p)].astype(f32)
    for offset in plane_order:
        q = from_beside(*offset)
        to_plane(q, q).wait_recv()
        total = total + xr[q].astype(f32)
    zs[...] = total.astype(bf).reshape(4, 16, 128)

    for offset in line_order:
        to_along(lax.rem(z + offset, n_z), z).start()
    over_rows(two_rows, 4, 8)

    def mid_rows(i, _):
        rows = [4 + 8 * i + n for n in range(8)]
        one = jnp.concatenate([xm[q, 32:64] for q in rows], axis=1)
        acc_mid[...] += nt(windows_of(xd, rows), one)
        return 0

    lax.fori_loop(0, 4, mid_rows, 0)
    for j in range(3):
        b_rows[9 + 96 * (2 - j) : 9 + 96 * (2 - j) + 96, 0:32] = acc_mid[96 * j : 96 * j + 96]
    rows = mine.shape[0]
    layer = b_rows[pl.ds(0, rows, stride=4), :]
    for g in range(1, 4):
        layer = layer + pltpu.roll(b_rows[pl.ds(g, rows, stride=4), :], 32 * g, 1)
    mine[...] = layer * scale
    is_owner = (p < UNITS) & (lax.rem(p, 2) == core)

    def to_owner(unit, slot):
        return remote(mine.at[pl.ds(8 * unit, 8)], mine_x.at[slot], sem_l.at[unit], sem_lx.at[slot], plane(unit, unit % 2))

    def is_other(unit):
        return (p != unit) | (core != unit % 2)

    for unit in range(UNITS):

        @pl.when(is_other(unit))
        def _():
            to_owner(unit, n_p * core + p).start()

    def third(windows, one):
        one_f = one.astype(f32)
        d_one = dot(w3[...], windows) * (1.0 - one_f * one_f)
        high, low = halves(d_one)
        return high, low, dot(w_back, jnp.concatenate([high, low, high], axis=0))

    _, _, t_s = third(xds[...], one_s)

    def three_rows(rows, inner=True):
        windows = windows_of(xd, rows)
        one = jnp.concatenate([xm[q, 32:64] for q in rows], axis=1)
        high, low, t_values = third(windows, one)
        for i, q in enumerate(rows):
            t_rows[pl.ds(pl.multiple_of(16 * q, 16), 16), :] = t_values[:, 128 * i : 128 * i + 128]
        if inner:
            values = jnp.concatenate([taps[pl.ds(pl.multiple_of(16 * q, 16), 16), :] for q in rows], axis=1)
            m_high, m_low = halves(values)
            parts = nt(jnp.concatenate([m_high, m_low], axis=0), jnp.concatenate([high, low], axis=0))
            parts = parts[0:16] + parts[16:32]
            b_in[0:9, 0:32] += (parts[:, 0:32] + parts[:, 32:64])[0:9]

    b_in[...] = jnp.zeros(b_in.shape, f32)
    three_rows([3, 36], inner=False)
    over_rows(three_rows)


    late = b_in[pl.ds(0, 4, stride=4), :]
    for g in range(1, 4):
        late = late + pltpu.roll(b_in[pl.ds(g, 4, stride=4), :], 32 * g, 1)
    me = n_p * core + p
    late_x[me] = late * scale

    def to_late(q, which, slot):
        return remote(late_x.at[me], late_x.at[slot], sem_ls.at[which, q], sem_lr.at[slot], plane(q, which))

    for offset in plane_order:
        to_late(beside(*offset), core, me).start()
        to_late(beside(*offset), other, me).start()
    to_late(p, other, me).start()

    def column_sum(b):
        total = None
        for a in range(3):
            part = t_rows[pl.ds(16 * (5 - a) + 3 * a + b, 32, stride=16), :]
            total = part if total is None else total + part
        return total

    def edge_sum(b, side):
        total = None
        for a in range(3):
            k = 3 * a + b
            part = flat_roll(t_s[k : k + 1, 384 * side : 384 * side + 384], 8 * (1 - a))
            total = part if total is None else total + part
        return total

    lane = lanes_of((32, 128))
    from_right = unflat(edge_sum(0, 1), 4)[4:36]
    from_left = unflat(edge_sum(2, 0), 3)[4:36]
    d_masked = (
        jnp.where(lane == 127, from_right, pltpu.roll(column_sum(0), 127, 1))
        + column_sum(1)
        + jnp.where(lane == 0, from_left, pltpu.roll(column_sum(2), 1, 1))
    )
    frozen = check_ref[...].astype(f32)
    unfrozen = 1.0 - frozen
    expo = jnp.exp(pair_rows[pl.ds(32, 32, stride=8), :])
    offset = pair_rows[pl.ds(33, 32, stride=8), :]
    values, cot = field_ref[0], cot_ref[0]
    coupled_ref[0] = frozen * values + unfrozen * (values * expo + offset)
    fgrad_ref[0] = frozen * cot + unfrozen * cot * expo + frozen * d_masked


    def to_along_mine(w, slot):
        return remote(own_sum, mine_z.at[slot], sem_lz.at[0, w], sem_lz.at[1, slot], along(w))

    @pl.when(is_owner)
    def _():
        def take(i, total):
            slot = lax.rem(n_p * core + p + i, 2 * n_p)
            to_owner(0, slot).wait_recv()
            return total + mine_x[slot]

        own_sum[...] = lax.fori_loop(1, 2 * n_p, take, mine[chunk(p, 8)])
        for offset in line_order:
            to_along_mine(lax.rem(z + offset, n_z), z).start()

    tile = lax.rem(z, 4)

    total = zs[tile].astype(f32)
    for offset in line_order:
        w = lax.rem(z + n_z - offset, n_z)
        to_along(w, w).wait_recv()
        total = total + zr[w].astype(f32)
    fin[core, chunk(4 * p + tile, 16)] = total.astype(bf)

    def to_four(i, slot):
        w = lax.rem(z + n_z + (1, -1, -2)[i - 1], n_z)
        at = chunk(4 * p + slot, 16)
        return remote(fin.at[core, chunk(4 * p + tile, 16)], fin.at[core, at], sem_t.at[0, i], sem_t.at[1, slot], along(w))

    for i in range(1, 4):
        to_four(i, tile).start()

    for i in range(1, 4):
        to_four(i, lax.rem(tile + i, 4)).wait_recv()

    def all_plane(q, slot):
        return remote(fin.at[core, chunk(p)], fin.at[core, chunk(slot)], sem_a.at[0, q], sem_a.at[1, slot], plane(q))

    def to_partner(which, slot):
        return remote(fin.at[core, chunk(slot)], fin.at[which, chunk(slot)], sem_b.at[0, slot], sem_b.at[1, slot], partner)

    to_partner(core, p).start()
    for offset in plane_order:
        all_plane(beside(*offset), p).start()

    def late_arrives(i, _):
        to_late(p, other, lax.rem(me + i, 2 * n_p)).wait_recv()
        return 0

    lax.fori_loop(1, 2 * n_p, late_arrives, 0)
    late_z[z] = lax.fori_loop(0, 2 * n_p, lambda i, total: total + late_x[i], jnp.zeros((4, 128), f32))

    def late_along(w, slot):
        return remote(late_z.at[z], late_z.at[slot], sem_lt.at[0, w], sem_lt.at[1, slot], along(w))

    for offset in line_order:
        late_along(lax.rem(z + offset, n_z), z).start()

    def to_all_mine(q, which, unit):
        return remote(mine_fin.at[unit], mine_fin.at[unit], sem_la.at[which, q], sem_mr.at[unit], plane(q, which))

    @pl.when(is_owner)
    def _():
        def take(i, total):
            w = lax.rem(z + n_z - i, n_z)
            to_along_mine(w, w).wait_recv()
            return total + mine_z[w]

        mine_fin[p] = lax.fori_loop(1, n_z, take, own_sum[...])
        for offset in plane_order:
            to_all_mine(beside(*offset), core, p).start()
            to_all_mine(beside(*offset), other, p).start()
        to_all_mine(p, other, p).start()

    for offset in plane_order:
        q = from_beside(*offset)
        all_plane(q, q).wait_recv()
        to_partner(core, q).start()

    def late_final(i, _):
        w = lax.rem(z + i, n_z)
        late_along(w, w).wait_recv()
        return 0

    lax.fori_loop(1, n_z, late_final, 0)
    late_fin[...] = lax.fori_loop(0, n_z, lambda i, total: total + late_z[i], jnp.zeros((4, 128), f32))
    for q in range(n_p):
        to_partner(other, q).wait_recv()
    for unit in range(UNITS):

        @pl.when(is_other(unit))
        def _():
            to_all_mine(p, other, unit).wait_recv()

    for copy in (*swaps, *posts, *pieces):
        copy.wait_send()

    def drain_plane(i, _):
        q = lax.rem(p + i, n_p)
        to_plane(q, p).wait_send()
        all_plane(q, p).wait_send()
        return 0

    def drain_along(i, _):
        to_along(lax.rem(z + i, n_z), z).wait_send()
        return 0

    to_partner(core, p).wait_send()
    for offset in plane_order:
        to_partner(core, from_beside(*offset)).wait_send()
    def drain_late(i, _):
        q = lax.rem(p + i, n_p)
        to_late(q, core, me).wait_send()
        to_late(q, other, me).wait_send()
        return 0

    def drain_late_along(i, _):
        late_along(lax.rem(z + i, n_z), z).wait_send()
        return 0

    lax.fori_loop(1, n_p, drain_late, 0)
    to_late(p, other, me).wait_send()
    lax.fori_loop(1, n_z, drain_late_along, 0)
    lax.fori_loop(1, n_p, drain_plane, 0)
    lax.fori_loop(1, n_z, drain_along, 0)
    for i in range(1, 4):
        to_four(i, tile).wait_send()
    for unit in range(UNITS):

        @pl.when(is_other(unit))
        def _():
            to_owner(unit, n_p * core + p).wait_send()

    @pl.when(is_owner)
    def _():
        def drain_z(i, _):
            to_along_mine(lax.rem(z + i, n_z), z).wait_send()
            return 0

        def drain_all(i, _):
            q = lax.rem(p + i, n_p)
            to_all_mine(q, core, p).wait_send()
            to_all_mine(q, other, p).wait_send()
            return 0

        lax.fori_loop(1, n_z, drain_z, 0)
        lax.fori_loop(1, n_p, drain_all, 0)
        to_all_mine(p, other, p).wait_send()


def unpack_kernel(coupled_in, fgrad_in, fin, mine_fin, late_fin, coupled_ref, fgrad_ref, out_ref, wide):
    coupled_ref[...] = coupled_in[...]
    fgrad_ref[...] = fgrad_in[...]
    n_rows, n_cols = out_ref.shape
    share = n_rows // 2
    for unit in range(UNITS):
        wide[8 * unit : 8 * unit + 8] = mine_fin[unit]
    wide[0:4] += late_fin[...]
    for which in range(2):
        base = 80 * (1 + (n_rows - 1 - share) * which)

        def widen(r, _):
            rows = fin[which, pl.ds(pl.multiple_of(80 * r, 16), 80)].astype(jnp.float32)
            wide[pl.ds(pl.multiple_of(base + 80 * r, 16), 80)] = rows
            return 0

        lax.fori_loop(0, share, widen, 0, unroll=2)

    def unpack(k, _):
        out_ref[:, pl.ds(pl.multiple_of(k * 128, 128), 128)] = wide[pl.ds(k, n_rows, stride=80), :]
        return 0

    whole = n_cols // 128
    lax.fori_loop(0, whole, unpack, 0, unroll=2)
    out_ref[:, 128 * whole :] = wide[pl.ds(whole, n_rows, stride=80), :][:, : n_cols - 128 * whole]


def unpack_call(coupled, fgrad, fin, mine_fin, late_fin, rows, cols):
    f32 = jnp.float32
    vmem = pl.BlockSpec(memory_space=pltpu.VMEM)
    return pl.pallas_call(
        unpack_kernel,
        out_shape=(
            jax.ShapeDtypeStruct(coupled.shape, f32),
            jax.ShapeDtypeStruct(fgrad.shape, f32),
            jax.ShapeDtypeStruct((rows, cols), f32),
        ),
        in_specs=[vmem] * 5,
        out_specs=(vmem,) * 3,
        scratch_shapes=[pltpu.VMEM((80 * rows, 128), f32)],
    )(coupled, fgrad, fin, mine_fin, late_fin)


def fused_call(scale, field, cot, checker, weight_in, weight_mid, weight_head, prior):
    f32, bf = jnp.float32, jnp.bfloat16
    sem = pltpu.SemaphoreType.DMA
    vmem = pl.BlockSpec(memory_space=pltpu.VMEM)
    n_p, n_z = 2 * lax.axis_size("gy"), lax.axis_size("dp") // 2
    rows, _, cols = prior.shape
    share = (rows + 1) // 2
    return pl.pallas_call(
        functools.partial(fused_kernel, scale),
        out_shape=(
            jax.ShapeDtypeStruct(field.shape, f32),
            jax.ShapeDtypeStruct(field.shape, f32),
            jax.ShapeDtypeStruct((2, n_p * 64, 128), bf),
            jax.ShapeDtypeStruct((UNITS, 8, 128), f32),
            jax.ShapeDtypeStruct((4, 128), f32),
        ),
        in_specs=[vmem] * 6 + [pl.BlockSpec(memory_space=pl.ANY)],
        out_specs=(vmem,) * 5,
        scratch_shapes=[
            pltpu.VMEM(field.shape, f32), pltpu.VMEM(field.shape, f32), pltpu.VMEM(checker.shape, jnp.int32),
            pltpu.VMEM((3, 48, 128), f32),
            pltpu.VMEM((8, 128), f32), pltpu.VMEM((5, 8, 128), f32),
            pltpu.VMEM((640, 128), f32), pltpu.VMEM((16, 768), f32),
            pltpu.VMEM((16, 128), f32), pltpu.VMEM((32, 288), bf), pltpu.VMEM((32, 288), bf),
            pltpu.VMEM((40, 96, 128), bf), pltpu.VMEM((288, 768), bf),
            pltpu.VMEM((40, 96, 128), bf), pltpu.VMEM((288, 768), bf),
            pltpu.VMEM((3, 32, 128), f32),
            pltpu.VMEM((320, 128), f32), pltpu.VMEM((640, 128), f32),
            pltpu.VMEM((288, 32), f32), pltpu.VMEM((320, 128), f32),
            pltpu.VMEM((share, 1, cols), f32), pltpu.VMEM((share, 1, cols), f32),
            pltpu.VMEM((n_p * 64, 128), bf), pltpu.VMEM((n_p, 64, 128), bf),
            pltpu.VMEM((4, 16, 128), bf), pltpu.VMEM((n_z, 16, 128), bf),
            pltpu.VMEM((80, 128), f32),
            pltpu.VMEM((2 * n_p, 8, 128), f32), pltpu.VMEM((n_z, 8, 128), f32),
            pltpu.VMEM((8, 128), f32),
            pltpu.VMEM((16, 128), f32), pltpu.VMEM((2 * n_p, 4, 128), f32), pltpu.VMEM((n_z, 4, 128), f32),
            sem((2, 3)), sem((2, 5)), sem, sem((2, PIECES)), sem((2, n_p)), sem((2, n_z)), sem((2, 4)), sem((2, n_p)), sem((2, n_p)),
            sem((UNITS,)), sem((2 * n_p,)), sem((2, n_z)), sem((2, n_p)), sem((UNITS,)),
            sem((2, n_p)), sem((2 * n_p,)), sem((2, n_z)),
        ],
        compiler_params=pltpu.CompilerParams(collective_id=0, has_side_effects=True),
    )(field, cot, checker, weight_in, weight_mid, weight_head, prior)


def on_device(field, cotangent, checker, weight_in, weight_mid, weight_head, prior_grads):
    cell_total = field.size * lax.axis_size("dp") * lax.axis_size("gx") * lax.axis_size("gy")
    scale = 1.0 / math.sqrt(cell_total)
    prior = prior_grads.reshape(prior_grads.shape[3], 1, prior_grads.shape[4])
    sums = fused_call(scale, field, cotangent, checker, weight_in, weight_mid, weight_head, prior)
    return unpack_call(*sums, prior.shape[0] + 1, prior.shape[2])


def solution(mesh):
    placed = (
        P("dp", "gx", "gy"),
        P("dp", "gx", "gy"),
        P("gx", "gy"),
        P(),
        P(),
        P(),
        P("dp", "gx", "gy", None, None),
    )
    return jax.shard_map(
        on_device,
        mesh=mesh,
        in_specs=placed,
        out_specs=(P("dp", "gx", "gy"), P("dp", "gx", "gy"), P()),
        check_vma=False,
    )
```

```python
import functools
import itertools
import math

import jax
import jax.numpy as jnp
from jax import lax
from jax.experimental import pallas as pl
from jax.experimental.pallas import tpu as pltpu
from jax.sharding import PartitionSpec as P

MESH = pl.DeviceIdType.MESH
PIECES = 3
UNITS = 10


def ring_distance(offset, size):
    return min(offset, size - offset)


def farthest_first(*sizes):
    offsets = [at for at in itertools.product(*(range(n) for n in sizes)) if any(at)]
    return sorted(offsets, key=lambda at: -sum(ring_distance(o, n) for o, n in zip(at, sizes)))


def flat_roll(value, offset):
    return pltpu.roll(value, (-offset) % value.shape[-1], value.ndim - 1)


def halves(value):
    high = value.astype(jnp.bfloat16)
    return high, (value - high.astype(jnp.float32)).astype(jnp.bfloat16)


def nt(a, b, **how):
    return lax.dot_general(a, b, (((1,), (1,)), ((), ())), preferred_element_type=jnp.float32, **how)


def dot(a, b):
    return jnp.dot(a, b, preferred_element_type=jnp.float32)


def lanes_of(shape):
    return lax.broadcasted_iota(jnp.int32, shape, len(shape) - 1)


def fused_kernel(scale, field_ref, cot_ref, check_ref, win_ref, wmid_ref, whead_ref, prior_ref,
                 coupled_ref, fgrad_ref, fin, mine_fin, late_fin,
                 near_f, near_c, near_k, ext, pack_out, pack_in, taps, edge_taps, w9, w2, w3,
                 xm, xs_one, xd, xds, cp, pair_rows, t_rows, acc_mid, b_rows,
                 c_own, c_in, xs, xr, zs, zr, mine, mine_x, mine_z, own_sum, b_in, late_x, late_z,
                 sem_r, sem_p, sem_own, sem_c, sem_x, sem_z, sem_t, sem_a, sem_b, sem_l, sem_lx, sem_lz, sem_la, sem_mr, sem_ls, sem_lr, sem_lt):
    f32, bf = jnp.float32, jnp.bfloat16
    dp, core, gy = lax.axis_index("dp"), lax.axis_index("gx"), lax.axis_index("gy")
    n_gy = lax.axis_size("gy")
    n_z = lax.axis_size("dp") // 2
    n_p = 2 * n_gy
    z = lax.rem(dp, n_z)
    p = lax.div(dp, n_z) * n_gy + gy
    other = 1 - core
    share = c_own.shape[0]

    n_x, n_y = n_gy // 2, 4
    at_x, at_y = lax.div(gy, 2), 2 * lax.rem(gy, 2) + lax.div(dp, n_z)
    plane_order = farthest_first(n_x, n_y)
    line_order = [w for (w,) in farthest_first(n_z)]

    def beside(dx, dy):
        to_x, to_y = lax.rem(at_x + dx, n_x), lax.rem(at_y + dy, n_y)
        return lax.rem(to_y, 2) * n_gy + 2 * to_x + lax.div(to_y, 2)

    def from_beside(dx, dy):
        return beside(n_x - dx, n_y - dy)

    def plane(q, which=core):
        return {"dp": lax.div(q, n_gy) * n_z + z, "gx": which, "gy": lax.rem(q, n_gy)}

    def along(w):
        return {"dp": dp - z + w, "gx": core, "gy": gy}

    def chunk(q, rows=64):
        return pl.ds(pl.multiple_of(rows * q, rows), rows)

    partner = {"dp": dp, "gx": other, "gy": gy}
    left = {"dp": dp, "gx": core, "gy": lax.rem(gy + n_gy - 1, n_gy)}
    right = {"dp": dp, "gx": core, "gy": lax.rem(gy + 1, n_gy)}
    barrier = pltpu.get_barrier_semaphore()

    def hello(who):
        pl.semaphore_signal(barrier, inc=1, device_id=who, device_id_type=MESH)

    def hello_along(i, _):
        hello(along(lax.rem(z + i, n_z)))
        return 0

    def hello_plane(i, _):
        hello(plane(lax.rem(p + i, n_p)))
        hello(plane(lax.rem(p + i, n_p), other))
        return 0

    lax.fori_loop(1, n_z, hello_along, 0)
    lax.fori_loop(1, n_p, hello_plane, 0)
    hello(partner)

    def remote(src, dst, sends, recvs, who):
        return pltpu.make_async_remote_copy(src_ref=src, dst_ref=dst, send_sem=sends, recv_sem=recvs, device_id=who, device_id_type=MESH)

    skip = prior_ref.shape[0] - share
    load = pltpu.make_async_copy(prior_ref.at[pl.ds(skip * core, share)], c_own, sem_own)
    load.start()

    def to_plane(q, slot):
        return remote(xs.at[chunk(q)], xr.at[slot], sem_x.at[0, q], sem_x.at[1, slot], plane(q))

    def to_along(w, slot):
        return remote(zs.at[lax.rem(w, 4)], zr.at[slot], sem_z.at[0, w], sem_z.at[1, slot], along(w))

    for a in range(3):
        w9[3 * a : 3 * a + 3, 0:32] = win_ref[a]
    w9[9:16, 0:32] = jnp.zeros((7, 32), f32)
    eye_f = (lax.broadcasted_iota(jnp.int32, (32, 32), 0) == lanes_of((32, 32))).astype(f32)
    eye = eye_f.astype(bf)
    w_taps = w9[:, 0:32]
    taps_t = nt(eye_f, w_taps, precision=lax.Precision.HIGHEST)
    th, tl = halves(taps_t)
    w_one = jnp.concatenate([th, th, tl], axis=1)
    wh, wl = halves(w_taps)
    w_back = jnp.concatenate([wh, wh, wl], axis=1)
    head = whead_ref[...]
    head_t = nt(eye, head)
    head_0, head_1 = head_t[:, 0:1], head_t[:, 1:2]
    for a in range(3):
        for b in range(3):
            k = 3 * a + b
            w2[:, 32 * k : 32 * k + 32] = wmid_ref[a, b]
            kb = 3 * (2 - a) + b
            w3[:, 32 * kb : 32 * kb + 32] = wmid_ref[a, b].astype(f32).T.astype(bf)

    zeros = jnp.zeros((8, 128), f32)
    for i in range(3):
        ext[i, 40:48] = zeros
    ext[0, 4:36] = field_ref[0]
    ext[1, 4:36] = cot_ref[0]
    ext[2, 4:36] = check_ref[...].astype(f32)
    row_16 = lax.broadcasted_iota(jnp.int32, (16, 128), 0)
    lane_16 = lanes_of((16, 128))
    own_lanes = lax.div(lane_16, 8) == row_16
    for i in range(3):
        for t in range(2):
            turned = pltpu.roll(ext[i, 4 + 16 * t : 20 + 16 * t], 4, 1, stride=8, stride_axis=0)
            pack_out[2 * i + t : 2 * i + t + 1] = jnp.sum(jnp.where(own_lanes, turned, 0.0), axis=0, keepdims=True)
    pack_out[6:8] = jnp.zeros((2, 128), f32)
    pl.semaphore_wait(barrier, 1 + 2 * (n_p - 1) + (n_z - 1))
    swaps = [
        pltpu.make_async_remote_copy(src_ref=src, dst_ref=dst, send_sem=sem_r.at[0, i], recv_sem=sem_r.at[1, i], device_id=partner, device_id_type=MESH)
        for i, (src, dst) in enumerate(((field_ref, near_f), (cot_ref, near_c), (check_ref, near_k)))
    ]
    for swap in swaps:
        swap.start()
    posts = [
        remote(pack_out, pack_in.at[slot], sem_p.at[0, slot], sem_p.at[1, slot], who)
        for slot, who in (
            (1, left), (0, right), (3, {**left, "gx": other}), (2, {**right, "gx": other}), (4, partner),
        )
    ]
    for post in posts:
        post.start()
    piece = share // PIECES
    pieces = [
        remote(prior_ref.at[pl.ds(skip * other + piece * k, piece)], c_in.at[pl.ds(piece * k, piece)], sem_c.at[0, k], sem_c.at[1, k], partner)
        for k in range(PIECES)
    ]
    for copy in pieces:
        copy.start()
    for swap in swaps:
        swap.wait_recv()
    ext[0, 0:4], ext[0, 36:40] = near_f[0, 28:32], near_f[0, 0:4]
    ext[1, 0:4], ext[1, 36:40] = near_c[0, 28:32], near_c[0, 0:4]
    ext[2, 0:4], ext[2, 36:40] = near_k[28:32].astype(f32), near_k[0:4].astype(f32)


    load.wait()
    n_cols = prior_ref.shape[2]
    whole = n_cols // 128 * 128

    def pair_sum(r, _):
        at = pl.multiple_of(80 * r, 16)
        for j in range(4):
            cols = slice(2048 * j, 2048 * j + 2048)
            value = c_own[r, :, cols] + c_in[r, :, cols]
            xs[pl.ds(at + 16 * j, 16)] = value.reshape(16, 128).astype(bf)
        value = (c_own[r, :, 8192:whole] + c_in[r, :, 8192:whole]).reshape((whole - 8192) // 128, 128)
        last = c_own[r, :, whole:] + c_in[r, :, whole:]
        last = jnp.concatenate([last, jnp.zeros((1, whole + 128 - n_cols), f32)], axis=1)
        value = jnp.concatenate([value, last, jnp.zeros((16 - 1 - value.shape[0], 128), f32)], axis=0)
        xs[pl.ds(at + 64, 16)] = value.astype(bf)
        return 0

    xs[80 * share :] = jnp.zeros((xs.shape[0] - 80 * share, 128), bf)
    chunks = 80 * piece // 64

    def reduce_piece(k):
        pieces[k].wait_recv()
        lax.fori_loop(piece * k, piece * k + piece, pair_sum, 0)
        for q in range(chunks * k, n_p if k == PIECES - 1 else chunks * k + chunks):

            @pl.when(p != q)
            def _():
                to_plane(q, p).start()

    for k in range(PIECES):
        reduce_piece(k)

    for post in posts:
        post.wait_recv()
    column = lax.rem(lanes_of((8, 128)), 8)
    own = pack_out[...]
    sides = (
        (jnp.where(column >= 4, own, pack_in[0]), jnp.where(column >= 4, pack_in[4], pack_in[2])),
        (jnp.where(column < 4, own, pack_in[1]), jnp.where(column < 4, pack_in[4], pack_in[3])),
    )
    lane_flat = lanes_of((1, 384))
    blank = jnp.zeros((1, 128), f32)

    def flat(side, i):
        near, far = (part[2 * i : 2 * i + 2] for part in side)
        inner = pltpu.roll(jnp.concatenate([near[0:1], near[1:2], blank], axis=1), 32, 1)
        outer = jnp.concatenate([pltpu.roll(far[1:2], 32, 1), blank, pltpu.roll(far[0:1], 32, 1)], axis=1)
        value = jnp.where((lane_flat >= 32) & (lane_flat < 288), inner, outer)
        return jnp.where(lane_flat < 320, value, 0.0)

    def flat_both(i):
        return jnp.concatenate([flat(sides[0], i), flat(sides[1], i)], axis=1)

    field_s, cot_s, frozen_s = flat_both(0), flat_both(1), flat_both(2)
    masked_s = field_s * frozen_s

    def both_rolled(value, offset):
        return jnp.concatenate([flat_roll(value[:, :384], offset), flat_roll(value[:, 384:], offset)], axis=1)

    def unflat(vector, e):
        parts = []
        for t in range(3):
            spread = jnp.broadcast_to(vector[:, 128 * t : 128 * t + 128], (16, 128))
            parts.append(jnp.sum(jnp.where(lane_16 == 8 * row_16 + e, spread, 0.0), axis=1, keepdims=True))
        return jnp.concatenate(parts, axis=0)

    masked = ext[0] * ext[2]
    lane_48 = lanes_of((48, 128))
    shifts = (
        jnp.where(lane_48 == 0, unflat(masked_s[:, :384], 3), pltpu.roll(masked, 1, 1)),
        masked,
        jnp.where(lane_48 == 127, unflat(masked_s[:, 384:], 4), pltpu.roll(masked, 127, 1)),
    )
    taps[...] = jnp.zeros(taps.shape, f32)
    edge_taps[...] = jnp.zeros(edge_taps.shape, f32)
    for a in range(3):
        for b in range(3):
            k = 3 * a + b
            taps[pl.ds(16 + k, 38, stride=16), :] = shifts[b][a : a + 38]
            edge_taps[k : k + 1, :] = both_rolled(masked_s, 8 * (a - 1) + b - 1)

    def first(tap_values):
        high, low = halves(tap_values)
        return jnp.tanh(dot(w_one, jnp.concatenate([high, low, high], axis=0))).astype(bf)

    lane_384 = lanes_of((32, 384))

    def spread_edges(value, back, store):
        for a in range(3):
            for b in range(3):
                k = 3 * a + b
                offset = 8 * (a - 1) + (1 - b if back else b - 1)
                store[32 * k : 32 * k + 32, :] = both_rolled(value, offset).astype(bf)
        mixed = jnp.where(lax.rem(lane_384, 8) == 4, flat_roll(value[:, :384], -1), flat_roll(value[:, 384:], 1))
        for t in range(3):
            cp[t] = mixed[:, 128 * t : 128 * t + 128]

    lane_32 = lanes_of((32, 128))

    def spread_row(q, value, back, store):
        edge = pltpu.roll(cp[lax.div(q, 16)], lax.rem(252 - 8 * lax.rem(q, 16), 128), 1)
        before = jnp.where(lane_32 == 0, edge, pltpu.roll(value, 1, 1)).astype(bf)
        after = jnp.where(lane_32 == 127, edge, pltpu.roll(value, 127, 1)).astype(bf)
        store[q, 0:32] = after if back else before
        store[q, 32:64] = value.astype(bf)
        store[q, 64:96] = before if back else after

    one_s = first(edge_taps[...])
    spread_edges(one_s.astype(f32), False, xs_one)

    def one_rows(rows):
        values = jnp.concatenate([taps[pl.ds(pl.multiple_of(16 * q, 16), 16), :] for q in rows], axis=1)
        out = first(values).astype(f32)
        for i, q in enumerate(rows):
            spread_row(q, out[:, 128 * i : 128 * i + 128], False, xm)

    def over_rows(step, first_group=0, last_group=2):
        def body(i, _):
            step([4 + 16 * i + n for n in range(16)])
            return 0

        lax.fori_loop(first_group, last_group, body, 0)

    for q in (0, 39):
        xm[q] = jnp.zeros((96, 128), bf)
    one_rows([1, 2, 3, 36])
    one_rows([37, 38])
    over_rows(one_rows)

    def second(windows, field, cot, frozen):
        two = jnp.tanh(dot(w2[...], windows)).astype(bf)
        pair = dot(head, two)
        expo = jnp.exp(pair[0:1])
        open_cot = (1.0 - frozen) * cot
        d_0 = (open_cot * field * expo).astype(bf)
        d_1 = open_cot.astype(bf)
        two_f = two.astype(f32)
        d_two = (head_0 * d_0.astype(f32) + head_1 * d_1.astype(f32)) * (1.0 - two_f * two_f)
        return two, pair, d_0, d_1, d_two.astype(bf).astype(f32)

    _, _, _, _, d_two_s = second(xs_one[...], field_s, cot_s, frozen_s)
    spread_edges(d_two_s, True, xds)

    def windows_of(store, rows):
        return jnp.concatenate([store[pl.ds(q - 1, 3)].reshape(288, 128) for q in rows], axis=1)

    def rows_of(i, rows):
        return jnp.concatenate([ext[i, pl.ds(q, 1), :] for q in rows], axis=1)

    acc_mid[...] = jnp.zeros(acc_mid.shape, f32)
    b_rows[...] = jnp.zeros(b_rows.shape, f32)

    def two_rows(rows, inner=True):
        two, pair, d_0, d_1, d_two = second(windows_of(xm, rows), rows_of(0, rows), rows_of(1, rows), rows_of(2, rows))
        for i, q in enumerate(rows):
            at = slice(128 * i, 128 * i + 128)
            spread_row(q, d_two[:, at], True, xd)
            if inner:
                pair_rows[pl.ds(pl.multiple_of(8 * q, 8), 2), :] = pair[:, at]
        if inner:
            b_rows[297:299, 0:32] += nt(jnp.concatenate([d_0, d_1], axis=0), two)

    for q in (0, 1, 38, 39):
        xd[q] = jnp.zeros((96, 128), bf)
    two_rows([2, 3, 36, 37], inner=False)
    over_rows(two_rows, 0, 1)
    total = xs[chunk(p)].astype(f32)
    for offset in plane_order:
        q = from_beside(*offset)
        to_plane(q, q).wait_recv()
        total = total + xr[q].astype(f32)
    zs[...] = total.astype(bf).reshape(4, 16, 128)

    for offset in line_order:
        to_along(lax.rem(z + offset, n_z), z).start()
    over_rows(two_rows, 1, 2)

    def mid_rows(i, _):
        rows = [4 + 16 * i + n for n in range(16)]
        one = jnp.concatenate([xm[q, 32:64] for q in rows], axis=1)
        acc_mid[...] += nt(windows_of(xd, rows), one)
        return 0

    lax.fori_loop(0, 2, mid_rows, 0)
    for j in range(3):
        b_rows[9 + 96 * (2 - j) : 9 + 96 * (2 - j) + 96, 0:32] = acc_mid[96 * j : 96 * j + 96]
    rows = mine.shape[0]
    layer = b_rows[pl.ds(0, rows, stride=4), :]
    for g in range(1, 4):
        layer = layer + pltpu.roll(b_rows[pl.ds(g, rows, stride=4), :], 32 * g, 1)
    mine[...] = layer * scale
    is_owner = (p < UNITS) & (lax.rem(p, 2) == core)

    def to_owner(unit, slot):
        return remote(mine.at[pl.ds(8 * unit, 8)], mine_x.at[slot], sem_l.at[unit], sem_lx.at[slot], plane(unit, unit % 2))

    def is_other(unit):
        return (p != unit) | (core != unit % 2)

    for unit in range(UNITS):

        @pl.when(is_other(unit))
        def _():
            to_owner(unit, n_p * core + p).start()

    def third(windows, one):
        one_f = one.astype(f32)
        d_one = dot(w3[...], windows) * (1.0 - one_f * one_f)
        high, low = halves(d_one)
        return high, low, dot(w_back, jnp.concatenate([high, low, high], axis=0))

    _, _, t_s = third(xds[...], one_s)

    def three_rows(rows, inner=True):
        windows = windows_of(xd, rows)
        one = jnp.concatenate([xm[q, 32:64] for q in rows], axis=1)
        high, low, t_values = third(windows, one)
        for i, q in enumerate(rows):
            t_rows[pl.ds(pl.multiple_of(16 * q, 16), 16), :] = t_values[:, 128 * i : 128 * i + 128]
        if inner:
            values = jnp.concatenate([taps[pl.ds(pl.multiple_of(16 * q, 16), 16), :] for q in rows], axis=1)
            m_high, m_low = halves(values)
            parts = nt(jnp.concatenate([m_high, m_low], axis=0), jnp.concatenate([high, low], axis=0))
            parts = parts[0:16] + parts[16:32]
            b_in[0:9, 0:32] += (parts[:, 0:32] + parts[:, 32:64])[0:9]

    b_in[...] = jnp.zeros(b_in.shape, f32)
    three_rows([3, 36], inner=False)
    over_rows(three_rows)


    late = b_in[pl.ds(0, 4, stride=4), :]
    for g in range(1, 4):
        late = late + pltpu.roll(b_in[pl.ds(g, 4, stride=4), :], 32 * g, 1)
    me = n_p * core + p
    late_x[me] = late * scale

    def to_late(q, which, slot):
        return remote(late_x.at[me], late_x.at[slot], sem_ls.at[which, q], sem_lr.at[slot], plane(q, which))

    for offset in plane_order:
        to_late(beside(*offset), core, me).start()
        to_late(beside(*offset), other, me).start()
    to_late(p, other, me).start()

    def column_sum(b):
        total = None
        for a in range(3):
            part = t_rows[pl.ds(16 * (5 - a) + 3 * a + b, 32, stride=16), :]
            total = part if total is None else total + part
        return total

    def edge_sum(b, side):
        total = None
        for a in range(3):
            k = 3 * a + b
            part = flat_roll(t_s[k : k + 1, 384 * side : 384 * side + 384], 8 * (1 - a))
            total = part if total is None else total + part
        return total

    lane = lanes_of((32, 128))
    from_right = unflat(edge_sum(0, 1), 4)[4:36]
    from_left = unflat(edge_sum(2, 0), 3)[4:36]
    d_masked = (
        jnp.where(lane == 127, from_right, pltpu.roll(column_sum(0), 127, 1))
        + column_sum(1)
        + jnp.where(lane == 0, from_left, pltpu.roll(column_sum(2), 1, 1))
    )
    frozen = check_ref[...].astype(f32)
    unfrozen = 1.0 - frozen
    expo = jnp.exp(pair_rows[pl.ds(32, 32, stride=8), :])
    offset = pair_rows[pl.ds(33, 32, stride=8), :]
    values, cot = field_ref[0], cot_ref[0]
    coupled_ref[0] = frozen * values + unfrozen * (values * expo + offset)
    fgrad_ref[0] = frozen * cot + unfrozen * cot * expo + frozen * d_masked


    def to_along_mine(w, slot):
        return remote(own_sum, mine_z.at[slot], sem_lz.at[0, w], sem_lz.at[1, slot], along(w))

    @pl.when(is_owner)
    def _():
        def take(i, total):
            slot = lax.rem(n_p * core + p + i, 2 * n_p)
            to_owner(0, slot).wait_recv()
            return total + mine_x[slot]

        own_sum[...] = lax.fori_loop(1, 2 * n_p, take, mine[chunk(p, 8)])
        for offset in line_order:
            to_along_mine(lax.rem(z + offset, n_z), z).start()

    tile = lax.rem(z, 4)

    total = zs[tile].astype(f32)
    for offset in line_order:
        w = lax.rem(z + n_z - offset, n_z)
        to_along(w, w).wait_recv()
        total = total + zr[w].astype(f32)
    fin[core, chunk(4 * p + tile, 16)] = total.astype(bf)

    def to_four(i, slot):
        w = lax.rem(z + n_z + (1, -1, -2)[i - 1], n_z)
        at = chunk(4 * p + slot, 16)
        return remote(fin.at[core, chunk(4 * p + tile, 16)], fin.at[core, at], sem_t.at[0, i], sem_t.at[1, slot], along(w))

    for i in range(1, 4):
        to_four(i, tile).start()

    for i in range(1, 4):
        to_four(i, lax.rem(tile + i, 4)).wait_recv()

    def all_plane(q, slot):
        return remote(fin.at[core, chunk(p)], fin.at[core, chunk(slot)], sem_a.at[0, q], sem_a.at[1, slot], plane(q))

    def to_partner(which, slot):
        return remote(fin.at[core, chunk(slot)], fin.at[which, chunk(slot)], sem_b.at[0, slot], sem_b.at[1, slot], partner)

    to_partner(core, p).start()
    for offset in plane_order:
        all_plane(beside(*offset), p).start()

    def late_arrives(i, _):
        to_late(p, other, lax.rem(me + i, 2 * n_p)).wait_recv()
        return 0

    lax.fori_loop(1, 2 * n_p, late_arrives, 0)
    late_z[z] = lax.fori_loop(0, 2 * n_p, lambda i, total: total + late_x[i], jnp.zeros((4, 128), f32))

    def late_along(w, slot):
        return remote(late_z.at[z], late_z.at[slot], sem_lt.at[0, w], sem_lt.at[1, slot], along(w))

    for offset in line_order:
        late_along(lax.rem(z + offset, n_z), z).start()

    def to_all_mine(q, which, unit):
        return remote(mine_fin.at[unit], mine_fin.at[unit], sem_la.at[which, q], sem_mr.at[unit], plane(q, which))

    @pl.when(is_owner)
    def _():
        def take(i, total):
            w = lax.rem(z + n_z - i, n_z)
            to_along_mine(w, w).wait_recv()
            return total + mine_z[w]

        mine_fin[p] = lax.fori_loop(1, n_z, take, own_sum[...])
        for offset in plane_order:
            to_all_mine(beside(*offset), core, p).start()
            to_all_mine(beside(*offset), other, p).start()
        to_all_mine(p, other, p).start()

    for offset in plane_order:
        q = from_beside(*offset)
        all_plane(q, q).wait_recv()
        to_partner(core, q).start()

    def late_final(i, _):
        w = lax.rem(z + i, n_z)
        late_along(w, w).wait_recv()
        return 0

    lax.fori_loop(1, n_z, late_final, 0)
    late_fin[...] = lax.fori_loop(0, n_z, lambda i, total: total + late_z[i], jnp.zeros((4, 128), f32))
    for q in range(n_p):
        to_partner(other, q).wait_recv()
    for unit in range(UNITS):

        @pl.when(is_other(unit))
        def _():
            to_all_mine(p, other, unit).wait_recv()

    for copy in (*swaps, *posts, *pieces):
        copy.wait_send()

    def drain_plane(i, _):
        q = lax.rem(p + i, n_p)
        to_plane(q, p).wait_send()
        all_plane(q, p).wait_send()
        return 0

    def drain_along(i, _):
        to_along(lax.rem(z + i, n_z), z).wait_send()
        return 0

    to_partner(core, p).wait_send()
    for offset in plane_order:
        to_partner(core, from_beside(*offset)).wait_send()
    def drain_late(i, _):
        q = lax.rem(p + i, n_p)
        to_late(q, core, me).wait_send()
        to_late(q, other, me).wait_send()
        return 0

    def drain_late_along(i, _):
        late_along(lax.rem(z + i, n_z), z).wait_send()
        return 0

    lax.fori_loop(1, n_p, drain_late, 0)
    to_late(p, other, me).wait_send()
    lax.fori_loop(1, n_z, drain_late_along, 0)
    lax.fori_loop(1, n_p, drain_plane, 0)
    lax.fori_loop(1, n_z, drain_along, 0)
    for i in range(1, 4):
        to_four(i, tile).wait_send()
    for unit in range(UNITS):

        @pl.when(is_other(unit))
        def _():
            to_owner(unit, n_p * core + p).wait_send()

    @pl.when(is_owner)
    def _():
        def drain_z(i, _):
            to_along_mine(lax.rem(z + i, n_z), z).wait_send()
            return 0

        def drain_all(i, _):
            q = lax.rem(p + i, n_p)
            to_all_mine(q, core, p).wait_send()
            to_all_mine(q, other, p).wait_send()
            return 0

        lax.fori_loop(1, n_z, drain_z, 0)
        lax.fori_loop(1, n_p, drain_all, 0)
        to_all_mine(p, other, p).wait_send()


def unpack_kernel(coupled_in, fgrad_in, fin, mine_fin, late_fin, coupled_ref, fgrad_ref, out_ref, wide):
    coupled_ref[...] = coupled_in[...]
    fgrad_ref[...] = fgrad_in[...]
    n_rows, n_cols = out_ref.shape
    share = n_rows // 2
    for unit in range(UNITS):
        wide[8 * unit : 8 * unit + 8] = mine_fin[unit]
    wide[0:4] += late_fin[...]
    for which in range(2):
        base = 80 * (1 + (n_rows - 1 - share) * which)

        def widen(r, _):
            rows = fin[which, pl.ds(pl.multiple_of(80 * r, 16), 80)].astype(jnp.float32)
            wide[pl.ds(pl.multiple_of(base + 80 * r, 16), 80)] = rows
            return 0

        lax.fori_loop(0, share, widen, 0, unroll=2)

    def unpack(k, _):
        out_ref[:, pl.ds(pl.multiple_of(k * 128, 128), 128)] = wide[pl.ds(k, n_rows, stride=80), :]
        return 0

    whole = n_cols // 128
    lax.fori_loop(0, whole, unpack, 0, unroll=2)
    out_ref[:, 128 * whole :] = wide[pl.ds(whole, n_rows, stride=80), :][:, : n_cols - 128 * whole]


def unpack_call(coupled, fgrad, fin, mine_fin, late_fin, rows, cols):
    f32 = jnp.float32
    vmem = pl.BlockSpec(memory_space=pltpu.VMEM)
    return pl.pallas_call(
        unpack_kernel,
        out_shape=(
            jax.ShapeDtypeStruct(coupled.shape, f32),
            jax.ShapeDtypeStruct(fgrad.shape, f32),
            jax.ShapeDtypeStruct((rows, cols), f32),
        ),
        in_specs=[vmem] * 5,
        out_specs=(vmem,) * 3,
        scratch_shapes=[pltpu.VMEM((80 * rows, 128), f32)],
    )(coupled, fgrad, fin, mine_fin, late_fin)


def fused_call(scale, field, cot, checker, weight_in, weight_mid, weight_head, prior):
    f32, bf = jnp.float32, jnp.bfloat16
    sem = pltpu.SemaphoreType.DMA
    vmem = pl.BlockSpec(memory_space=pltpu.VMEM)
    n_p, n_z = 2 * lax.axis_size("gy"), lax.axis_size("dp") // 2
    rows, _, cols = prior.shape
    share = (rows + 1) // 2
    return pl.pallas_call(
        functools.partial(fused_kernel, scale),
        out_shape=(
            jax.ShapeDtypeStruct(field.shape, f32),
            jax.ShapeDtypeStruct(field.shape, f32),
            jax.ShapeDtypeStruct((2, n_p * 64, 128), bf),
            jax.ShapeDtypeStruct((UNITS, 8, 128), f32),
            jax.ShapeDtypeStruct((4, 128), f32),
        ),
        in_specs=[vmem] * 6 + [pl.BlockSpec(memory_space=pl.ANY)],
        out_specs=(vmem,) * 5,
        scratch_shapes=[
            pltpu.VMEM(field.shape, f32), pltpu.VMEM(field.shape, f32), pltpu.VMEM(checker.shape, jnp.int32),
            pltpu.VMEM((3, 48, 128), f32),
            pltpu.VMEM((8, 128), f32), pltpu.VMEM((5, 8, 128), f32),
            pltpu.VMEM((640, 128), f32), pltpu.VMEM((16, 768), f32),
            pltpu.VMEM((16, 128), f32), pltpu.VMEM((32, 288), bf), pltpu.VMEM((32, 288), bf),
            pltpu.VMEM((40, 96, 128), bf), pltpu.VMEM((288, 768), bf),
            pltpu.VMEM((40, 96, 128), bf), pltpu.VMEM((288, 768), bf),
            pltpu.VMEM((3, 32, 128), f32),
            pltpu.VMEM((320, 128), f32), pltpu.VMEM((640, 128), f32),
            pltpu.VMEM((288, 32), f32), pltpu.VMEM((320, 128), f32),
            pltpu.VMEM((share, 1, cols), f32), pltpu.VMEM((share, 1, cols), f32),
            pltpu.VMEM((n_p * 64, 128), bf), pltpu.VMEM((n_p, 64, 128), bf),
            pltpu.VMEM((4, 16, 128), bf), pltpu.VMEM((n_z, 16, 128), bf),
            pltpu.VMEM((80, 128), f32),
            pltpu.VMEM((2 * n_p, 8, 128), f32), pltpu.VMEM((n_z, 8, 128), f32),
            pltpu.VMEM((8, 128), f32),
            pltpu.VMEM((16, 128), f32), pltpu.VMEM((2 * n_p, 4, 128), f32), pltpu.VMEM((n_z, 4, 128), f32),
            sem((2, 3)), sem((2, 5)), sem, sem((2, PIECES)), sem((2, n_p)), sem((2, n_z)), sem((2, 4)), sem((2, n_p)), sem((2, n_p)),
            sem((UNITS,)), sem((2 * n_p,)), sem((2, n_z)), sem((2, n_p)), sem((UNITS,)),
            sem((2, n_p)), sem((2 * n_p,)), sem((2, n_z)),
        ],
        compiler_params=pltpu.CompilerParams(collective_id=0, has_side_effects=True),
    )(field, cot, checker, weight_in, weight_mid, weight_head, prior)


def on_device(field, cotangent, checker, weight_in, weight_mid, weight_head, prior_grads):
    cell_total = field.size * lax.axis_size("dp") * lax.axis_size("gx") * lax.axis_size("gy")
    scale = 1.0 / math.sqrt(cell_total)
    prior = prior_grads.reshape(prior_grads.shape[3], 1, prior_grads.shape[4])
    sums = fused_call(scale, field, cotangent, checker, weight_in, weight_mid, weight_head, prior)
    return unpack_call(*sums, prior.shape[0] + 1, prior.shape[2])


def solution(mesh):
    placed = (
        P("dp", "gx", "gy"),
        P("dp", "gx", "gy"),
        P("gx", "gy"),
        P(),
        P(),
        P(),
        P("dp", "gx", "gy", None, None),
    )
    return jax.shard_map(
        on_device,
        mesh=mesh,
        in_specs=placed,
        out_specs=(P("dp", "gx", "gy"), P("dp", "gx", "gy"), P()),
        check_vma=False,
    )
```

```python
import functools
import itertools
import math

import jax
import jax.numpy as jnp
from jax import lax
from jax.experimental import pallas as pl
from jax.experimental.pallas import tpu as pltpu
from jax.sharding import PartitionSpec as P

MESH = pl.DeviceIdType.MESH
PIECES = 3
UNITS = 10


def ring_distance(offset, size):
    return min(offset, size - offset)


def farthest_first(*sizes):
    offsets = [at for at in itertools.product(*(range(n) for n in sizes)) if any(at)]
    return sorted(offsets, key=lambda at: -sum(ring_distance(o, n) for o, n in zip(at, sizes)))


def flat_roll(value, offset):
    return pltpu.roll(value, (-offset) % value.shape[-1], value.ndim - 1)


def halves(value):
    high = value.astype(jnp.bfloat16)
    return high, (value - high.astype(jnp.float32)).astype(jnp.bfloat16)


def nt(a, b, **how):
    return lax.dot_general(a, b, (((1,), (1,)), ((), ())), preferred_element_type=jnp.float32, **how)


def dot(a, b):
    return jnp.dot(a, b, preferred_element_type=jnp.float32)


def lanes_of(shape):
    return lax.broadcasted_iota(jnp.int32, shape, len(shape) - 1)


def fused_kernel(scale, field_ref, cot_ref, check_ref, win_ref, wmid_ref, whead_ref, prior_ref,
                 coupled_ref, fgrad_ref, fin, mine_fin, late_fin,
                 near_f, near_c, near_k, ext, pack_out, pack_in, taps, edge_taps, w9, w2, w3,
                 xm, xs_one, xd, xds, cp, pair_rows, t_rows, acc_mid, b_rows,
                 c_own, c_in, xs, xr, zs, zr, mine, mine_x, mine_z, own_sum, b_in, late_x, late_z,
                 sem_r, sem_p, sem_own, sem_c, sem_x, sem_z, sem_t, sem_a, sem_b, sem_l, sem_lx, sem_lz, sem_la, sem_mr, sem_ls, sem_lr, sem_lt):
    f32, bf = jnp.float32, jnp.bfloat16
    dp, core, gy = lax.axis_index("dp"), lax.axis_index("gx"), lax.axis_index("gy")
    n_gy = lax.axis_size("gy")
    n_z = lax.axis_size("dp") // 2
    n_p = 2 * n_gy
    z = lax.rem(dp, n_z)
    p = lax.div(dp, n_z) * n_gy + gy
    other = 1 - core
    share = c_own.shape[0]

    n_x, n_y = n_gy // 2, 4
    at_x, at_y = lax.div(gy, 2), 2 * lax.rem(gy, 2) + lax.div(dp, n_z)
    plane_order = farthest_first(n_x, n_y)
    line_order = [w for (w,) in farthest_first(n_z)]

    def beside(dx, dy):
        to_x, to_y = lax.rem(at_x + dx, n_x), lax.rem(at_y + dy, n_y)
        return lax.rem(to_y, 2) * n_gy + 2 * to_x + lax.div(to_y, 2)

    def from_beside(dx, dy):
        return beside(n_x - dx, n_y - dy)

    def plane(q, which=core):
        return {"dp": lax.div(q, n_gy) * n_z + z, "gx": which, "gy": lax.rem(q, n_gy)}

    def along(w):
        return {"dp": dp - z + w, "gx": core, "gy": gy}

    def chunk(q, rows=64):
        return pl.ds(pl.multiple_of(rows * q, rows), rows)

    partner = {"dp": dp, "gx": other, "gy": gy}
    left = {"dp": dp, "gx": core, "gy": lax.rem(gy + n_gy - 1, n_gy)}
    right = {"dp": dp, "gx": core, "gy": lax.rem(gy + 1, n_gy)}
    barrier = pltpu.get_barrier_semaphore()

    def hello(who):
        pl.semaphore_signal(barrier, inc=1, device_id=who, device_id_type=MESH)

    def hello_along(i, _):
        hello(along(lax.rem(z + i, n_z)))
        return 0

    def hello_plane(i, _):
        hello(plane(lax.rem(p + i, n_p)))
        hello(plane(lax.rem(p + i, n_p), other))
        return 0

    lax.fori_loop(1, n_z, hello_along, 0)
    lax.fori_loop(1, n_p, hello_plane, 0)
    hello(partner)

    def remote(src, dst, sends, recvs, who):
        return pltpu.make_async_remote_copy(src_ref=src, dst_ref=dst, send_sem=sends, recv_sem=recvs, device_id=who, device_id_type=MESH)

    skip = prior_ref.shape[0] - share
    load = pltpu.make_async_copy(prior_ref.at[pl.ds(skip * core, share)], c_own, sem_own)
    load.start()

    def to_plane(q, slot):
        return remote(xs.at[chunk(q)], xr.at[slot], sem_x.at[0, q], sem_x.at[1, slot], plane(q))

    def to_along(w, slot):
        return remote(zs.at[lax.rem(w, 4)], zr.at[slot], sem_z.at[0, w], sem_z.at[1, slot], along(w))

    for a in range(3):
        w9[3 * a : 3 * a + 3, 0:32] = win_ref[a]
    w9[9:16, 0:32] = jnp.zeros((7, 32), f32)
    eye_f = (lax.broadcasted_iota(jnp.int32, (32, 32), 0) == lanes_of((32, 32))).astype(f32)
    eye = eye_f.astype(bf)
    w_taps = w9[:, 0:32]
    taps_t = nt(eye_f, w_taps, precision=lax.Precision.HIGHEST)
    th, tl = halves(taps_t)
    w_one = jnp.concatenate([th, th, tl], axis=1)
    wh, wl = halves(w_taps)
    w_back = jnp.concatenate([wh, wh, wl], axis=1)
    head = whead_ref[...]
    head_t = nt(eye, head)
    head_0, head_1 = head_t[:, 0:1], head_t[:, 1:2]
    for a in range(3):
        for b in range(3):
            k = 3 * a + b
            w2[:, 32 * k : 32 * k + 32] = wmid_ref[a, b]
            kb = 3 * (2 - a) + b
            w3[:, 32 * kb : 32 * kb + 32] = wmid_ref[a, b].astype(f32).T.astype(bf)

    zeros = jnp.zeros((8, 128), f32)
    for i in range(3):
        ext[i, 40:48] = zeros
    ext[0, 4:36] = field_ref[0]
    ext[1, 4:36] = cot_ref[0]
    ext[2, 4:36] = check_ref[...].astype(f32)
    row_16 = lax.broadcasted_iota(jnp.int32, (16, 128), 0)
    lane_16 = lanes_of((16, 128))
    own_lanes = lax.div(lane_16, 8) == row_16
    for i in range(3):
        for t in range(2):
            turned = pltpu.roll(ext[i, 4 + 16 * t : 20 + 16 * t], 4, 1, stride=8, stride_axis=0)
            pack_out[2 * i + t : 2 * i + t + 1] = jnp.sum(jnp.where(own_lanes, turned, 0.0), axis=0, keepdims=True)
    pack_out[6:8] = jnp.zeros((2, 128), f32)
    pl.semaphore_wait(barrier, 1 + 2 * (n_p - 1) + (n_z - 1))
    swaps = [
        pltpu.make_async_remote_copy(src_ref=src, dst_ref=dst, send_sem=sem_r.at[0, i], recv_sem=sem_r.at[1, i], device_id=partner, device_id_type=MESH)
        for i, (src, dst) in enumerate(((field_ref, near_f), (cot_ref, near_c), (check_ref, near_k)))
    ]
    for swap in swaps:
        swap.start()
    posts = [
        remote(pack_out, pack_in.at[slot], sem_p.at[0, slot], sem_p.at[1, slot], who)
        for slot, who in (
            (1, left), (0, right), (3, {**left, "gx": other}), (2, {**right, "gx": other}), (4, partner),
        )
    ]
    for post in posts:
        post.start()
    piece = share // PIECES
    pieces = [
        remote(prior_ref.at[pl.ds(skip * other + piece * k, piece)], c_in.at[pl.ds(piece * k, piece)], sem_c.at[0, k], sem_c.at[1, k], partner)
        for k in range(PIECES)
    ]
    for copy in pieces:
        copy.start()
    for swap in swaps:
        swap.wait_recv()
    ext[0, 0:4], ext[0, 36:40] = near_f[0, 28:32], near_f[0, 0:4]
    ext[1, 0:4], ext[1, 36:40] = near_c[0, 28:32], near_c[0, 0:4]
    ext[2, 0:4], ext[2, 36:40] = near_k[28:32].astype(f32), near_k[0:4].astype(f32)


    load.wait()
    n_cols = prior_ref.shape[2]
    whole = n_cols // 128 * 128

    def pair_sum(r, _):
        at = pl.multiple_of(80 * r, 16)
        for j in range(4):
            cols = slice(2048 * j, 2048 * j + 2048)
            value = c_own[r, :, cols] + c_in[r, :, cols]
            xs[pl.ds(at + 16 * j, 16)] = value.reshape(16, 128).astype(bf)
        value = (c_own[r, :, 8192:whole] + c_in[r, :, 8192:whole]).reshape((whole - 8192) // 128, 128)
        last = c_own[r, :, whole:] + c_in[r, :, whole:]
        last = jnp.concatenate([last, jnp.zeros((1, whole + 128 - n_cols), f32)], axis=1)
        value = jnp.concatenate([value, last, jnp.zeros((16 - 1 - value.shape[0], 128), f32)], axis=0)
        xs[pl.ds(at + 64, 16)] = value.astype(bf)
        return 0

    xs[80 * share :] = jnp.zeros((xs.shape[0] - 80 * share, 128), bf)
    chunks = 80 * piece // 64

    def reduce_piece(k):
        pieces[k].wait_recv()
        lax.fori_loop(piece * k, piece * k + piece, pair_sum, 0)
        for q in range(chunks * k, n_p if k == PIECES - 1 else chunks * k + chunks):

            @pl.when(p != q)
            def _():
                to_plane(q, p).start()

    for k in range(PIECES):
        reduce_piece(k)

    for post in posts:
        post.wait_recv()
    column = lax.rem(lanes_of((8, 128)), 8)
    own = pack_out[...]
    sides = (
        (jnp.where(column >= 4, own, pack_in[0]), jnp.where(column >= 4, pack_in[4], pack_in[2])),
        (jnp.where(column < 4, own, pack_in[1]), jnp.where(column < 4, pack_in[4], pack_in[3])),
    )
    lane_flat = lanes_of((1, 384))
    blank = jnp.zeros((1, 128), f32)

    def flat(side, i):
        near, far = (part[2 * i : 2 * i + 2] for part in side)
        inner = pltpu.roll(jnp.concatenate([near[0:1], near[1:2], blank], axis=1), 32, 1)
        outer = jnp.concatenate([pltpu.roll(far[1:2], 32, 1), blank, pltpu.roll(far[0:1], 32, 1)], axis=1)
        value = jnp.where((lane_flat >= 32) & (lane_flat < 288), inner, outer)
        return jnp.where(lane_flat < 320, value, 0.0)

    def flat_both(i):
        return jnp.concatenate([flat(sides[0], i), flat(sides[1], i)], axis=1)

    field_s, cot_s, frozen_s = flat_both(0), flat_both(1), flat_both(2)
    masked_s = field_s * frozen_s

    def both_rolled(value, offset):
        return jnp.concatenate([flat_roll(value[:, :384], offset), flat_roll(value[:, 384:], offset)], axis=1)

    def unflat(vector, e):
        parts = []
        for t in range(3):
            spread = jnp.broadcast_to(vector[:, 128 * t : 128 * t + 128], (16, 128))
            parts.append(jnp.sum(jnp.where(lane_16 == 8 * row_16 + e, spread, 0.0), axis=1, keepdims=True))
        return jnp.concatenate(parts, axis=0)

    masked = ext[0] * ext[2]
    lane_48 = lanes_of((48, 128))
    shifts = (
        jnp.where(lane_48 == 0, unflat(masked_s[:, :384], 3), pltpu.roll(masked, 1, 1)),
        masked,
        jnp.where(lane_48 == 127, unflat(masked_s[:, 384:], 4), pltpu.roll(masked, 127, 1)),
    )
    taps[...] = jnp.zeros(taps.shape, f32)
    edge_taps[...] = jnp.zeros(edge_taps.shape, f32)
    for a in range(3):
        for b in range(3):
            k = 3 * a + b
            taps[pl.ds(16 + k, 38, stride=16), :] = shifts[b][a : a + 38]
            edge_taps[k : k + 1, :] = both_rolled(masked_s, 8 * (a - 1) + b - 1)

    def first(tap_values):
        high, low = halves(tap_values)
        return jnp.tanh(dot(w_one, jnp.concatenate([high, low, high], axis=0))).astype(bf)

    lane_384 = lanes_of((32, 384))

    def spread_edges(value, back, store):
        for a in range(3):
            for b in range(3):
                k = 3 * a + b
                offset = 8 * (a - 1) + (1 - b if back else b - 1)
                store[32 * k : 32 * k + 32, :] = both_rolled(value, offset).astype(bf)
        mixed = jnp.where(lax.rem(lane_384, 8) == 4, flat_roll(value[:, :384], -1), flat_roll(value[:, 384:], 1))
        for t in range(3):
            cp[t] = mixed[:, 128 * t : 128 * t + 128]

    lane_32 = lanes_of((32, 128))

    def spread_row(q, value, back, store):
        edge = pltpu.roll(cp[lax.div(q, 16)], lax.rem(252 - 8 * lax.rem(q, 16), 128), 1)
        before = jnp.where(lane_32 == 0, edge, pltpu.roll(value, 1, 1)).astype(bf)
        after = jnp.where(lane_32 == 127, edge, pltpu.roll(value, 127, 1)).astype(bf)
        store[q, 0:32] = after if back else before
        store[q, 32:64] = value.astype(bf)
        store[q, 64:96] = before if back else after

    one_s = first(edge_taps[...])
    spread_edges(one_s.astype(f32), False, xs_one)

    def one_rows(rows):
        values = jnp.concatenate([taps[pl.ds(pl.multiple_of(16 * q, 16), 16), :] for q in rows], axis=1)
        out = first(values).astype(f32)
        for i, q in enumerate(rows):
            spread_row(q, out[:, 128 * i : 128 * i + 128], False, xm)

    def over_rows(step, first_group=0, last_group=2):
        def body(i, _):
            step([4 + 16 * i + n for n in range(16)])
            return 0

        lax.fori_loop(first_group, last_group, body, 0)

    for q in (0, 39):
        xm[q] = jnp.zeros((96, 128), bf)
    one_rows([1, 2, 3, 36])
    one_rows([37, 38])
    over_rows(one_rows)

    def second(windows, field, cot, frozen):
        two = jnp.tanh(dot(w2[...], windows)).astype(bf)
        pair = dot(head, two)
        expo = jnp.exp(pair[0:1])
        open_cot = (1.0 - frozen) * cot
        d_0 = (open_cot * field * expo).astype(bf)
        d_1 = open_cot.astype(bf)
        two_f = two.astype(f32)
        d_two = (head_0 * d_0.astype(f32) + head_1 * d_1.astype(f32)) * (1.0 - two_f * two_f)
        return two, pair, d_0, d_1, d_two.astype(bf).astype(f32)

    _, _, _, _, d_two_s = second(xs_one[...], field_s, cot_s, frozen_s)
    spread_edges(d_two_s, True, xds)

    def windows_of(store, rows):
        return jnp.concatenate([store[pl.ds(q - 1, 3)].reshape(288, 128) for q in rows], axis=1)

    def rows_of(i, rows):
        return jnp.concatenate([ext[i, pl.ds(q, 1), :] for q in rows], axis=1)

    acc_mid[...] = jnp.zeros(acc_mid.shape, f32)
    b_rows[...] = jnp.zeros(b_rows.shape, f32)

    def two_rows(rows, inner=True):
        two, pair, d_0, d_1, d_two = second(windows_of(xm, rows), rows_of(0, rows), rows_of(1, rows), rows_of(2, rows))
        for i, q in enumerate(rows):
            at = slice(128 * i, 128 * i + 128)
            spread_row(q, d_two[:, at], True, xd)
            if inner:
                pair_rows[pl.ds(pl.multiple_of(8 * q, 8), 2), :] = pair[:, at]
        if inner:
            b_rows[297:299, 0:32] += nt(jnp.concatenate([d_0, d_1], axis=0), two)

    for q in (0, 1, 38, 39):
        xd[q] = jnp.zeros((96, 128), bf)
    two_rows([2, 3, 36, 37], inner=False)
    over_rows(two_rows, 0, 1)
    total = xs[chunk(p)].astype(f32)
    for offset in plane_order:
        q = from_beside(*offset)
        to_plane(q, q).wait_recv()
        total = total + xr[q].astype(f32)
    zs[...] = total.astype(bf).reshape(4, 16, 128)

    for offset in line_order:
        to_along(lax.rem(z + offset, n_z), z).start()
    over_rows(two_rows, 1, 2)

    def mid_rows(i, _):
        rows = [4 + 16 * i + n for n in range(16)]
        one = jnp.concatenate([xm[q, 32:64] for q in rows], axis=1)
        acc_mid[...] += nt(windows_of(xd, rows), one)
        return 0

    lax.fori_loop(0, 2, mid_rows, 0)
    for j in range(3):
        b_rows[9 + 96 * (2 - j) : 9 + 96 * (2 - j) + 96, 0:32] = acc_mid[96 * j : 96 * j + 96]
    rows = mine.shape[0]
    layer = b_rows[pl.ds(0, rows, stride=4), :]
    for g in range(1, 4):
        layer = layer + pltpu.roll(b_rows[pl.ds(g, rows, stride=4), :], 32 * g, 1)
    mine[...] = layer * scale
    is_owner = (p < UNITS) & (lax.rem(p, 2) == core)

    def to_owner(unit, slot):
        return remote(mine.at[pl.ds(8 * unit, 8)], mine_x.at[slot], sem_l.at[unit], sem_lx.at[slot], plane(unit, unit % 2))

    def is_other(unit):
        return (p != unit) | (core != unit % 2)

    for unit in range(UNITS):

        @pl.when(is_other(unit))
        def _():
            to_owner(unit, n_p * core + p).start()

    def third(windows, one):
        one_f = one.astype(f32)
        d_one = dot(w3[...], windows) * (1.0 - one_f * one_f)
        high, low = halves(d_one)
        return high, low, dot(w_back, jnp.concatenate([high, low, high], axis=0))

    _, _, t_s = third(xds[...], one_s)

    def three_rows(rows, inner=True):
        windows = windows_of(xd, rows)
        one = jnp.concatenate([xm[q, 32:64] for q in rows], axis=1)
        high, low, t_values = third(windows, one)
        for i, q in enumerate(rows):
            t_rows[pl.ds(pl.multiple_of(16 * q, 16), 16), :] = t_values[:, 128 * i : 128 * i + 128]
        if inner:
            values = jnp.concatenate([taps[pl.ds(pl.multiple_of(16 * q, 16), 16), :] for q in rows], axis=1)
            m_high, m_low = halves(values)
            parts = nt(jnp.concatenate([m_high, m_low], axis=0), jnp.concatenate([high, low], axis=0))
            parts = parts[0:16] + parts[16:32]
            b_in[0:9, 0:32] += (parts[:, 0:32] + parts[:, 32:64])[0:9]

    b_in[...] = jnp.zeros(b_in.shape, f32)
    three_rows([3, 36], inner=False)
    over_rows(three_rows)


    late = b_in[pl.ds(0, 4, stride=4), :]
    for g in range(1, 4):
        late = late + pltpu.roll(b_in[pl.ds(g, 4, stride=4), :], 32 * g, 1)
    me = n_p * core + p
    late_x[me] = late * scale

    def to_late(q, which, slot):
        return remote(late_x.at[me], late_x.at[slot], sem_ls.at[which, q], sem_lr.at[slot], plane(q, which))

    for offset in plane_order:
        to_late(beside(*offset), core, me).start()
        to_late(beside(*offset), other, me).start()
    to_late(p, other, me).start()

    def column_sum(b):
        total = None
        for a in range(3):
            part = t_rows[pl.ds(16 * (5 - a) + 3 * a + b, 32, stride=16), :]
            total = part if total is None else total + part
        return total

    def edge_sum(b, side):
        total = None
        for a in range(3):
            k = 3 * a + b
            part = flat_roll(t_s[k : k + 1, 384 * side : 384 * side + 384], 8 * (1 - a))
            total = part if total is None else total + part
        return total

    lane = lanes_of((32, 128))
    from_right = unflat(edge_sum(0, 1), 4)[4:36]
    from_left = unflat(edge_sum(2, 0), 3)[4:36]
    d_masked = (
        jnp.where(lane == 127, from_right, pltpu.roll(column_sum(0), 127, 1))
        + column_sum(1)
        + jnp.where(lane == 0, from_left, pltpu.roll(column_sum(2), 1, 1))
    )
    frozen = check_ref[...].astype(f32)
    unfrozen = 1.0 - frozen
    expo = jnp.exp(pair_rows[pl.ds(32, 32, stride=8), :])
    offset = pair_rows[pl.ds(33, 32, stride=8), :]
    values, cot = field_ref[0], cot_ref[0]
    coupled_ref[0] = frozen * values + unfrozen * (values * expo + offset)
    fgrad_ref[0] = frozen * cot + unfrozen * cot * expo + frozen * d_masked


    def to_along_mine(w, slot):
        return remote(own_sum, mine_z.at[slot], sem_lz.at[0, w], sem_lz.at[1, slot], along(w))

    @pl.when(is_owner)
    def _():
        def take(i, total):
            slot = lax.rem(n_p * core + p + i, 2 * n_p)
            to_owner(0, slot).wait_recv()
            return total + mine_x[slot]

        own_sum[...] = lax.fori_loop(1, 2 * n_p, take, mine[chunk(p, 8)])
        for offset in line_order:
            to_along_mine(lax.rem(z + offset, n_z), z).start()

    tile = lax.rem(z, 4)

    total = zs[tile].astype(f32)
    for offset in line_order:
        w = lax.rem(z + n_z - offset, n_z)
        to_along(w, w).wait_recv()
        total = total + zr[w].astype(f32)
    fin[core, chunk(4 * p + tile, 16)] = total.astype(bf)

    def to_four(i, slot):
        w = lax.rem(z + n_z + (1, -1, -2)[i - 1], n_z)
        at = chunk(4 * p + slot, 16)
        return remote(fin.at[core, chunk(4 * p + tile, 16)], fin.at[core, at], sem_t.at[0, i], sem_t.at[1, slot], along(w))

    for i in range(1, 4):
        to_four(i, tile).start()

    for i in range(1, 4):
        to_four(i, lax.rem(tile + i, 4)).wait_recv()

    def all_plane(q, slot):
        return remote(fin.at[core, chunk(p)], fin.at[core, chunk(slot)], sem_a.at[0, q], sem_a.at[1, slot], plane(q))

    def to_partner(which, slot):
        return remote(fin.at[core, chunk(slot)], fin.at[which, chunk(slot)], sem_b.at[0, slot], sem_b.at[1, slot], partner)

    to_partner(core, p).start()
    for offset in plane_order:
        all_plane(beside(*offset), p).start()

    def late_arrives(i, _):
        to_late(p, other, lax.rem(me + i, 2 * n_p)).wait_recv()
        return 0

    lax.fori_loop(1, 2 * n_p, late_arrives, 0)
    late_z[z] = lax.fori_loop(0, 2 * n_p, lambda i, total: total + late_x[i], jnp.zeros((4, 128), f32))

    def late_along(w, slot):
        return remote(late_z.at[z], late_z.at[slot], sem_lt.at[0, w], sem_lt.at[1, slot], along(w))

    for offset in line_order:
        late_along(lax.rem(z + offset, n_z), z).start()

    def to_all_mine(q, which, unit):
        return remote(mine_fin.at[unit], mine_fin.at[unit], sem_la.at[which, q], sem_mr.at[unit], plane(q, which))

    @pl.when(is_owner)
    def _():
        def take(i, total):
            w = lax.rem(z + n_z - i, n_z)
            to_along_mine(w, w).wait_recv()
            return total + mine_z[w]

        mine_fin[p] = lax.fori_loop(1, n_z, take, own_sum[...])
        for offset in plane_order:
            to_all_mine(beside(*offset), core, p).start()
            to_all_mine(beside(*offset), other, p).start()
        to_all_mine(p, other, p).start()

    for offset in plane_order:
        q = from_beside(*offset)
        all_plane(q, q).wait_recv()
        to_partner(core, q).start()

    def late_final(i, _):
        w = lax.rem(z + i, n_z)
        late_along(w, w).wait_recv()
        return 0

    lax.fori_loop(1, n_z, late_final, 0)
    late_fin[...] = lax.fori_loop(0, n_z, lambda i, total: total + late_z[i], jnp.zeros((4, 128), f32))
    for q in range(n_p):
        to_partner(other, q).wait_recv()
    for unit in range(UNITS):

        @pl.when(is_other(unit))
        def _():
            to_all_mine(p, other, unit).wait_recv()

    for copy in (*swaps, *posts, *pieces):
        copy.wait_send()

    def drain_plane(i, _):
        q = lax.rem(p + i, n_p)
        to_plane(q, p).wait_send()
        all_plane(q, p).wait_send()
        return 0

    def drain_along(i, _):
        to_along(lax.rem(z + i, n_z), z).wait_send()
        return 0

    to_partner(core, p).wait_send()
    for offset in plane_order:
        to_partner(core, from_beside(*offset)).wait_send()
    def drain_late(i, _):
        q = lax.rem(p + i, n_p)
        to_late(q, core, me).wait_send()
        to_late(q, other, me).wait_send()
        return 0

    def drain_late_along(i, _):
        late_along(lax.rem(z + i, n_z), z).wait_send()
        return 0

    lax.fori_loop(1, n_p, drain_late, 0)
    to_late(p, other, me).wait_send()
    lax.fori_loop(1, n_z, drain_late_along, 0)
    lax.fori_loop(1, n_p, drain_plane, 0)
    lax.fori_loop(1, n_z, drain_along, 0)
    for i in range(1, 4):
        to_four(i, tile).wait_send()
    for unit in range(UNITS):

        @pl.when(is_other(unit))
        def _():
            to_owner(unit, n_p * core + p).wait_send()

    @pl.when(is_owner)
    def _():
        def drain_z(i, _):
            to_along_mine(lax.rem(z + i, n_z), z).wait_send()
            return 0

        def drain_all(i, _):
            q = lax.rem(p + i, n_p)
            to_all_mine(q, core, p).wait_send()
            to_all_mine(q, other, p).wait_send()
            return 0

        lax.fori_loop(1, n_z, drain_z, 0)
        lax.fori_loop(1, n_p, drain_all, 0)
        to_all_mine(p, other, p).wait_send()


def unpack_kernel(coupled_in, fgrad_in, fin, mine_fin, late_fin, coupled_ref, fgrad_ref, out_ref, wide):
    coupled_ref[...] = coupled_in[...]
    fgrad_ref[...] = fgrad_in[...]
    n_rows, n_cols = out_ref.shape
    share = n_rows // 2
    for unit in range(UNITS):
        wide[8 * unit : 8 * unit + 8] = mine_fin[unit]
    wide[0:4] += late_fin[...]
    for which in range(2):
        base = 80 * (1 + (n_rows - 1 - share) * which)

        def widen(r, _):
            rows = fin[which, pl.ds(pl.multiple_of(80 * r, 16), 80)].astype(jnp.float32)
            wide[pl.ds(pl.multiple_of(base + 80 * r, 16), 80)] = rows
            return 0

        lax.fori_loop(0, share, widen, 0, unroll=4)

    def unpack(k, _):
        out_ref[:, pl.ds(pl.multiple_of(k * 128, 128), 128)] = wide[pl.ds(k, n_rows, stride=80), :]
        return 0

    whole = n_cols // 128
    lax.fori_loop(0, whole, unpack, 0, unroll=37)
    out_ref[:, 128 * whole :] = wide[pl.ds(whole, n_rows, stride=80), :][:, : n_cols - 128 * whole]


def unpack_call(coupled, fgrad, fin, mine_fin, late_fin, rows, cols):
    f32 = jnp.float32
    vmem = pl.BlockSpec(memory_space=pltpu.VMEM)
    return pl.pallas_call(
        unpack_kernel,
        out_shape=(
            jax.ShapeDtypeStruct(coupled.shape, f32),
            jax.ShapeDtypeStruct(fgrad.shape, f32),
            jax.ShapeDtypeStruct((rows, cols), f32),
        ),
        in_specs=[vmem] * 5,
        out_specs=(vmem,) * 3,
        scratch_shapes=[pltpu.VMEM((80 * rows, 128), f32)],
    )(coupled, fgrad, fin, mine_fin, late_fin)


def fused_call(scale, field, cot, checker, weight_in, weight_mid, weight_head, prior):
    f32, bf = jnp.float32, jnp.bfloat16
    sem = pltpu.SemaphoreType.DMA
    vmem = pl.BlockSpec(memory_space=pltpu.VMEM)
    n_p, n_z = 2 * lax.axis_size("gy"), lax.axis_size("dp") // 2
    rows, _, cols = prior.shape
    share = (rows + 1) // 2
    return pl.pallas_call(
        functools.partial(fused_kernel, scale),
        out_shape=(
            jax.ShapeDtypeStruct(field.shape, f32),
            jax.ShapeDtypeStruct(field.shape, f32),
            jax.ShapeDtypeStruct((2, n_p * 64, 128), bf),
            jax.ShapeDtypeStruct((UNITS, 8, 128), f32),
            jax.ShapeDtypeStruct((4, 128), f32),
        ),
        in_specs=[vmem] * 6 + [pl.BlockSpec(memory_space=pl.ANY)],
        out_specs=(vmem,) * 5,
        scratch_shapes=[
            pltpu.VMEM(field.shape, f32), pltpu.VMEM(field.shape, f32), pltpu.VMEM(checker.shape, jnp.int32),
            pltpu.VMEM((3, 48, 128), f32),
            pltpu.VMEM((8, 128), f32), pltpu.VMEM((5, 8, 128), f32),
            pltpu.VMEM((640, 128), f32), pltpu.VMEM((16, 768), f32),
            pltpu.VMEM((16, 128), f32), pltpu.VMEM((32, 288), bf), pltpu.VMEM((32, 288), bf),
            pltpu.VMEM((40, 96, 128), bf), pltpu.VMEM((288, 768), bf),
            pltpu.VMEM((40, 96, 128), bf), pltpu.VMEM((288, 768), bf),
            pltpu.VMEM((3, 32, 128), f32),
            pltpu.VMEM((320, 128), f32), pltpu.VMEM((640, 128), f32),
            pltpu.VMEM((288, 32), f32), pltpu.VMEM((320, 128), f32),
            pltpu.VMEM((share, 1, cols), f32), pltpu.VMEM((share, 1, cols), f32),
            pltpu.VMEM((n_p * 64, 128), bf), pltpu.VMEM((n_p, 64, 128), bf),
            pltpu.VMEM((4, 16, 128), bf), pltpu.VMEM((n_z, 16, 128), bf),
            pltpu.VMEM((80, 128), f32),
            pltpu.VMEM((2 * n_p, 8, 128), f32), pltpu.VMEM((n_z, 8, 128), f32),
            pltpu.VMEM((8, 128), f32),
            pltpu.VMEM((16, 128), f32), pltpu.VMEM((2 * n_p, 4, 128), f32), pltpu.VMEM((n_z, 4, 128), f32),
            sem((2, 3)), sem((2, 5)), sem, sem((2, PIECES)), sem((2, n_p)), sem((2, n_z)), sem((2, 4)), sem((2, n_p)), sem((2, n_p)),
            sem((UNITS,)), sem((2 * n_p,)), sem((2, n_z)), sem((2, n_p)), sem((UNITS,)),
            sem((2, n_p)), sem((2 * n_p,)), sem((2, n_z)),
        ],
        compiler_params=pltpu.CompilerParams(collective_id=0, has_side_effects=True),
    )(field, cot, checker, weight_in, weight_mid, weight_head, prior)


def on_device(field, cotangent, checker, weight_in, weight_mid, weight_head, prior_grads):
    cell_total = field.size * lax.axis_size("dp") * lax.axis_size("gx") * lax.axis_size("gy")
    scale = 1.0 / math.sqrt(cell_total)
    prior = prior_grads.reshape(prior_grads.shape[3], 1, prior_grads.shape[4])
    sums = fused_call(scale, field, cotangent, checker, weight_in, weight_mid, weight_head, prior)
    return unpack_call(*sums, prior.shape[0] + 1, prior.shape[2])


def solution(mesh):
    placed = (
        P("dp", "gx", "gy"),
        P("dp", "gx", "gy"),
        P("gx", "gy"),
        P(),
        P(),
        P(),
        P("dp", "gx", "gy", None, None),
    )
    return jax.shard_map(
        on_device,
        mesh=mesh,
        in_specs=placed,
        out_specs=(P("dp", "gx", "gy"), P("dp", "gx", "gy"), P()),
        check_vma=False,
    )
```
